512 devices in a mesh: lon: 32 (over z_lo, y), lat: 16 (over z_hi, x, core).
Axes of the slice: x: 4, y: 4, z: 16 (z_hi: 2, z_lo: 8; z = z_hi * 8 + z_lo), core: 2. Of those that a mesh axis runs over, the one named last changes fastest.
Arguments:
- fields: bfloat16 [16, 64, 32, 4096], P('lat', None, None, 'lon'), may hold values from -40 to 40
- ocean_mask: int32 [16, 32, 4096], P('lat', None, 'lon'), may hold values 0 or 1
- norm_gain: float32 [64], replicated, may hold values from 0.5 to 1.5
- w_vert: bfloat16 [5, 8, 8, 8], replicated, may hold values from -1 to 1
- b_vert: float32 [64], replicated, may hold values from -3 to 3
- w_horiz: bfloat16 [5, 64, 5, 64], replicated, may hold values from -0.15625 to 0.15625
- b_horiz: float32 [64], replicated, may hold values from -3 to 3
Outputs:
- updated: bfloat16 [16, 64, 32, 4096], P('lat', None, None, 'lon')
The draws below stay inside these ranges and needn't reach their ends.
All inputs are finite; a program needn't handle non-finite values. No bound on the sum of `ocean_mask` on one device may be relied on, other than what follows from the above.
Results may differ from the reference program's by a relative error of at most 0.0023.
Values may be sent and summed in bfloat16 or wider, within the bound.
A program may use at most 64 MiB of HBM per device.

```python
import math
import jax
import jax.numpy as jnp
from jax import lax

C = 64
CG = 8
TAPS = 5
LAT_DEV = 2
G = 8
LEV = 16
NLAT = 32
NLON = 4096


def draw_fields(key, part):
    first, second, third = jax.random.split(key, 3)
    shape = (LEV, C, NLAT, NLON)
    base = jnp.clip(jax.random.normal(first, shape, jnp.float32), -4.0, 4.0)
    cell_scale = 0.3 * jnp.exp(jax.random.uniform(second, (LEV, 1, NLAT, NLON), jnp.float32, 0.0, math.log(10.0)))
    chan_scale = jnp.exp(jax.random.uniform(third, (1, C, 1, 1), jnp.float32, -0.5, 0.5))
    return (base * cell_scale * chan_scale).astype(jnp.bfloat16)


def set_ends(array, key, least, top_value):
    longest = array.shape.index(max(array.shape))
    spots = []
    for shift in (0, 1):
        where = [jax.random.randint(jax.random.fold_in(key, axis), (), 0, length) for axis, length in enumerate(array.shape)]
        where[longest] = (where[longest] + shift) % array.shape[longest]
        spots.append(tuple(where))
    return array.at[spots[0]].set(least).at[spots[1]].set(top_value)


def scatter_about(own_key, extent, width, limit, kind=jnp.bfloat16):
    return jnp.clip(width * jax.random.normal(own_key, extent, jnp.float32), -limit, limit).astype(kind)


def setup_inputs(seed: int = 0) -> dict:
    seeds = jax.random.split(jax.random.key(seed), 8)
    return {
        "fields": draw_fields(jax.random.fold_in(seeds[7], 71), 0),
        "ocean_mask": set_ends((jax.random.randint(seeds[1], (LEV, NLAT, NLON), 0, 4) < 3).astype(jnp.int32), jax.random.fold_in(seeds[1], 1), 0, 1),
        "norm_gain": jnp.clip(1.0 + 0.1 * jax.random.normal(seeds[2], (C,), jnp.float32), 0.5, 1.5),
        "w_vert": scatter_about(seeds[3], (TAPS, G, CG, CG), (TAPS * CG) ** -0.5, 1.0),
        "b_vert": scatter_about(seeds[4], (C,), 0.5, 3.0, jnp.float32),
        "w_horiz": scatter_about(seeds[5], (TAPS, C, TAPS, C), (TAPS * TAPS * C) ** -0.5, 0.15625),
        "b_horiz": scatter_about(seeds[6], (C,), 0.5, 3.0, jnp.float32),
    }


def normalize(block, norm_gain):
    values = block.astype(jnp.float32)
    center = lax.optimization_barrier(jnp.mean(values, axis=1, keepdims=True))
    spread = lax.optimization_barrier(jnp.mean((values - center) ** 2, axis=1, keepdims=True))
    return ((values - center) * lax.rsqrt(spread + 1e-05) * norm_gain[None, :, None, None]).astype(jnp.bfloat16)

def vertical(normed, w_vert, b_vert):
    count_lev, channels, rows_lat, cols_lon = normed.shape
    groups, width_in, width_out = (w_vert.shape[1], w_vert.shape[2], w_vert.shape[3])
    padded = jnp.pad(normed, ((2, 2), (0, 0), (0, 0), (0, 0)))
    summed = jnp.zeros((count_lev, groups, width_out, rows_lat, cols_lon), jnp.float32)
    for tap_index in range(w_vert.shape[0]):
        grouped = padded[tap_index:tap_index + count_lev].reshape(count_lev, groups, width_in, rows_lat, cols_lon)
        summed = summed + jnp.einsum('gio,ngiab->ngoab', w_vert[tap_index].astype(jnp.float32), grouped.astype(jnp.float32))
    summed = summed.reshape(count_lev, channels, rows_lat, cols_lon) + b_vert[None, :, None, None]
    return jax.nn.gelu(summed).astype(jnp.bfloat16)

def horizontal(level_in, fields_in, ocean_in, w_horiz, b_horiz):
    channels, rows_lat, cols_lon = level_in.shape
    extended = jnp.concatenate([level_in[:, :, -2:], level_in, level_in[:, :, :2]], axis=2)
    extended = jnp.pad(extended, ((0, 0), (2, 2), (0, 0)))
    summed = jnp.zeros((channels, rows_lat, cols_lon), jnp.float32)
    for row_tap in range(w_horiz.shape[0]):
        stacked = jnp.concatenate([extended[:, row_tap:row_tap + rows_lat, col_tap:col_tap + cols_lon] for col_tap in range(w_horiz.shape[2])], axis=0)
        kernel = w_horiz[row_tap].reshape(channels, -1)
        summed = summed + jnp.einsum('oj,jab->oab', kernel.astype(jnp.float32), stacked.astype(jnp.float32))
    ocean = ocean_in[None].astype(jnp.float32)
    return (fields_in.astype(jnp.float32) + ocean * (summed + b_horiz[:, None, None])).astype(jnp.bfloat16)

def reference(fields, ocean_mask, norm_gain, w_vert, b_vert, w_horiz, b_horiz):
    blocks = NLAT // LAT_DEV

    def column_block(block_index):
        start = (block_index * LAT_DEV).astype(jnp.int32)
        piece = lax.dynamic_slice_in_dim(fields, start, LAT_DEV, 2)
        return vertical(normalize(piece, norm_gain), w_vert, b_vert)
    mixed = lax.map(column_block, jnp.arange(blocks, dtype=jnp.int32))
    mixed = jnp.moveaxis(mixed, 0, 2).reshape(LEV, C, NLAT, NLON)
    masked = mixed * ocean_mask[:, None].astype(jnp.bfloat16)

    def level_step(operands):
        return horizontal(operands[0], operands[1], operands[2], w_horiz, b_horiz)
    return lax.map(level_step, (masked, fields, ocean_mask))
```

```python
import jax
import jax.numpy as jnp
from jax import lax
from jax.sharding import PartitionSpec as P


def extended_2(shard, sides, width):
    for axis, dim in sides:
        devices, length = (lax.axis_size(axis), shard.shape[dim])
        up = [(i, (i + 1) % devices) for i in range(devices)]
        down = [(j, i) for i, j in up]
        last = lax.slice_in_dim(shard, length - width, length, axis=dim)
        leading = lax.slice_in_dim(shard, 0, width, axis=dim)
        before = lax.ppermute(last, axis, up)
        after = lax.ppermute(leading, axis, down)
        shard = jnp.concatenate([before, shard, after], axis=dim)
    return shard


def normalize(block, norm_gain):
    values = block.astype(jnp.float32)
    center = jnp.mean(values, axis=1, keepdims=True)
    spread = jnp.mean((values - center) ** 2, axis=1, keepdims=True)
    return ((values - center) * lax.rsqrt(spread + 1e-05) * norm_gain[None, :, None, None]).astype(
        jnp.bfloat16
    )


def vertical(taps, w_vert, b_vert):
    count_lev, channels, rows_lat, cols_lon = taps[0].shape
    groups, width_in, width_out = (w_vert.shape[1], w_vert.shape[2], w_vert.shape[3])
    summed = jnp.zeros((count_lev, groups, width_out, rows_lat, cols_lon), jnp.float32)
    for tap_index in range(len(taps)):
        grouped = taps[tap_index].reshape(count_lev, groups, width_in, rows_lat, cols_lon)
        summed = summed + jnp.einsum(
            "gio,ngiab->ngoab", w_vert[tap_index], grouped, preferred_element_type=jnp.float32
        )
    summed = summed.reshape(count_lev, channels, rows_lat, cols_lon) + b_vert[None, :, None, None]
    return jax.nn.gelu(summed).astype(jnp.bfloat16)


def local(fields, ocean_mask, norm_gain, w_vert, b_vert, w_horiz, b_horiz):
    normed = normalize(fields, norm_gain)
    reach = w_vert.shape[0] // 2
    columns = lax.all_to_all(normed, "lat_lo", split_axis=2, concat_axis=0, tiled=True)
    count_lev = columns.shape[0]
    upper = lax.axis_index("lat_hi") == 0
    send = jnp.where(upper, columns[count_lev - reach :], columns[:reach])
    recv = lax.ppermute(send, "lat_hi", [(0, 1), (1, 0)])
    zeros = jnp.zeros_like(recv)
    below = jnp.where(upper, zeros, recv)
    above = jnp.where(upper, recv, zeros)
    padded = jnp.concatenate([below, columns, above], axis=0)
    taps = [padded[tap_index : tap_index + count_lev] for tap_index in range(w_vert.shape[0])]
    mixed = lax.all_to_all(
        vertical(taps, w_vert, b_vert), "lat_lo", split_axis=0, concat_axis=2, tiled=True
    )
    masked = mixed * ocean_mask[:, None].astype(jnp.bfloat16)
    extended = extended_2(masked, (("lon", 3),), 2)
    extended = jnp.pad(extended, ((0, 0), (0, 0), (2, 2), (0, 0)))
    channels, rows_lat, cols_lon = (masked.shape[1], masked.shape[2], masked.shape[3])
    summed = jnp.zeros(masked.shape, jnp.float32)
    for row_tap in range(w_horiz.shape[0]):
        stacked = jnp.concatenate(
            [
                extended[:, :, row_tap : row_tap + rows_lat, col_tap : col_tap + cols_lon]
                for col_tap in range(w_horiz.shape[2])
            ],
            axis=1,
        )
        kernel = w_horiz[row_tap].reshape(channels, -1)
        summed = summed + jnp.einsum(
            "oj,njab->noab", kernel, stacked, preferred_element_type=jnp.float32
        )
    ocean = ocean_mask[:, None].astype(jnp.float32)
    return (fields.astype(jnp.float32) + ocean * (summed + b_horiz[None, :, None, None])).astype(
        jnp.bfloat16
    )


def solution(mesh):
    halves = 2
    lon_count, lat_count = mesh.devices.shape
    split = jax.sharding.Mesh(
        mesh.devices.reshape(lon_count, halves, lat_count // halves), ("lon", "lat_hi", "lat_lo")
    )
    lat = ("lat_hi", "lat_lo")
    placed = (P(lat, None, None, "lon"), P(lat, None, "lon"), P(), P(), P(), P(), P())
    return jax.shard_map(
        local, mesh=split, in_specs=placed, out_specs=P(lat, None, None, "lon"), check_vma=False
    )
```

```python
import jax
import jax.numpy as jnp
from jax import lax
from jax.sharding import PartitionSpec as P


def extended_2(shard, sides, width):
    for axis, dim in sides:
        devices, length = (lax.axis_size(axis), shard.shape[dim])
        up = [(i, (i + 1) % devices) for i in range(devices)]
        down = [(j, i) for i, j in up]
        last = lax.slice_in_dim(shard, length - width, length, axis=dim)
        leading = lax.slice_in_dim(shard, 0, width, axis=dim)
        before = lax.ppermute(last, axis, up)
        after = lax.ppermute(leading, axis, down)
        shard = jnp.concatenate([before, shard, after], axis=dim)
    return shard


def normalize(block, norm_gain):
    values = block.astype(jnp.float32)
    center = jnp.mean(values, axis=1, keepdims=True)
    spread = jnp.mean((values - center) ** 2, axis=1, keepdims=True)
    return ((values - center) * lax.rsqrt(spread + 1e-05) * norm_gain[None, :, None, None]).astype(
        jnp.bfloat16
    )


def vertical(taps, w_vert, b_vert):
    count_lev, channels, rows_lat, cols_lon = taps[0].shape
    groups, width_in, width_out = (w_vert.shape[1], w_vert.shape[2], w_vert.shape[3])
    summed = jnp.zeros((count_lev, groups, width_out, rows_lat, cols_lon), jnp.float32)
    for tap_index in range(len(taps)):
        grouped = taps[tap_index].reshape(count_lev, groups, width_in, rows_lat, cols_lon)
        summed = summed + jnp.einsum(
            "gio,ngiab->ngoab", w_vert[tap_index], grouped, preferred_element_type=jnp.float32
        )
    summed = summed.reshape(count_lev, channels, rows_lat, cols_lon) + b_vert[None, :, None, None]
    return jax.nn.gelu(summed).astype(jnp.bfloat16)


def shifted(block, axis, offset):
    devices = lax.axis_size(axis)
    pairs = [(i, i - offset) for i in range(devices) if 0 <= i - offset < devices]
    return lax.ppermute(block, axis, pairs)


def lon_halo(block, width):
    devices = lax.axis_size("lon")
    length = block.shape[-1]
    up = [(i, (i + 1) % devices) for i in range(devices)]
    down = [(j, i) for i, j in up]
    before = lax.ppermute(block[..., length - width :], "lon", up)
    after = lax.ppermute(block[..., :width], "lon", down)
    return before, after


def local(fields, ocean_mask, norm_gain, w_vert, b_vert, w_horiz, b_horiz):
    reach = w_vert.shape[0] // 2
    lat = ("lat_hi", "lat_lo")
    field_before, field_after = lon_halo(fields, reach)
    mask_before, mask_after = lon_halo(ocean_mask, reach)
    halo = jnp.concatenate([field_before, field_after], axis=3)
    halo_normed = normalize(halo, norm_gain)
    halo_taps = [
        halo_normed if tap == reach else shifted(halo_normed, lat, tap - reach)
        for tap in range(w_vert.shape[0])
    ]
    halo_mask = jnp.concatenate([mask_before, mask_after], axis=2)
    halo_masked = vertical(halo_taps, w_vert, b_vert) * halo_mask[:, None].astype(jnp.bfloat16)

    normed = normalize(fields, norm_gain)
    columns = lax.all_to_all(normed, "lat_lo", split_axis=2, concat_axis=0, tiled=True)
    count_lev = columns.shape[0]
    upper = lax.axis_index("lat_hi") == 0
    send = jnp.where(upper, columns[count_lev - reach :], columns[:reach])
    recv = lax.ppermute(send, "lat_hi", [(0, 1), (1, 0)])
    zeros = jnp.zeros_like(recv)
    below = jnp.where(upper, zeros, recv)
    above = jnp.where(upper, recv, zeros)
    padded = jnp.concatenate([below, columns, above], axis=0)
    taps = [padded[tap_index : tap_index + count_lev] for tap_index in range(w_vert.shape[0])]
    mixed = lax.all_to_all(
        vertical(taps, w_vert, b_vert), "lat_lo", split_axis=0, concat_axis=2, tiled=True
    )
    masked = mixed * ocean_mask[:, None].astype(jnp.bfloat16)
    extended = jnp.concatenate(
        [halo_masked[..., :reach], masked, halo_masked[..., reach:]], axis=3
    )
    extended = jnp.pad(extended, ((0, 0), (0, 0), (2, 2), (0, 0)))
    channels, rows_lat, cols_lon = (masked.shape[1], masked.shape[2], masked.shape[3])
    summed = jnp.zeros(masked.shape, jnp.float32)
    for row_tap in range(w_horiz.shape[0]):
        stacked = jnp.concatenate(
            [
                extended[:, :, row_tap : row_tap + rows_lat, col_tap : col_tap + cols_lon]
                for col_tap in range(w_horiz.shape[2])
            ],
            axis=1,
        )
        kernel = w_horiz[row_tap].reshape(channels, -1)
        summed = summed + jnp.einsum(
            "oj,njab->noab", kernel, stacked, preferred_element_type=jnp.float32
        )
    ocean = ocean_mask[:, None].astype(jnp.float32)
    return (fields.astype(jnp.float32) + ocean * (summed + b_horiz[None, :, None, None])).astype(
        jnp.bfloat16
    )


def solution(mesh):
    halves = 2
    lon_count, lat_count = mesh.devices.shape
    split = jax.sharding.Mesh(
        mesh.devices.reshape(lon_count, halves, lat_count // halves), ("lon", "lat_hi", "lat_lo")
    )
    lat = ("lat_hi", "lat_lo")
    placed = (P(lat, None, None, "lon"), P(lat, None, "lon"), P(), P(), P(), P(), P())
    return jax.shard_map(
        local, mesh=split, in_specs=placed, out_specs=P(lat, None, None, "lon"), check_vma=False
    )
```

```python
import jax
from jax.experimental import pallas as pl
from jax.experimental.pallas import tpu as pltpu
import jax.numpy as jnp
from jax import lax
from jax.sharding import PartitionSpec as P


def normalize(block, norm_gain):
    values = block.astype(jnp.float32)
    center = jnp.mean(values, axis=1, keepdims=True)
    spread = jnp.mean((values - center) ** 2, axis=1, keepdims=True)
    return ((values - center) * lax.rsqrt(spread + 1e-05) * norm_gain[None, :, None, None]).astype(
        jnp.bfloat16
    )


def vertical(taps, w_vert, b_vert):
    count_lev, channels, rows_lat, cols_lon = taps[0].shape
    groups, width_in, width_out = (w_vert.shape[1], w_vert.shape[2], w_vert.shape[3])
    summed = jnp.zeros((count_lev, groups, width_out, rows_lat, cols_lon), jnp.float32)
    for tap_index in range(len(taps)):
        grouped = taps[tap_index].reshape(count_lev, groups, width_in, rows_lat, cols_lon)
        summed = summed + jnp.einsum(
            "gio,ngiab->ngoab", w_vert[tap_index], grouped, preferred_element_type=jnp.float32
        )
    summed = summed.reshape(count_lev, channels, rows_lat, cols_lon) + b_vert[None, :, None, None]
    return jax.nn.gelu(summed).astype(jnp.bfloat16)


def local(fields, ocean_mask, norm_gain, w_vert, b_vert, w_horiz, b_horiz):
    normed = normalize(fields, norm_gain)
    reach = w_vert.shape[0] // 2
    columns = lax.all_to_all(normed, "lat_lo", split_axis=2, concat_axis=0, tiled=True)
    count_lev = columns.shape[0]
    upper = lax.axis_index("lat_hi") == 0
    send = jnp.where(upper, columns[count_lev - reach :], columns[:reach])
    recv = lax.ppermute(send, "lat_hi", [(0, 1), (1, 0)])
    zeros = jnp.zeros_like(recv)
    below = jnp.where(upper, zeros, recv)
    above = jnp.where(upper, recv, zeros)
    padded = jnp.concatenate([below, columns, above], axis=0)
    taps = [padded[tap_index : tap_index + count_lev] for tap_index in range(w_vert.shape[0])]
    mixed = lax.all_to_all(
        vertical(taps, w_vert, b_vert), "lat_lo", split_axis=0, concat_axis=2, tiled=True
    )
    masked = mixed * ocean_mask[:, None].astype(jnp.bfloat16)
    conv = horizontal(masked, w_horiz)
    ocean = ocean_mask[:, None].astype(jnp.float32)
    return (fields.astype(jnp.float32) + ocean * (conv + b_horiz[None, :, None, None])).astype(
        jnp.bfloat16
    )


def horizontal_kernel(x_ref, w_ref, o_ref):
    taps, channels, rows = (w_ref.shape[0] // o_ref.shape[1], o_ref.shape[1], o_ref.shape[0])
    lanes = x_ref.shape[2]
    reach = taps // 2
    weights = w_ref[...]

    def row(a, carry):
        window = x_ref[pl.ds(a, taps)].reshape(taps * x_ref.shape[1], lanes)
        partial = jnp.dot(weights, window, preferred_element_type=jnp.float32)
        total = jnp.zeros((channels, lanes), jnp.float32)
        for col_tap in range(taps):
            piece = partial[col_tap * channels : (col_tap + 1) * channels]
            total = total + pltpu.roll(piece, (reach - col_tap) % lanes, 1)
        o_ref[a] = total[:, : o_ref.shape[2]]
        return carry

    lax.fori_loop(0, rows, row, 0)


def horizontal(masked, w_horiz):
    row_taps, channels, col_taps, _ = w_horiz.shape
    reach_row, reach_col = row_taps // 2, col_taps // 2
    _, _, rows_lat, cols_lon = masked.shape
    before, after = lon_halo(masked, reach_col)
    lanes = 2 * cols_lon
    gap = jnp.zeros(masked.shape[:3] + (lanes - cols_lon - 2 * reach_col,), masked.dtype)
    wide = jnp.concatenate([masked, after, gap, before], axis=3)[0]
    wide = jnp.transpose(wide, (1, 0, 2))
    wide = jnp.pad(wide, ((reach_row, reach_row), (0, 0), (0, 0)))
    weights = jnp.transpose(w_horiz, (2, 1, 0, 3)).reshape(col_taps * channels, row_taps * channels)
    conv = pl.pallas_call(
        horizontal_kernel,
        out_shape=jax.ShapeDtypeStruct((rows_lat, channels, cols_lon), jnp.float32),
        in_specs=[pl.BlockSpec(memory_space=pltpu.VMEM)] * 2,
        out_specs=pl.BlockSpec(memory_space=pltpu.VMEM),
        cost_estimate=pl.CostEstimate(
            flops=2 * rows_lat * lanes * weights.shape[0] * weights.shape[1],
            bytes_accessed=wide.size * 2 + weights.size * 2 + rows_lat * channels * cols_lon * 4,
            transcendentals=0,
        ),
    )(wide, weights)
    return jnp.transpose(conv, (1, 0, 2))[None]


def lon_halo(block, width):
    devices = lax.axis_size("lon")
    length = block.shape[-1]
    up = [(i, (i + 1) % devices) for i in range(devices)]
    down = [(j, i) for i, j in up]
    before = lax.ppermute(block[..., length - width :], "lon", up)
    after = lax.ppermute(block[..., :width], "lon", down)
    return before, after


def solution(mesh):
    halves = 2
    lon_count, lat_count = mesh.devices.shape
    split = jax.sharding.Mesh(
        mesh.devices.reshape(lon_count, halves, lat_count // halves), ("lon", "lat_hi", "lat_lo")
    )
    lat = ("lat_hi", "lat_lo")
    placed = (P(lat, None, None, "lon"), P(lat, None, "lon"), P(), P(), P(), P(), P())
    return jax.shard_map(
        local, mesh=split, in_specs=placed, out_specs=P(lat, None, None, "lon"), check_vma=False
    )
```

```python
import jax
from jax.experimental import pallas as pl
from jax.experimental.pallas import tpu as pltpu
import jax.numpy as jnp
from jax import lax
from jax.sharding import PartitionSpec as P


def normalize(block, norm_gain):
    values = block.astype(jnp.float32)
    center = jnp.mean(values, axis=1, keepdims=True)
    spread = jnp.mean((values - center) ** 2, axis=1, keepdims=True)
    return ((values - center) * lax.rsqrt(spread + 1e-05) * norm_gain[None, :, None, None]).astype(
        jnp.bfloat16
    )


def vertical(taps, w_vert, b_vert):
    count_lev, channels, rows_lat, cols_lon = taps[0].shape
    groups, width_in, width_out = (w_vert.shape[1], w_vert.shape[2], w_vert.shape[3])
    summed = jnp.zeros((count_lev, groups, width_out, rows_lat, cols_lon), jnp.float32)
    for tap_index in range(len(taps)):
        grouped = taps[tap_index].reshape(count_lev, groups, width_in, rows_lat, cols_lon)
        summed = summed + jnp.einsum(
            "gio,ngiab->ngoab", w_vert[tap_index], grouped, preferred_element_type=jnp.float32
        )
    summed = summed.reshape(count_lev, channels, rows_lat, cols_lon) + b_vert[None, :, None, None]
    return jax.nn.gelu(summed).astype(jnp.bfloat16)


def local(fields, ocean_mask, norm_gain, w_vert, b_vert, w_horiz, b_horiz):
    normed = normalize(fields, norm_gain)
    reach = w_vert.shape[0] // 2
    columns = lax.all_to_all(normed, "lat_lo", split_axis=2, concat_axis=0, tiled=True)
    count_lev = columns.shape[0]
    upper = lax.axis_index("lat_hi") == 0
    send = jnp.where(upper, columns[count_lev - reach :], columns[:reach])
    recv = lax.ppermute(send, "lat_hi", [(0, 1), (1, 0)])
    zeros = jnp.zeros_like(recv)
    below = jnp.where(upper, zeros, recv)
    above = jnp.where(upper, recv, zeros)
    padded = jnp.concatenate([below, columns, above], axis=0)
    taps = [padded[tap_index : tap_index + count_lev] for tap_index in range(w_vert.shape[0])]
    mixed = lax.all_to_all(
        vertical(taps, w_vert, b_vert), "lat_lo", split_axis=0, concat_axis=2, tiled=True
    )
    masked = mixed * ocean_mask[:, None].astype(jnp.bfloat16)
    conv = horizontal(masked, w_horiz)
    ocean = ocean_mask[:, None].astype(jnp.float32)
    return (fields.astype(jnp.float32) + ocean * (conv + b_horiz[None, :, None, None])).astype(
        jnp.bfloat16
    )


def horizontal_kernel(x_ref, w_ref, o_ref):
    rows, channels, cols_lon = o_ref.shape
    taps = w_ref.shape[0] // channels
    segment = x_ref.shape[1] // (rows + taps - 1)
    chunk = 8
    weights = w_ref[...]
    for start in range(0, rows, chunk):
        window = jnp.concatenate(
            [
                x_ref[:, (start + row_tap) * segment : (start + row_tap + chunk) * segment]
                for row_tap in range(taps)
            ],
            axis=0,
        )
        partial = jnp.dot(weights, window, preferred_element_type=jnp.float32)
        total = partial[:channels]
        for col_tap in range(1, taps):
            piece = partial[col_tap * channels : (col_tap + 1) * channels]
            total = total + pltpu.roll(piece, chunk * segment - col_tap, 1)
        for row in range(chunk):
            o_ref[start + row] = total[:, row * segment : row * segment + cols_lon]


def horizontal(masked, w_horiz):
    row_taps, channels, col_taps, _ = w_horiz.shape
    reach_row, reach_col = row_taps // 2, col_taps // 2
    _, _, rows_lat, cols_lon = masked.shape
    before, after = lon_halo(masked, reach_col)
    segment = 2 * cols_lon
    gap = jnp.zeros(masked.shape[:3] + (segment - cols_lon - 2 * reach_col,), masked.dtype)
    wide = jnp.concatenate([before, masked, after, gap], axis=3)[0]
    wide = jnp.pad(wide, ((0, 0), (reach_row, reach_row), (0, 0)))
    wide = wide.reshape(channels, (rows_lat + 2 * reach_row) * segment)
    weights = jnp.transpose(w_horiz, (2, 1, 0, 3)).reshape(col_taps * channels, row_taps * channels)
    conv = pl.pallas_call(
        horizontal_kernel,
        out_shape=jax.ShapeDtypeStruct((rows_lat, channels, cols_lon), jnp.float32),
        in_specs=[pl.BlockSpec(memory_space=pltpu.VMEM)] * 2,
        out_specs=pl.BlockSpec(memory_space=pltpu.VMEM),
        cost_estimate=pl.CostEstimate(
            flops=2 * rows_lat * segment * weights.shape[0] * weights.shape[1],
            bytes_accessed=wide.size * 2 + weights.size * 2 + rows_lat * channels * cols_lon * 4,
            transcendentals=0,
        ),
    )(wide, weights)
    return jnp.transpose(conv, (1, 0, 2))[None]


def lon_halo(block, width):
    devices = lax.axis_size("lon")
    length = block.shape[-1]
    up = [(i, (i + 1) % devices) for i in range(devices)]
    down = [(j, i) for i, j in up]
    before = lax.ppermute(block[..., length - width :], "lon", up)
    after = lax.ppermute(block[..., :width], "lon", down)
    return before, after


def solution(mesh):
    halves = 2
    lon_count, lat_count = mesh.devices.shape
    split = jax.sharding.Mesh(
        mesh.devices.reshape(lon_count, halves, lat_count // halves), ("lon", "lat_hi", "lat_lo")
    )
    lat = ("lat_hi", "lat_lo")
    placed = (P(lat, None, None, "lon"), P(lat, None, "lon"), P(), P(), P(), P(), P())
    return jax.shard_map(
        local, mesh=split, in_specs=placed, out_specs=P(lat, None, None, "lon"), check_vma=False
    )
```

```python
import functools

import jax
from jax.experimental import pallas as pl
from jax.experimental.pallas import tpu as pltpu
import jax.numpy as jnp
from jax import lax
from jax.sharding import PartitionSpec as P


def normalize(block, norm_gain):
    values = block.astype(jnp.float32)
    center = jnp.mean(values, axis=1, keepdims=True)
    spread = jnp.mean((values - center) ** 2, axis=1, keepdims=True)
    return ((values - center) * lax.rsqrt(spread + 1e-05) * norm_gain[None, :, None, None]).astype(
        jnp.bfloat16
    )


def vertical(taps, w_vert, b_vert):
    count_lev, channels, rows_lat, cols_lon = taps[0].shape
    groups, width_in, width_out = (w_vert.shape[1], w_vert.shape[2], w_vert.shape[3])
    summed = jnp.zeros((count_lev, groups, width_out, rows_lat, cols_lon), jnp.float32)
    for tap_index in range(len(taps)):
        grouped = taps[tap_index].reshape(count_lev, groups, width_in, rows_lat, cols_lon)
        summed = summed + jnp.einsum(
            "gio,ngiab->ngoab", w_vert[tap_index], grouped, preferred_element_type=jnp.float32
        )
    summed = summed.reshape(count_lev, channels, rows_lat, cols_lon) + b_vert[None, :, None, None]
    return jax.nn.gelu(summed).astype(jnp.bfloat16)


def local(fields, ocean_mask, norm_gain, w_vert, b_vert, w_horiz, b_horiz):
    normed = normalize(fields, norm_gain)
    reach = w_vert.shape[0] // 2
    columns = lax.all_to_all(normed, "lat_lo", split_axis=2, concat_axis=0, tiled=True)
    count_lev = columns.shape[0]
    upper = lax.axis_index("lat_hi") == 0
    send = jnp.where(upper, columns[count_lev - reach :], columns[:reach])
    recv = lax.ppermute(send, "lat_hi", [(0, 1), (1, 0)])
    zeros = jnp.zeros_like(recv)
    below = jnp.where(upper, zeros, recv)
    above = jnp.where(upper, recv, zeros)
    padded = jnp.concatenate([below, columns, above], axis=0)
    taps = [padded[tap_index : tap_index + count_lev] for tap_index in range(w_vert.shape[0])]
    mixed = lax.all_to_all(
        vertical(taps, w_vert, b_vert), "lat_lo", split_axis=0, concat_axis=2, tiled=True
    )
    masked = mixed * ocean_mask[:, None].astype(jnp.bfloat16)
    conv = horizontal(masked, w_horiz)
    ocean = ocean_mask[:, None].astype(jnp.float32)
    return (fields.astype(jnp.float32) + ocean * (conv + b_horiz[None, :, None, None])).astype(
        jnp.bfloat16
    )


def horizontal_kernel(x_ref, w_ref, o_ref):
    rows, channels, cols_lon = o_ref.shape
    taps = w_ref.shape[0] // channels
    segment = x_ref.shape[1] // (rows + taps - 1)
    chunk = 8
    weights = w_ref[...]
    for start in range(0, rows, chunk):
        window = jnp.concatenate(
            [
                x_ref[:, (start + row_tap) * segment : (start + row_tap + chunk) * segment]
                for row_tap in range(taps)
            ],
            axis=0,
        )
        partial = jnp.dot(weights, window, preferred_element_type=jnp.float32)
        total = partial[:channels]
        for col_tap in range(1, taps):
            piece = partial[col_tap * channels : (col_tap + 1) * channels]
            total = total + pltpu.roll(piece, chunk * segment - col_tap, 1)
        for row in range(chunk):
            o_ref[start + row] = total[:, row * segment : row * segment + cols_lon]


def horizontal(masked, w_horiz):
    row_taps, channels, col_taps, _ = w_horiz.shape
    reach_row, reach_col = row_taps // 2, col_taps // 2
    _, _, rows_lat, cols_lon = masked.shape
    before, after = lon_halo(masked, reach_col)
    segment = 2 * cols_lon
    gap = jnp.zeros(masked.shape[:3] + (segment - cols_lon - 2 * reach_col,), masked.dtype)
    wide = jnp.concatenate([before, masked, after, gap], axis=3)[0]
    wide = jnp.pad(wide, ((0, 0), (reach_row, reach_row), (0, 0)))
    wide = wide.reshape(channels, (rows_lat + 2 * reach_row) * segment)
    weights = jnp.transpose(w_horiz, (2, 1, 0, 3)).reshape(col_taps * channels, row_taps * channels)
    conv = pl.pallas_call(
        horizontal_kernel,
        out_shape=jax.ShapeDtypeStruct((rows_lat, channels, cols_lon), jnp.float32),
        in_specs=[pl.BlockSpec(memory_space=pltpu.VMEM)] * 2,
        out_specs=pl.BlockSpec(memory_space=pltpu.VMEM),
        cost_estimate=pl.CostEstimate(
            flops=2 * rows_lat * segment * weights.shape[0] * weights.shape[1],
            bytes_accessed=wide.size * 2 + weights.size * 2 + rows_lat * channels * cols_lon * 4,
            transcendentals=0,
        ),
    )(wide, weights)
    return jnp.transpose(conv, (1, 0, 2))[None]


def halo_kernel(count, left_edge, right_edge, from_left, from_right, send_sems, recv_sems):
    me = lax.axis_index("lon")
    right, left = lax.rem(me + 1, count), lax.rem(me + count - 1, count)
    rest = (lax.axis_index("lat_hi"), lax.axis_index("lat_lo"))
    mesh_ids = pl.DeviceIdType.MESH
    barrier = pltpu.get_barrier_semaphore()
    for neighbour in (left, right):
        pl.semaphore_signal(barrier, inc=1, device_id=(neighbour,) + rest, device_id_type=mesh_ids)
    pl.semaphore_wait(barrier, 2)
    to_right = pltpu.make_async_remote_copy(
        src_ref=right_edge,
        dst_ref=from_left,
        send_sem=send_sems.at[0],
        recv_sem=recv_sems.at[0],
        device_id=(right,) + rest,
        device_id_type=mesh_ids,
    )
    to_left = pltpu.make_async_remote_copy(
        src_ref=left_edge,
        dst_ref=from_right,
        send_sem=send_sems.at[1],
        recv_sem=recv_sems.at[1],
        device_id=(left,) + rest,
        device_id_type=mesh_ids,
    )
    to_right.start()
    to_left.start()
    to_right.wait()
    to_left.wait()


def lon_halo(block, width):
    count = lax.axis_size("lon")
    length = block.shape[-1]
    edge_shape = block.shape[:-1] + (width,)
    flat = (block.shape[1], block.shape[2] * width)
    left_edge = block[..., :width].reshape(flat)
    right_edge = block[..., length - width :].reshape(flat)
    any_spec = pl.BlockSpec(memory_space=pl.ANY)
    from_left, from_right = pl.pallas_call(
        functools.partial(halo_kernel, count),
        out_shape=(jax.ShapeDtypeStruct(flat, block.dtype),) * 2,
        in_specs=[any_spec] * 2,
        out_specs=(any_spec,) * 2,
        scratch_shapes=[pltpu.SemaphoreType.DMA((2,)), pltpu.SemaphoreType.DMA((2,))],
        compiler_params=pltpu.CompilerParams(collective_id=0, has_side_effects=True),
    )(left_edge, right_edge)
    return from_left.reshape(edge_shape), from_right.reshape(edge_shape)


def solution(mesh):
    halves = 2
    lon_count, lat_count = mesh.devices.shape
    split = jax.sharding.Mesh(
        mesh.devices.reshape(lon_count, halves, lat_count // halves), ("lon", "lat_hi", "lat_lo")
    )
    lat = ("lat_hi", "lat_lo")
    placed = (P(lat, None, None, "lon"), P(lat, None, "lon"), P(), P(), P(), P(), P())
    return jax.shard_map(
        local, mesh=split, in_specs=placed, out_specs=P(lat, None, None, "lon"), check_vma=False
    )
```

```python
import functools

import jax
from jax.experimental import pallas as pl
from jax.experimental.pallas import tpu as pltpu
import jax.numpy as jnp
from jax import lax
from jax.sharding import PartitionSpec as P


def normalize(block, norm_gain):
    values = block.astype(jnp.float32)
    center = jnp.mean(values, axis=1, keepdims=True)
    spread = jnp.mean((values - center) ** 2, axis=1, keepdims=True)
    return ((values - center) * lax.rsqrt(spread + 1e-05) * norm_gain[None, :, None, None]).astype(
        jnp.bfloat16
    )


def vertical(taps, w_vert, b_vert):
    count_lev, channels, rows_lat, cols_lon = taps[0].shape
    groups, width_in, width_out = (w_vert.shape[1], w_vert.shape[2], w_vert.shape[3])
    summed = jnp.zeros((count_lev, groups, width_out, rows_lat, cols_lon), jnp.float32)
    for tap_index in range(len(taps)):
        grouped = taps[tap_index].reshape(count_lev, groups, width_in, rows_lat, cols_lon)
        summed = summed + jnp.einsum(
            "gio,ngiab->ngoab", w_vert[tap_index], grouped, preferred_element_type=jnp.float32
        )
    summed = summed.reshape(count_lev, channels, rows_lat, cols_lon) + b_vert[None, :, None, None]
    return jax.nn.gelu(summed).astype(jnp.bfloat16)


def local(fields, ocean_mask, norm_gain, w_vert, b_vert, w_horiz, b_horiz):
    normed = normalize(fields, norm_gain)
    reach = w_vert.shape[0] // 2
    columns = lax.all_to_all(normed, "lat_lo", split_axis=2, concat_axis=0, tiled=True)
    count_lev = columns.shape[0]
    upper = lax.axis_index("lat_hi") == 0
    send = jnp.where(upper, columns[count_lev - reach :], columns[:reach])
    recv = lax.ppermute(send, "lat_hi", [(0, 1), (1, 0)])
    zeros = jnp.zeros_like(recv)
    below = jnp.where(upper, zeros, recv)
    above = jnp.where(upper, recv, zeros)
    padded = jnp.concatenate([below, columns, above], axis=0)
    taps = [padded[tap_index : tap_index + count_lev] for tap_index in range(w_vert.shape[0])]
    mixed = lax.all_to_all(
        vertical(taps, w_vert, b_vert), "lat_lo", split_axis=0, concat_axis=2, tiled=True
    )
    masked = mixed * ocean_mask[:, None].astype(jnp.bfloat16)
    conv = horizontal(masked, w_horiz)
    ocean = ocean_mask[:, None].astype(jnp.float32)
    return (fields.astype(jnp.float32) + ocean * (conv + b_horiz[None, :, None, None])).astype(
        jnp.bfloat16
    )


def horizontal_kernel(
    count, x_ref, w_ref, right_ref, left_ref, o_ref, yl_ref, yr_ref,
    from_left, from_right, send_sems, recv_sems,
):
    me = lax.axis_index("lon")
    right, left = lax.rem(me + 1, count), lax.rem(me + count - 1, count)
    rest = (lax.axis_index("lat_hi"), lax.axis_index("lat_lo"))
    mesh_ids = pl.DeviceIdType.MESH
    barrier = pltpu.get_barrier_semaphore()
    for neighbour in (left, right):
        pl.semaphore_signal(barrier, inc=1, device_id=(neighbour,) + rest, device_id_type=mesh_ids)

    rows, channels, cols_lon = o_ref.shape
    taps = w_ref.shape[0] // channels
    segment = x_ref.shape[1] // (rows + taps - 1)
    chunk = 8
    weights = w_ref[...]
    for start in range(0, rows, chunk):
        window = jnp.concatenate(
            [
                x_ref[:, (start + row_tap) * segment : (start + row_tap + chunk) * segment]
                for row_tap in range(taps)
            ],
            axis=0,
        )
        partial = jnp.dot(weights, window, preferred_element_type=jnp.float32)
        total = partial[:channels]
        for col_tap in range(1, taps):
            piece = partial[col_tap * channels : (col_tap + 1) * channels]
            total = total + pltpu.roll(piece, chunk * segment - col_tap, 1)
        for row in range(chunk):
            o_ref[start + row] = total[:, row * segment : row * segment + cols_lon]

    pl.semaphore_wait(barrier, 2)
    to_right = pltpu.make_async_remote_copy(
        src_ref=right_ref,
        dst_ref=from_left,
        send_sem=send_sems.at[0],
        recv_sem=recv_sems.at[0],
        device_id=(right,) + rest,
        device_id_type=mesh_ids,
    )
    to_left = pltpu.make_async_remote_copy(
        src_ref=left_ref,
        dst_ref=from_right,
        send_sem=send_sems.at[1],
        recv_sem=recv_sems.at[1],
        device_id=(left,) + rest,
        device_id_type=mesh_ids,
    )
    to_right.start()
    to_left.start()
    to_right.wait()
    to_left.wait()
    yl_ref[...] = jnp.dot(weights, from_left[...], preferred_element_type=jnp.float32)
    yr_ref[...] = jnp.dot(weights, from_right[...], preferred_element_type=jnp.float32)


def stacked_edge(edge, reach_row):
    channels, rows_lat, width = edge.shape
    padded = jnp.pad(edge, ((0, 0), (reach_row, reach_row), (0, 0)))
    return jnp.concatenate(
        [
            padded[:, row_tap : row_tap + rows_lat].reshape(channels, rows_lat * width)
            for row_tap in range(2 * reach_row + 1)
        ],
        axis=0,
    )


def horizontal(masked, w_horiz):
    row_taps, channels, col_taps, _ = w_horiz.shape
    reach_row, reach_col = row_taps // 2, col_taps // 2
    _, _, rows_lat, cols_lon = masked.shape
    count = lax.axis_size("lon")
    segment = 2 * cols_lon
    block = masked[0]
    side = jnp.zeros((channels, rows_lat, reach_col), masked.dtype)
    gap = jnp.zeros((channels, rows_lat, segment - cols_lon - 2 * reach_col), masked.dtype)
    wide = jnp.concatenate([side, block, side, gap], axis=2)
    wide = jnp.pad(wide, ((0, 0), (reach_row, reach_row), (0, 0)))
    wide = wide.reshape(channels, (rows_lat + 2 * reach_row) * segment)
    weights = jnp.transpose(w_horiz, (2, 1, 0, 3)).reshape(col_taps * channels, row_taps * channels)
    right_edge = stacked_edge(block[:, :, cols_lon - reach_col :], reach_row)
    left_edge = stacked_edge(block[:, :, :reach_col], reach_row)
    vmem = pl.BlockSpec(memory_space=pltpu.VMEM)
    edge_out = jax.ShapeDtypeStruct((weights.shape[0], right_edge.shape[1]), jnp.float32)
    conv, from_left, from_right = pl.pallas_call(
        functools.partial(horizontal_kernel, count),
        out_shape=(
            jax.ShapeDtypeStruct((rows_lat, channels, cols_lon), jnp.float32),
            edge_out,
            edge_out,
        ),
        in_specs=[vmem] * 4,
        out_specs=(vmem,) * 3,
        scratch_shapes=[
            pltpu.VMEM(right_edge.shape, right_edge.dtype),
            pltpu.VMEM(left_edge.shape, left_edge.dtype),
            pltpu.SemaphoreType.DMA((2,)),
            pltpu.SemaphoreType.DMA((2,)),
        ],
        compiler_params=pltpu.CompilerParams(collective_id=0, has_side_effects=True),
        cost_estimate=pl.CostEstimate(
            flops=2 * rows_lat * segment * weights.shape[0] * weights.shape[1],
            bytes_accessed=wide.size * 2 + weights.size * 2 + rows_lat * channels * cols_lon * 4,
            transcendentals=0,
        ),
    )(wide, weights, right_edge, left_edge)
    conv = jnp.transpose(conv, (1, 0, 2))
    lanes = lambda y, tap, col: y[tap * channels : (tap + 1) * channels, col::reach_col]
    first = lanes(from_left, 0, 0) + lanes(from_left, 1, 1)
    second = lanes(from_left, 0, 1)
    before_last = lanes(from_right, col_taps - 1, 0)
    last = lanes(from_right, col_taps - 2, 0) + lanes(from_right, col_taps - 1, 1)
    middle = jnp.zeros((channels, rows_lat, cols_lon - 2 * reach_col), jnp.float32)
    fix = jnp.concatenate(
        [first[..., None], second[..., None], middle, before_last[..., None], last[..., None]], axis=2
    )
    return (conv + fix)[None]


def solution(mesh):
    halves = 2
    lon_count, lat_count = mesh.devices.shape
    split = jax.sharding.Mesh(
        mesh.devices.reshape(lon_count, halves, lat_count // halves), ("lon", "lat_hi", "lat_lo")
    )
    lat = ("lat_hi", "lat_lo")
    placed = (P(lat, None, None, "lon"), P(lat, None, "lon"), P(), P(), P(), P(), P())
    return jax.shard_map(
        local, mesh=split, in_specs=placed, out_specs=P(lat, None, None, "lon"), check_vma=False
    )
```

```python
import functools

import jax
from jax.experimental import pallas as pl
from jax.experimental.pallas import tpu as pltpu
import jax.numpy as jnp
from jax import lax
from jax.sharding import PartitionSpec as P


def normalize(block, norm_gain):
    values = block.astype(jnp.float32)
    center = jnp.mean(values, axis=1, keepdims=True)
    spread = jnp.mean((values - center) ** 2, axis=1, keepdims=True)
    return ((values - center) * lax.rsqrt(spread + 1e-05) * norm_gain[None, :, None, None]).astype(
        jnp.bfloat16
    )


def vertical(taps, w_vert, b_vert):
    count_lev, channels, rows_lat, cols_lon = taps[0].shape
    groups, width_in, width_out = (w_vert.shape[1], w_vert.shape[2], w_vert.shape[3])
    summed = jnp.zeros((count_lev, groups, width_out, rows_lat, cols_lon), jnp.float32)
    for tap_index in range(len(taps)):
        grouped = taps[tap_index].reshape(count_lev, groups, width_in, rows_lat, cols_lon)
        summed = summed + jnp.einsum(
            "gio,ngiab->ngoab", w_vert[tap_index], grouped, preferred_element_type=jnp.float32
        )
    summed = summed.reshape(count_lev, channels, rows_lat, cols_lon) + b_vert[None, :, None, None]
    return jax.nn.gelu(summed).astype(jnp.bfloat16)


def local(fields, ocean_mask, norm_gain, w_vert, b_vert, w_horiz, b_horiz):
    normed = normalize(fields, norm_gain)
    reach = w_vert.shape[0] // 2
    columns = lax.all_to_all(normed, "lat_lo", split_axis=2, concat_axis=0, tiled=True)
    count_lev = columns.shape[0]
    upper = lax.axis_index("lat_hi") == 0
    send = jnp.where(upper, columns[count_lev - reach :], columns[:reach])
    recv = lax.ppermute(send, "lat_hi", [(0, 1), (1, 0)])
    zeros = jnp.zeros_like(recv)
    below = jnp.where(upper, zeros, recv)
    above = jnp.where(upper, recv, zeros)
    padded = jnp.concatenate([below, columns, above], axis=0)
    taps = [padded[tap_index : tap_index + count_lev] for tap_index in range(w_vert.shape[0])]
    mixed = lax.all_to_all(
        vertical(taps, w_vert, b_vert), "lat_lo", split_axis=0, concat_axis=2, tiled=True
    )
    masked = mixed * ocean_mask[:, None].astype(jnp.bfloat16)
    conv = horizontal(masked, w_horiz)
    ocean = ocean_mask[:, None].astype(jnp.float32)
    return (fields.astype(jnp.float32) + ocean * (conv + b_horiz[None, :, None, None])).astype(
        jnp.bfloat16
    )


def horizontal_kernel(
    count, x_ref, w_ref, right_ref, left_ref, o_ref, fix_ref, from_left, from_right, send_sems, recv_sems,
):
    me = lax.axis_index("lon")
    right, left = lax.rem(me + 1, count), lax.rem(me + count - 1, count)
    rest = (lax.axis_index("lat_hi"), lax.axis_index("lat_lo"))
    mesh_ids = pl.DeviceIdType.MESH
    barrier = pltpu.get_barrier_semaphore()
    for neighbour in (left, right):
        pl.semaphore_signal(barrier, inc=1, device_id=(neighbour,) + rest, device_id_type=mesh_ids)

    rows, channels, cols_lon = o_ref.shape
    taps = w_ref.shape[0] // channels
    segment = x_ref.shape[1] // (rows + taps - 1)
    chunk = 8
    weights = w_ref[...]
    for start in range(0, rows, chunk):
        window = jnp.concatenate(
            [
                x_ref[:, (start + row_tap) * segment : (start + row_tap + chunk) * segment]
                for row_tap in range(taps)
            ],
            axis=0,
        )
        partial = jnp.dot(weights, window, preferred_element_type=jnp.float32)
        total = partial[:channels]
        for col_tap in range(1, taps):
            piece = partial[col_tap * channels : (col_tap + 1) * channels]
            total = total + pltpu.roll(piece, chunk * segment - col_tap, 1)
        for row in range(chunk):
            o_ref[start + row] = total[:, row * segment : row * segment + cols_lon]

    pl.semaphore_wait(barrier, 2)
    to_right = pltpu.make_async_remote_copy(
        src_ref=right_ref,
        dst_ref=from_left,
        send_sem=send_sems.at[0],
        recv_sem=recv_sems.at[0],
        device_id=(right,) + rest,
        device_id_type=mesh_ids,
    )
    to_left = pltpu.make_async_remote_copy(
        src_ref=left_ref,
        dst_ref=from_right,
        send_sem=send_sems.at[1],
        recv_sem=recv_sems.at[1],
        device_id=(left,) + rest,
        device_id_type=mesh_ids,
    )
    to_right.start()
    to_left.start()
    to_right.wait()
    to_left.wait()
    mix = lambda edge: jnp.dot(weights, edge, preferred_element_type=jnp.float32)
    near_left, far_left = mix(from_left[0]), mix(from_left[1])
    near_right, far_right = mix(from_right[0]), mix(from_right[1])
    tap = lambda y, col_tap: y[col_tap * channels : (col_tap + 1) * channels]
    fix_ref[0] = tap(near_left, 0) + tap(far_left, 1)
    fix_ref[1] = tap(far_left, 0)
    fix_ref[2] = tap(near_right, taps - 1)
    fix_ref[3] = tap(near_right, taps - 2) + tap(far_right, taps - 1)


def stacked_edge(edge, reach_row):
    channels, rows_lat, width = edge.shape
    padded = jnp.pad(edge, ((0, 0), (reach_row, reach_row), (0, 0)))
    return jnp.stack(
        [
            jnp.concatenate(
                [padded[:, row_tap : row_tap + rows_lat, col] for row_tap in range(2 * reach_row + 1)],
                axis=0,
            )
            for col in range(width)
        ]
    )


def horizontal(masked, w_horiz):
    row_taps, channels, col_taps, _ = w_horiz.shape
    reach_row, reach_col = row_taps // 2, col_taps // 2
    _, _, rows_lat, cols_lon = masked.shape
    count = lax.axis_size("lon")
    segment = 2 * cols_lon
    block = masked[0]
    side = jnp.zeros((channels, rows_lat, reach_col), masked.dtype)
    gap = jnp.zeros((channels, rows_lat, segment - cols_lon - 2 * reach_col), masked.dtype)
    wide = jnp.concatenate([side, block, side, gap], axis=2)
    wide = jnp.pad(wide, ((0, 0), (reach_row, reach_row), (0, 0)))
    wide = wide.reshape(channels, (rows_lat + 2 * reach_row) * segment)
    weights = jnp.transpose(w_horiz, (2, 1, 0, 3)).reshape(col_taps * channels, row_taps * channels)
    right_edge = stacked_edge(block[:, :, cols_lon - reach_col :], reach_row)
    left_edge = stacked_edge(block[:, :, :reach_col], reach_row)
    vmem = pl.BlockSpec(memory_space=pltpu.VMEM)
    conv, fix = pl.pallas_call(
        functools.partial(horizontal_kernel, count),
        out_shape=(
            jax.ShapeDtypeStruct((rows_lat, channels, cols_lon), jnp.float32),
            jax.ShapeDtypeStruct((2 * reach_col, channels, rows_lat), jnp.float32),
        ),
        in_specs=[vmem] * 4,
        out_specs=(vmem,) * 2,
        scratch_shapes=[
            pltpu.VMEM(right_edge.shape, right_edge.dtype),
            pltpu.VMEM(left_edge.shape, left_edge.dtype),
            pltpu.SemaphoreType.DMA((2,)),
            pltpu.SemaphoreType.DMA((2,)),
        ],
        compiler_params=pltpu.CompilerParams(collective_id=0, has_side_effects=True),
        cost_estimate=pl.CostEstimate(
            flops=2 * rows_lat * segment * weights.shape[0] * weights.shape[1],
            bytes_accessed=wide.size * 2 + weights.size * 2 + rows_lat * channels * cols_lon * 4,
            transcendentals=0,
        ),
    )(wide, weights, right_edge, left_edge)
    conv = jnp.transpose(conv, (1, 0, 2))
    column = lax.broadcasted_iota(jnp.int32, conv.shape, 2)
    edge_cols = (0, 1, cols_lon - 2, cols_lon - 1)
    for index, col in enumerate(edge_cols):
        conv = conv + jnp.where(column == col, fix[index][..., None], 0.0)
    return conv[None]


def solution(mesh):
    halves = 2
    lon_count, lat_count = mesh.devices.shape
    split = jax.sharding.Mesh(
        mesh.devices.reshape(lon_count, halves, lat_count // halves), ("lon", "lat_hi", "lat_lo")
    )
    lat = ("lat_hi", "lat_lo")
    placed = (P(lat, None, None, "lon"), P(lat, None, "lon"), P(), P(), P(), P(), P())
    return jax.shard_map(
        local, mesh=split, in_specs=placed, out_specs=P(lat, None, None, "lon"), check_vma=False
    )
```

```python
import functools

import jax
from jax.experimental import pallas as pl
from jax.experimental.pallas import tpu as pltpu
import jax.numpy as jnp
from jax import lax
from jax.sharding import PartitionSpec as P


def normalize_kernel(x_ref, g_ref, o_ref):
    values = x_ref[...].astype(jnp.float32)
    channels = values.shape[1]
    center = jnp.sum(values, axis=1, keepdims=True) / channels
    spread = jnp.sum((values - center) ** 2, axis=1, keepdims=True) / channels
    scale = lax.rsqrt(spread + 1e-05)
    o_ref[...] = ((values - center) * scale * g_ref[...]).astype(o_ref.dtype)


def normalize(block, norm_gain):
    vmem = pl.BlockSpec(memory_space=pltpu.VMEM)
    gain = jnp.broadcast_to(norm_gain[None, :, None, None], (1, norm_gain.shape[0], 1, block.shape[3]))
    return pl.pallas_call(
        normalize_kernel,
        out_shape=jax.ShapeDtypeStruct(block.shape, jnp.bfloat16),
        in_specs=[vmem, vmem],
        out_specs=vmem,
    )(block, gain)


def vertical(taps, w_vert, b_vert):
    count_lev, channels, rows_lat, cols_lon = taps[0].shape
    groups, width_in, width_out = (w_vert.shape[1], w_vert.shape[2], w_vert.shape[3])
    summed = jnp.zeros((count_lev, groups, width_out, rows_lat, cols_lon), jnp.float32)
    for tap_index in range(len(taps)):
        grouped = taps[tap_index].reshape(count_lev, groups, width_in, rows_lat, cols_lon)
        summed = summed + jnp.einsum(
            "gio,ngiab->ngoab", w_vert[tap_index], grouped, preferred_element_type=jnp.float32
        )
    summed = summed.reshape(count_lev, channels, rows_lat, cols_lon) + b_vert[None, :, None, None]
    return jax.nn.gelu(summed).astype(jnp.bfloat16)


def local(fields, ocean_mask, norm_gain, w_vert, b_vert, w_horiz, b_horiz):
    normed = normalize(fields, norm_gain)
    reach = w_vert.shape[0] // 2
    columns = lax.all_to_all(normed, "lat_lo", split_axis=2, concat_axis=0, tiled=True)
    count_lev = columns.shape[0]
    upper = lax.axis_index("lat_hi") == 0
    send = jnp.where(upper, columns[count_lev - reach :], columns[:reach])
    recv = lax.ppermute(send, "lat_hi", [(0, 1), (1, 0)])
    zeros = jnp.zeros_like(recv)
    below = jnp.where(upper, zeros, recv)
    above = jnp.where(upper, recv, zeros)
    padded = jnp.concatenate([below, columns, above], axis=0)
    taps = [padded[tap_index : tap_index + count_lev] for tap_index in range(w_vert.shape[0])]
    mixed = lax.all_to_all(
        vertical(taps, w_vert, b_vert), "lat_lo", split_axis=0, concat_axis=2, tiled=True
    )
    masked = mixed * ocean_mask[:, None].astype(jnp.bfloat16)
    conv = horizontal(masked, w_horiz)
    ocean = ocean_mask[:, None].astype(jnp.float32)
    return (fields.astype(jnp.float32) + ocean * (conv + b_horiz[None, :, None, None])).astype(
        jnp.bfloat16
    )


def horizontal_kernel(x_ref, w_ref, o_ref):
    rows, channels, cols_lon = o_ref.shape
    taps = w_ref.shape[0] // channels
    segment = x_ref.shape[1] // (rows + taps - 1)
    chunk = 8
    weights = w_ref[...]
    for start in range(0, rows, chunk):
        window = jnp.concatenate(
            [
                x_ref[:, (start + row_tap) * segment : (start + row_tap + chunk) * segment]
                for row_tap in range(taps)
            ],
            axis=0,
        )
        partial = jnp.dot(weights, window, preferred_element_type=jnp.float32)
        total = partial[:channels]
        for col_tap in range(1, taps):
            piece = partial[col_tap * channels : (col_tap + 1) * channels]
            total = total + pltpu.roll(piece, chunk * segment - col_tap, 1)
        for row in range(chunk):
            o_ref[start + row] = total[:, row * segment : row * segment + cols_lon]


def horizontal(masked, w_horiz):
    row_taps, channels, col_taps, _ = w_horiz.shape
    reach_row, reach_col = row_taps // 2, col_taps // 2
    _, _, rows_lat, cols_lon = masked.shape
    before, after = lon_halo(masked, reach_col)
    segment = 2 * cols_lon
    gap = jnp.zeros(masked.shape[:3] + (segment - cols_lon - 2 * reach_col,), masked.dtype)
    wide = jnp.concatenate([before, masked, after, gap], axis=3)[0]
    wide = jnp.pad(wide, ((0, 0), (reach_row, reach_row), (0, 0)))
    wide = wide.reshape(channels, (rows_lat + 2 * reach_row) * segment)
    weights = jnp.transpose(w_horiz, (2, 1, 0, 3)).reshape(col_taps * channels, row_taps * channels)
    conv = pl.pallas_call(
        horizontal_kernel,
        out_shape=jax.ShapeDtypeStruct((rows_lat, channels, cols_lon), jnp.float32),
        in_specs=[pl.BlockSpec(memory_space=pltpu.VMEM)] * 2,
        out_specs=pl.BlockSpec(memory_space=pltpu.VMEM),
        cost_estimate=pl.CostEstimate(
            flops=2 * rows_lat * segment * weights.shape[0] * weights.shape[1],
            bytes_accessed=wide.size * 2 + weights.size * 2 + rows_lat * channels * cols_lon * 4,
            transcendentals=0,
        ),
    )(wide, weights)
    return jnp.transpose(conv, (1, 0, 2))[None]


def halo_kernel(count, left_edge, right_edge, from_left, from_right, send_sems, recv_sems):
    me = lax.axis_index("lon")
    right, left = lax.rem(me + 1, count), lax.rem(me + count - 1, count)
    rest = (lax.axis_index("lat_hi"), lax.axis_index("lat_lo"))
    mesh_ids = pl.DeviceIdType.MESH
    barrier = pltpu.get_barrier_semaphore()
    for neighbour in (left, right):
        pl.semaphore_signal(barrier, inc=1, device_id=(neighbour,) + rest, device_id_type=mesh_ids)
    pl.semaphore_wait(barrier, 2)
    to_right = pltpu.make_async_remote_copy(
        src_ref=right_edge,
        dst_ref=from_left,
        send_sem=send_sems.at[0],
        recv_sem=recv_sems.at[0],
        device_id=(right,) + rest,
        device_id_type=mesh_ids,
    )
    to_left = pltpu.make_async_remote_copy(
        src_ref=left_edge,
        dst_ref=from_right,
        send_sem=send_sems.at[1],
        recv_sem=recv_sems.at[1],
        device_id=(left,) + rest,
        device_id_type=mesh_ids,
    )
    to_right.start()
    to_left.start()
    to_right.wait()
    to_left.wait()


def lon_halo(block, width):
    count = lax.axis_size("lon")
    length = block.shape[-1]
    edge_shape = block.shape[:-1] + (width,)
    flat = (block.shape[1], block.shape[2] * width)
    left_edge = block[..., :width].reshape(flat)
    right_edge = block[..., length - width :].reshape(flat)
    any_spec = pl.BlockSpec(memory_space=pl.ANY)
    from_left, from_right = pl.pallas_call(
        functools.partial(halo_kernel, count),
        out_shape=(jax.ShapeDtypeStruct(flat, block.dtype),) * 2,
        in_specs=[any_spec] * 2,
        out_specs=(any_spec,) * 2,
        scratch_shapes=[pltpu.SemaphoreType.DMA((2,)), pltpu.SemaphoreType.DMA((2,))],
        compiler_params=pltpu.CompilerParams(collective_id=0, has_side_effects=True),
    )(left_edge, right_edge)
    return from_left.reshape(edge_shape), from_right.reshape(edge_shape)


def solution(mesh):
    halves = 2
    lon_count, lat_count = mesh.devices.shape
    split = jax.sharding.Mesh(
        mesh.devices.reshape(lon_count, halves, lat_count // halves), ("lon", "lat_hi", "lat_lo")
    )
    lat = ("lat_hi", "lat_lo")
    placed = (P(lat, None, None, "lon"), P(lat, None, "lon"), P(), P(), P(), P(), P())
    return jax.shard_map(
        local, mesh=split, in_specs=placed, out_specs=P(lat, None, None, "lon"), check_vma=False
    )
```

```python
import functools

import jax
from jax.experimental import pallas as pl
from jax.experimental.pallas import tpu as pltpu
import jax.numpy as jnp
from jax import lax
from jax.sharding import PartitionSpec as P


def normalize(block, norm_gain):
    values = block.astype(jnp.float32)
    center = jnp.mean(values, axis=1, keepdims=True)
    spread = jnp.mean((values - center) ** 2, axis=1, keepdims=True)
    return ((values - center) * lax.rsqrt(spread + 1e-05) * norm_gain[None, :, None, None]).astype(
        jnp.bfloat16
    )


def vertical(taps, w_vert, b_vert):
    count_lev, channels, rows_lat, cols_lon = taps[0].shape
    groups, width_in, width_out = (w_vert.shape[1], w_vert.shape[2], w_vert.shape[3])
    summed = jnp.zeros((count_lev, groups, width_out, rows_lat, cols_lon), jnp.float32)
    for tap_index in range(len(taps)):
        grouped = taps[tap_index].reshape(count_lev, groups, width_in, rows_lat, cols_lon)
        summed = summed + jnp.einsum(
            "gio,ngiab->ngoab", w_vert[tap_index], grouped, preferred_element_type=jnp.float32
        )
    summed = summed.reshape(count_lev, channels, rows_lat, cols_lon) + b_vert[None, :, None, None]
    return jax.nn.gelu(summed).astype(jnp.bfloat16)


def column_kernel(halves, group, reach, blocks_ref, out_ref, send_sems, recv_sems, own_sem):
    lon = lax.axis_index("lon")
    half, place = lax.axis_index("lat_hi"), lax.axis_index("lat_lo")
    upper = halves - 1 - half
    mesh_ids = pl.DeviceIdType.MESH
    partner = (lon, upper, place)
    barrier = pltpu.get_barrier_semaphore()
    for other in range(group):

        @pl.when(place != other)
        def _():
            pl.semaphore_signal(barrier, inc=1, device_id=(lon, half, other), device_id_type=mesh_ids)

    pl.semaphore_signal(barrier, inc=1, device_id=partner, device_id_type=mesh_ids)
    pl.semaphore_wait(barrier, group)

    own = pltpu.make_async_copy(blocks_ref.at[place], out_ref.at[reach + place], own_sem.at[0])
    own.start()

    def inward(other):
        return pltpu.make_async_remote_copy(
            src_ref=blocks_ref.at[other],
            dst_ref=out_ref.at[reach + place],
            send_sem=send_sems.at[other],
            recv_sem=recv_sems.at[reach + place],
            device_id=(lon, half, other),
            device_id_type=mesh_ids,
        )

    def arrival(slot):
        return pltpu.make_async_remote_copy(
            src_ref=blocks_ref.at[0],
            dst_ref=out_ref.at[slot],
            send_sem=send_sems.at[group],
            recv_sem=recv_sems.at[slot],
            device_id=partner,
            device_id_type=mesh_ids,
        )

    for other in range(group):

        @pl.when(place != other)
        def _():
            inward(other).start()

    edge = (group - reach) * upper
    mine = jnp.logical_and(place >= edge, place < edge + reach)
    forwards = []
    for level in range(reach):
        source = edge + level

        @pl.when(place != source)
        def _():
            arrival(reach + source).wait_recv()

        @pl.when(place == source)
        def _():
            own.wait()

        forward = pltpu.make_async_remote_copy(
            src_ref=out_ref.at[reach + source],
            dst_ref=out_ref.at[(group + reach) * half + level],
            send_sem=send_sems.at[group + level],
            recv_sem=recv_sems.at[(group + reach) * half + level],
            device_id=partner,
            device_id_type=mesh_ids,
        )
        forward.start()
        forwards.append(forward)

    for other in range(group):
        boundary = jnp.logical_and(other >= edge, other < edge + reach)

        @pl.when(jnp.logical_and(place != other, jnp.logical_not(boundary)))
        def _():
            arrival(reach + other).wait_recv()

    @pl.when(jnp.logical_not(mine))
    def _():
        own.wait()

    for level in range(reach):
        arrival((group + reach) * upper + level).wait_recv()
    for other in range(group):

        @pl.when(place != other)
        def _():
            inward(other).wait_send()

    for forward in forwards:
        forward.wait_send()


def columns_of(normed, reach):
    halves, group = lax.axis_size("lat_hi"), lax.axis_size("lat_lo")
    _, channels, rows_lat, cols_lon = normed.shape
    rows = rows_lat // group
    blocks = normed[0].reshape(channels, group, rows, cols_lon).transpose(1, 0, 2, 3)
    any_spec = pl.BlockSpec(memory_space=pl.ANY)
    slots = group + 2 * reach
    out = pl.pallas_call(
        functools.partial(column_kernel, halves, group, reach),
        out_shape=jax.ShapeDtypeStruct((slots, channels, rows, cols_lon), normed.dtype),
        in_specs=[any_spec],
        out_specs=any_spec,
        scratch_shapes=[
            pltpu.SemaphoreType.DMA((group + reach,)),
            pltpu.SemaphoreType.DMA((slots,)),
            pltpu.SemaphoreType.DMA((1,)),
        ],
        compiler_params=pltpu.CompilerParams(collective_id=1, has_side_effects=True),
    )(blocks)
    half = lax.axis_index("lat_hi")
    slot = lax.broadcasted_iota(jnp.int32, (slots, 1, 1, 1), 0)
    real = jnp.logical_and(slot >= reach * (1 - half), slot < slots - reach * half)
    return jnp.where(real, out, jnp.zeros_like(out))


def local(fields, ocean_mask, norm_gain, w_vert, b_vert, w_horiz, b_horiz):
    normed = normalize(fields, norm_gain)
    reach = w_vert.shape[0] // 2
    padded = columns_of(normed, reach)
    count_lev = padded.shape[0] - 2 * reach
    taps = [padded[tap_index : tap_index + count_lev] for tap_index in range(w_vert.shape[0])]
    mixed = lax.all_to_all(
        vertical(taps, w_vert, b_vert), "lat_lo", split_axis=0, concat_axis=2, tiled=True
    )
    masked = mixed * ocean_mask[:, None].astype(jnp.bfloat16)
    conv = horizontal(masked, w_horiz)
    ocean = ocean_mask[:, None].astype(jnp.float32)
    return (fields.astype(jnp.float32) + ocean * (conv + b_horiz[None, :, None, None])).astype(
        jnp.bfloat16
    )


def horizontal_kernel(x_ref, w_ref, o_ref):
    rows, channels, cols_lon = o_ref.shape
    taps = w_ref.shape[0] // channels
    segment = x_ref.shape[1] // (rows + taps - 1)
    chunk = 8
    weights = w_ref[...]
    for start in range(0, rows, chunk):
        window = jnp.concatenate(
            [
                x_ref[:, (start + row_tap) * segment : (start + row_tap + chunk) * segment]
                for row_tap in range(taps)
            ],
            axis=0,
        )
        partial = jnp.dot(weights, window, preferred_element_type=jnp.float32)
        total = partial[:channels]
        for col_tap in range(1, taps):
            piece = partial[col_tap * channels : (col_tap + 1) * channels]
            total = total + pltpu.roll(piece, chunk * segment - col_tap, 1)
        for row in range(chunk):
            o_ref[start + row] = total[:, row * segment : row * segment + cols_lon]


def horizontal(masked, w_horiz):
    row_taps, channels, col_taps, _ = w_horiz.shape
    reach_row, reach_col = row_taps // 2, col_taps // 2
    _, _, rows_lat, cols_lon = masked.shape
    before, after = lon_halo(masked, reach_col)
    segment = 2 * cols_lon
    gap = jnp.zeros(masked.shape[:3] + (segment - cols_lon - 2 * reach_col,), masked.dtype)
    wide = jnp.concatenate([before, masked, after, gap], axis=3)[0]
    wide = jnp.pad(wide, ((0, 0), (reach_row, reach_row), (0, 0)))
    wide = wide.reshape(channels, (rows_lat + 2 * reach_row) * segment)
    weights = jnp.transpose(w_horiz, (2, 1, 0, 3)).reshape(col_taps * channels, row_taps * channels)
    conv = pl.pallas_call(
        horizontal_kernel,
        out_shape=jax.ShapeDtypeStruct((rows_lat, channels, cols_lon), jnp.float32),
        in_specs=[pl.BlockSpec(memory_space=pltpu.VMEM)] * 2,
        out_specs=pl.BlockSpec(memory_space=pltpu.VMEM),
        cost_estimate=pl.CostEstimate(
            flops=2 * rows_lat * segment * weights.shape[0] * weights.shape[1],
            bytes_accessed=wide.size * 2 + weights.size * 2 + rows_lat * channels * cols_lon * 4,
            transcendentals=0,
        ),
    )(wide, weights)
    return jnp.transpose(conv, (1, 0, 2))[None]


def halo_kernel(count, left_edge, right_edge, from_left, from_right, send_sems, recv_sems):
    me = lax.axis_index("lon")
    right, left = lax.rem(me + 1, count), lax.rem(me + count - 1, count)
    rest = (lax.axis_index("lat_hi"), lax.axis_index("lat_lo"))
    mesh_ids = pl.DeviceIdType.MESH
    barrier = pltpu.get_barrier_semaphore()
    for neighbour in (left, right):
        pl.semaphore_signal(barrier, inc=1, device_id=(neighbour,) + rest, device_id_type=mesh_ids)
    pl.semaphore_wait(barrier, 2)
    to_right = pltpu.make_async_remote_copy(
        src_ref=right_edge,
        dst_ref=from_left,
        send_sem=send_sems.at[0],
        recv_sem=recv_sems.at[0],
        device_id=(right,) + rest,
        device_id_type=mesh_ids,
    )
    to_left = pltpu.make_async_remote_copy(
        src_ref=left_edge,
        dst_ref=from_right,
        send_sem=send_sems.at[1],
        recv_sem=recv_sems.at[1],
        device_id=(left,) + rest,
        device_id_type=mesh_ids,
    )
    to_right.start()
    to_left.start()
    to_right.wait()
    to_left.wait()


def lon_halo(block, width):
    count = lax.axis_size("lon")
    length = block.shape[-1]
    edge_shape = block.shape[:-1] + (width,)
    flat = (block.shape[1], block.shape[2] * width)
    left_edge = block[..., :width].reshape(flat)
    right_edge = block[..., length - width :].reshape(flat)
    any_spec = pl.BlockSpec(memory_space=pl.ANY)
    from_left, from_right = pl.pallas_call(
        functools.partial(halo_kernel, count),
        out_shape=(jax.ShapeDtypeStruct(flat, block.dtype),) * 2,
        in_specs=[any_spec] * 2,
        out_specs=(any_spec,) * 2,
        scratch_shapes=[pltpu.SemaphoreType.DMA((2,)), pltpu.SemaphoreType.DMA((2,))],
        compiler_params=pltpu.CompilerParams(collective_id=0, has_side_effects=True),
    )(left_edge, right_edge)
    return from_left.reshape(edge_shape), from_right.reshape(edge_shape)


def solution(mesh):
    halves = 2
    lon_count, lat_count = mesh.devices.shape
    split = jax.sharding.Mesh(
        mesh.devices.reshape(lon_count, halves, lat_count // halves), ("lon", "lat_hi", "lat_lo")
    )
    lat = ("lat_hi", "lat_lo")
    placed = (P(lat, None, None, "lon"), P(lat, None, "lon"), P(), P(), P(), P(), P())
    return jax.shard_map(
        local, mesh=split, in_specs=placed, out_specs=P(lat, None, None, "lon"), check_vma=False
    )
```

```python
import functools

import jax
from jax.experimental import pallas as pl
from jax.experimental.pallas import tpu as pltpu
import jax.numpy as jnp
from jax import lax
from jax.sharding import PartitionSpec as P


def normalize(block, norm_gain):
    values = block.astype(jnp.float32)
    center = jnp.mean(values, axis=1, keepdims=True)
    spread = jnp.mean((values - center) ** 2, axis=1, keepdims=True)
    return ((values - center) * lax.rsqrt(spread + 1e-05) * norm_gain[None, :, None, None]).astype(
        jnp.bfloat16
    )


def vertical(taps, w_vert, b_vert):
    count_lev, channels, rows_lat, cols_lon = taps[0].shape
    groups, width_in, width_out = (w_vert.shape[1], w_vert.shape[2], w_vert.shape[3])
    summed = jnp.zeros((count_lev, groups, width_out, rows_lat, cols_lon), jnp.float32)
    for tap_index in range(len(taps)):
        grouped = taps[tap_index].reshape(count_lev, groups, width_in, rows_lat, cols_lon)
        summed = summed + jnp.einsum(
            "gio,ngiab->ngoab", w_vert[tap_index], grouped, preferred_element_type=jnp.float32
        )
    summed = summed.reshape(count_lev, channels, rows_lat, cols_lon) + b_vert[None, :, None, None]
    return jax.nn.gelu(summed).astype(jnp.bfloat16)


def column_kernel(halves, group, reach, blocks_ref, out_ref, send_sems, recv_sems, own_sem):
    cross = reach > 0
    lon = lax.axis_index("lon")
    half, place = lax.axis_index("lat_hi"), lax.axis_index("lat_lo")
    upper = halves - 1 - half
    mesh_ids = pl.DeviceIdType.MESH
    partner = (lon, upper, place)
    barrier = pltpu.get_barrier_semaphore()
    for other in range(group):

        @pl.when(place != other)
        def _():
            pl.semaphore_signal(barrier, inc=1, device_id=(lon, half, other), device_id_type=mesh_ids)

    if cross:
        pl.semaphore_signal(barrier, inc=1, device_id=partner, device_id_type=mesh_ids)
    pl.semaphore_wait(barrier, group - 1 + cross)

    own = pltpu.make_async_copy(blocks_ref.at[place], out_ref.at[reach + place], own_sem.at[0])
    own.start()

    def inward(other):
        return pltpu.make_async_remote_copy(
            src_ref=blocks_ref.at[other],
            dst_ref=out_ref.at[reach + place],
            send_sem=send_sems.at[other],
            recv_sem=recv_sems.at[reach + place],
            device_id=(lon, half, other),
            device_id_type=mesh_ids,
        )

    def arrival(slot):
        return pltpu.make_async_remote_copy(
            src_ref=blocks_ref.at[0],
            dst_ref=out_ref.at[slot],
            send_sem=send_sems.at[group],
            recv_sem=recv_sems.at[slot],
            device_id=partner,
            device_id_type=mesh_ids,
        )

    for other in range(group):

        @pl.when(place != other)
        def _():
            inward(other).start()

    edge = (group - reach) * upper
    mine = jnp.logical_and(place >= edge, place < edge + reach)
    forwards = []
    for level in range(reach):
        source = edge + level

        @pl.when(place != source)
        def _():
            arrival(reach + source).wait_recv()

        @pl.when(place == source)
        def _():
            own.wait()

        forward = pltpu.make_async_remote_copy(
            src_ref=out_ref.at[reach + source],
            dst_ref=out_ref.at[(group + reach) * half + level],
            send_sem=send_sems.at[group + level],
            recv_sem=recv_sems.at[(group + reach) * half + level],
            device_id=partner,
            device_id_type=mesh_ids,
        )
        forward.start()
        forwards.append(forward)

    for other in range(group):
        boundary = jnp.logical_and(other >= edge, other < edge + reach)

        @pl.when(jnp.logical_and(place != other, jnp.logical_not(boundary)))
        def _():
            arrival(reach + other).wait_recv()

    @pl.when(jnp.logical_not(mine))
    def _():
        own.wait()

    for level in range(reach):
        arrival((group + reach) * upper + level).wait_recv()
    for other in range(group):

        @pl.when(place != other)
        def _():
            inward(other).wait_send()

    for forward in forwards:
        forward.wait_send()


def exchange(blocks, reach, collective):
    halves, group = lax.axis_size("lat_hi"), lax.axis_size("lat_lo")
    any_spec = pl.BlockSpec(memory_space=pl.ANY)
    slots = group + 2 * reach
    return pl.pallas_call(
        functools.partial(column_kernel, halves, group, reach),
        out_shape=jax.ShapeDtypeStruct((slots,) + blocks.shape[1:], blocks.dtype),
        in_specs=[any_spec],
        out_specs=any_spec,
        scratch_shapes=[
            pltpu.SemaphoreType.DMA((group + reach,)),
            pltpu.SemaphoreType.DMA((slots,)),
            pltpu.SemaphoreType.DMA((1,)),
        ],
        compiler_params=pltpu.CompilerParams(collective_id=collective, has_side_effects=True),
    )(blocks)


def columns_of(normed, reach):
    group = lax.axis_size("lat_lo")
    _, channels, rows_lat, cols_lon = normed.shape
    rows = rows_lat // group
    blocks = normed[0].reshape(channels, group, rows, cols_lon).transpose(1, 0, 2, 3)
    out = exchange(blocks, reach, 1)
    slots = out.shape[0]
    half = lax.axis_index("lat_hi")
    slot = lax.broadcasted_iota(jnp.int32, (slots, 1, 1, 1), 0)
    real = jnp.logical_and(slot >= reach * (1 - half), slot < slots - reach * half)
    return jnp.where(real, out, jnp.zeros_like(out))


def rows_of(mixed):
    group, channels, rows, cols_lon = mixed.shape
    back = exchange(mixed, 0, 2)
    return back.transpose(1, 0, 2, 3).reshape(1, channels, group * rows, cols_lon)


def local(fields, ocean_mask, norm_gain, w_vert, b_vert, w_horiz, b_horiz):
    normed = normalize(fields, norm_gain)
    reach = w_vert.shape[0] // 2
    padded = columns_of(normed, reach)
    count_lev = padded.shape[0] - 2 * reach
    taps = [padded[tap_index : tap_index + count_lev] for tap_index in range(w_vert.shape[0])]
    mixed = rows_of(vertical(taps, w_vert, b_vert))
    masked = mixed * ocean_mask[:, None].astype(jnp.bfloat16)
    conv = horizontal(masked, w_horiz)
    ocean = ocean_mask[:, None].astype(jnp.float32)
    return (fields.astype(jnp.float32) + ocean * (conv + b_horiz[None, :, None, None])).astype(
        jnp.bfloat16
    )


def horizontal_kernel(x_ref, w_ref, o_ref):
    rows, channels, cols_lon = o_ref.shape
    taps = w_ref.shape[0] // channels
    segment = x_ref.shape[1] // (rows + taps - 1)
    chunk = 8
    weights = w_ref[...]
    for start in range(0, rows, chunk):
        window = jnp.concatenate(
            [
                x_ref[:, (start + row_tap) * segment : (start + row_tap + chunk) * segment]
                for row_tap in range(taps)
            ],
            axis=0,
        )
        partial = jnp.dot(weights, window, preferred_element_type=jnp.float32)
        total = partial[:channels]
        for col_tap in range(1, taps):
            piece = partial[col_tap * channels : (col_tap + 1) * channels]
            total = total + pltpu.roll(piece, chunk * segment - col_tap, 1)
        for row in range(chunk):
            o_ref[start + row] = total[:, row * segment : row * segment + cols_lon]


def horizontal(masked, w_horiz):
    row_taps, channels, col_taps, _ = w_horiz.shape
    reach_row, reach_col = row_taps // 2, col_taps // 2
    _, _, rows_lat, cols_lon = masked.shape
    before, after = lon_halo(masked, reach_col)
    segment = 2 * cols_lon
    gap = jnp.zeros(masked.shape[:3] + (segment - cols_lon - 2 * reach_col,), masked.dtype)
    wide = jnp.concatenate([before, masked, after, gap], axis=3)[0]
    wide = jnp.pad(wide, ((0, 0), (reach_row, reach_row), (0, 0)))
    wide = wide.reshape(channels, (rows_lat + 2 * reach_row) * segment)
    weights = jnp.transpose(w_horiz, (2, 1, 0, 3)).reshape(col_taps * channels, row_taps * channels)
    conv = pl.pallas_call(
        horizontal_kernel,
        out_shape=jax.ShapeDtypeStruct((rows_lat, channels, cols_lon), jnp.float32),
        in_specs=[pl.BlockSpec(memory_space=pltpu.VMEM)] * 2,
        out_specs=pl.BlockSpec(memory_space=pltpu.VMEM),
        cost_estimate=pl.CostEstimate(
            flops=2 * rows_lat * segment * weights.shape[0] * weights.shape[1],
            bytes_accessed=wide.size * 2 + weights.size * 2 + rows_lat * channels * cols_lon * 4,
            transcendentals=0,
        ),
    )(wide, weights)
    return jnp.transpose(conv, (1, 0, 2))[None]


def halo_kernel(count, left_edge, right_edge, from_left, from_right, send_sems, recv_sems):
    me = lax.axis_index("lon")
    right, left = lax.rem(me + 1, count), lax.rem(me + count - 1, count)
    rest = (lax.axis_index("lat_hi"), lax.axis_index("lat_lo"))
    mesh_ids = pl.DeviceIdType.MESH
    barrier = pltpu.get_barrier_semaphore()
    for neighbour in (left, right):
        pl.semaphore_signal(barrier, inc=1, device_id=(neighbour,) + rest, device_id_type=mesh_ids)
    pl.semaphore_wait(barrier, 2)
    to_right = pltpu.make_async_remote_copy(
        src_ref=right_edge,
        dst_ref=from_left,
        send_sem=send_sems.at[0],
        recv_sem=recv_sems.at[0],
        device_id=(right,) + rest,
        device_id_type=mesh_ids,
    )
    to_left = pltpu.make_async_remote_copy(
        src_ref=left_edge,
        dst_ref=from_right,
        send_sem=send_sems.at[1],
        recv_sem=recv_sems.at[1],
        device_id=(left,) + rest,
        device_id_type=mesh_ids,
    )
    to_right.start()
    to_left.start()
    to_right.wait()
    to_left.wait()


def lon_halo(block, width):
    count = lax.axis_size("lon")
    length = block.shape[-1]
    edge_shape = block.shape[:-1] + (width,)
    flat = (block.shape[1], block.shape[2] * width)
    left_edge = block[..., :width].reshape(flat)
    right_edge = block[..., length - width :].reshape(flat)
    any_spec = pl.BlockSpec(memory_space=pl.ANY)
    from_left, from_right = pl.pallas_call(
        functools.partial(halo_kernel, count),
        out_shape=(jax.ShapeDtypeStruct(flat, block.dtype),) * 2,
        in_specs=[any_spec] * 2,
        out_specs=(any_spec,) * 2,
        scratch_shapes=[pltpu.SemaphoreType.DMA((2,)), pltpu.SemaphoreType.DMA((2,))],
        compiler_params=pltpu.CompilerParams(collective_id=0, has_side_effects=True),
    )(left_edge, right_edge)
    return from_left.reshape(edge_shape), from_right.reshape(edge_shape)


def solution(mesh):
    halves = 2
    lon_count, lat_count = mesh.devices.shape
    split = jax.sharding.Mesh(
        mesh.devices.reshape(lon_count, halves, lat_count // halves), ("lon", "lat_hi", "lat_lo")
    )
    lat = ("lat_hi", "lat_lo")
    placed = (P(lat, None, None, "lon"), P(lat, None, "lon"), P(), P(), P(), P(), P())
    return jax.shard_map(
        local, mesh=split, in_specs=placed, out_specs=P(lat, None, None, "lon"), check_vma=False
    )
```

```python
import functools

import jax
from jax.experimental import pallas as pl
from jax.experimental.pallas import tpu as pltpu
import jax.numpy as jnp
from jax import lax
from jax.sharding import PartitionSpec as P


def normalize(block, norm_gain):
    values = block.astype(jnp.float32)
    center = jnp.mean(values, axis=1, keepdims=True)
    spread = jnp.mean((values - center) ** 2, axis=1, keepdims=True)
    return ((values - center) * lax.rsqrt(spread + 1e-05) * norm_gain[None, :, None, None]).astype(
        jnp.bfloat16
    )


def vertical(taps, w_vert, b_vert):
    count_lev, channels, rows_lat, cols_lon = taps[0].shape
    groups, width_in, width_out = (w_vert.shape[1], w_vert.shape[2], w_vert.shape[3])
    summed = jnp.zeros((count_lev, groups, width_out, rows_lat, cols_lon), jnp.float32)
    for tap_index in range(len(taps)):
        grouped = taps[tap_index].reshape(count_lev, groups, width_in, rows_lat, cols_lon)
        summed = summed + jnp.einsum(
            "gio,ngiab->ngoab", w_vert[tap_index], grouped, preferred_element_type=jnp.float32
        )
    summed = summed.reshape(count_lev, channels, rows_lat, cols_lon) + b_vert[None, :, None, None]
    return jax.nn.gelu(summed).astype(jnp.bfloat16)


def column_kernel(
    halves, group, reach, blocks_ref, out_ref, send_sems, recv_sems, own_sem, zero_ref, zero_sems
):
    cross = reach > 0
    lon = lax.axis_index("lon")
    half, place = lax.axis_index("lat_hi"), lax.axis_index("lat_lo")
    upper = halves - 1 - half
    mesh_ids = pl.DeviceIdType.MESH
    partner = (lon, upper, place)
    barrier = pltpu.get_barrier_semaphore()
    for other in range(group):

        @pl.when(place != other)
        def _():
            pl.semaphore_signal(barrier, inc=1, device_id=(lon, half, other), device_id_type=mesh_ids)

    if cross:
        pl.semaphore_signal(barrier, inc=1, device_id=partner, device_id_type=mesh_ids)
    pl.semaphore_wait(barrier, group - 1 + cross)

    own = pltpu.make_async_copy(blocks_ref.at[place], out_ref.at[reach + place], own_sem.at[0])
    own.start()
    zero_ref[...] = jnp.zeros(zero_ref.shape, zero_ref.dtype)
    blanks = [
        pltpu.make_async_copy(zero_ref, out_ref.at[(group + reach) * half + level], zero_sems.at[level])
        for level in range(reach)
    ]
    for blank in blanks:
        blank.start()

    def inward(other):
        return pltpu.make_async_remote_copy(
            src_ref=blocks_ref.at[other],
            dst_ref=out_ref.at[reach + place],
            send_sem=send_sems.at[other],
            recv_sem=recv_sems.at[reach + place],
            device_id=(lon, half, other),
            device_id_type=mesh_ids,
        )

    def arrival(slot):
        return pltpu.make_async_remote_copy(
            src_ref=blocks_ref.at[0],
            dst_ref=out_ref.at[slot],
            send_sem=send_sems.at[group],
            recv_sem=recv_sems.at[slot],
            device_id=partner,
            device_id_type=mesh_ids,
        )

    for other in range(group):

        @pl.when(place != other)
        def _():
            inward(other).start()

    edge = (group - reach) * upper
    mine = jnp.logical_and(place >= edge, place < edge + reach)
    forwards = []
    for level in range(reach):
        source = edge + level

        @pl.when(place != source)
        def _():
            arrival(reach + source).wait_recv()

        @pl.when(place == source)
        def _():
            own.wait()

        forward = pltpu.make_async_remote_copy(
            src_ref=out_ref.at[reach + source],
            dst_ref=out_ref.at[(group + reach) * half + level],
            send_sem=send_sems.at[group + level],
            recv_sem=recv_sems.at[(group + reach) * half + level],
            device_id=partner,
            device_id_type=mesh_ids,
        )
        forward.start()
        forwards.append(forward)

    for other in range(group):
        boundary = jnp.logical_and(other >= edge, other < edge + reach)

        @pl.when(jnp.logical_and(place != other, jnp.logical_not(boundary)))
        def _():
            arrival(reach + other).wait_recv()

    @pl.when(jnp.logical_not(mine))
    def _():
        own.wait()

    for level in range(reach):
        arrival((group + reach) * upper + level).wait_recv()
    for other in range(group):

        @pl.when(place != other)
        def _():
            inward(other).wait_send()

    for forward in forwards:
        forward.wait_send()
    for blank in blanks:
        blank.wait()


def exchange(blocks, reach, collective):
    halves, group = lax.axis_size("lat_hi"), lax.axis_size("lat_lo")
    any_spec = pl.BlockSpec(memory_space=pl.ANY)
    slots = group + 2 * reach
    return pl.pallas_call(
        functools.partial(column_kernel, halves, group, reach),
        out_shape=jax.ShapeDtypeStruct((slots,) + blocks.shape[1:], blocks.dtype),
        in_specs=[any_spec],
        out_specs=any_spec,
        scratch_shapes=[
            pltpu.SemaphoreType.DMA((group + reach,)),
            pltpu.SemaphoreType.DMA((slots,)),
            pltpu.SemaphoreType.DMA((1,)),
            pltpu.VMEM(blocks.shape[1:], blocks.dtype),
            pltpu.SemaphoreType.DMA((max(reach, 1),)),
        ],
        compiler_params=pltpu.CompilerParams(collective_id=collective, has_side_effects=True),
    )(blocks)


def columns_of(normed, reach):
    group = lax.axis_size("lat_lo")
    _, channels, rows_lat, cols_lon = normed.shape
    rows = rows_lat // group
    blocks = normed[0].reshape(channels, group, rows, cols_lon).transpose(1, 0, 2, 3)
    return exchange(blocks, reach, 1)


def rows_of(mixed):
    group, channels, rows, cols_lon = mixed.shape
    back = exchange(mixed, 0, 2)
    return back.transpose(1, 0, 2, 3).reshape(1, channels, group * rows, cols_lon)


def local(fields, ocean_mask, norm_gain, w_vert, b_vert, w_horiz, b_horiz):
    normed = normalize(fields, norm_gain)
    reach = w_vert.shape[0] // 2
    padded = columns_of(normed, reach)
    count_lev = padded.shape[0] - 2 * reach
    taps = [padded[tap_index : tap_index + count_lev] for tap_index in range(w_vert.shape[0])]
    mixed = rows_of(vertical(taps, w_vert, b_vert))
    masked = mixed * ocean_mask[:, None].astype(jnp.bfloat16)
    conv = horizontal(masked, w_horiz)
    ocean = ocean_mask[:, None].astype(jnp.float32)
    return (fields.astype(jnp.float32) + ocean * (conv + b_horiz[None, :, None, None])).astype(
        jnp.bfloat16
    )


def horizontal_kernel(x_ref, w_ref, o_ref):
    rows, channels, cols_lon = o_ref.shape
    taps = w_ref.shape[0] // channels
    segment = x_ref.shape[1] // (rows + taps - 1)
    chunk = 8
    weights = w_ref[...]
    for start in range(0, rows, chunk):
        window = jnp.concatenate(
            [
                x_ref[:, (start + row_tap) * segment : (start + row_tap + chunk) * segment]
                for row_tap in range(taps)
            ],
            axis=0,
        )
        partial = jnp.dot(weights, window, preferred_element_type=jnp.float32)
        total = partial[:channels]
        for col_tap in range(1, taps):
            piece = partial[col_tap * channels : (col_tap + 1) * channels]
            total = total + pltpu.roll(piece, chunk * segment - col_tap, 1)
        for row in range(chunk):
            o_ref[start + row] = total[:, row * segment : row * segment + cols_lon]


def horizontal(masked, w_horiz):
    row_taps, channels, col_taps, _ = w_horiz.shape
    reach_row, reach_col = row_taps // 2, col_taps // 2
    _, _, rows_lat, cols_lon = masked.shape
    before, after = lon_halo(masked, reach_col)
    segment = 2 * cols_lon
    gap = jnp.zeros(masked.shape[:3] + (segment - cols_lon - 2 * reach_col,), masked.dtype)
    wide = jnp.concatenate([before, masked, after, gap], axis=3)[0]
    wide = jnp.pad(wide, ((0, 0), (reach_row, reach_row), (0, 0)))
    wide = wide.reshape(channels, (rows_lat + 2 * reach_row) * segment)
    weights = jnp.transpose(w_horiz, (2, 1, 0, 3)).reshape(col_taps * channels, row_taps * channels)
    conv = pl.pallas_call(
        horizontal_kernel,
        out_shape=jax.ShapeDtypeStruct((rows_lat, channels, cols_lon), jnp.float32),
        in_specs=[pl.BlockSpec(memory_space=pltpu.VMEM)] * 2,
        out_specs=pl.BlockSpec(memory_space=pltpu.VMEM),
        cost_estimate=pl.CostEstimate(
            flops=2 * rows_lat * segment * weights.shape[0] * weights.shape[1],
            bytes_accessed=wide.size * 2 + weights.size * 2 + rows_lat * channels * cols_lon * 4,
            transcendentals=0,
        ),
    )(wide, weights)
    return jnp.transpose(conv, (1, 0, 2))[None]


def halo_kernel(count, left_edge, right_edge, from_left, from_right, send_sems, recv_sems):
    me = lax.axis_index("lon")
    right, left = lax.rem(me + 1, count), lax.rem(me + count - 1, count)
    rest = (lax.axis_index("lat_hi"), lax.axis_index("lat_lo"))
    mesh_ids = pl.DeviceIdType.MESH
    barrier = pltpu.get_barrier_semaphore()
    for neighbour in (left, right):
        pl.semaphore_signal(barrier, inc=1, device_id=(neighbour,) + rest, device_id_type=mesh_ids)
    pl.semaphore_wait(barrier, 2)
    to_right = pltpu.make_async_remote_copy(
        src_ref=right_edge,
        dst_ref=from_left,
        send_sem=send_sems.at[0],
        recv_sem=recv_sems.at[0],
        device_id=(right,) + rest,
        device_id_type=mesh_ids,
    )
    to_left = pltpu.make_async_remote_copy(
        src_ref=left_edge,
        dst_ref=from_right,
        send_sem=send_sems.at[1],
        recv_sem=recv_sems.at[1],
        device_id=(left,) + rest,
        device_id_type=mesh_ids,
    )
    to_right.start()
    to_left.start()
    to_right.wait()
    to_left.wait()


def lon_halo(block, width):
    count = lax.axis_size("lon")
    length = block.shape[-1]
    edge_shape = block.shape[:-1] + (width,)
    flat = (block.shape[1], block.shape[2] * width)
    left_edge = block[..., :width].reshape(flat)
    right_edge = block[..., length - width :].reshape(flat)
    any_spec = pl.BlockSpec(memory_space=pl.ANY)
    from_left, from_right = pl.pallas_call(
        functools.partial(halo_kernel, count),
        out_shape=(jax.ShapeDtypeStruct(flat, block.dtype),) * 2,
        in_specs=[any_spec] * 2,
        out_specs=(any_spec,) * 2,
        scratch_shapes=[pltpu.SemaphoreType.DMA((2,)), pltpu.SemaphoreType.DMA((2,))],
        compiler_params=pltpu.CompilerParams(collective_id=0, has_side_effects=True),
    )(left_edge, right_edge)
    return from_left.reshape(edge_shape), from_right.reshape(edge_shape)


def solution(mesh):
    halves = 2
    lon_count, lat_count = mesh.devices.shape
    split = jax.sharding.Mesh(
        mesh.devices.reshape(lon_count, halves, lat_count // halves), ("lon", "lat_hi", "lat_lo")
    )
    lat = ("lat_hi", "lat_lo")
    placed = (P(lat, None, None, "lon"), P(lat, None, "lon"), P(), P(), P(), P(), P())
    return jax.shard_map(
        local, mesh=split, in_specs=placed, out_specs=P(lat, None, None, "lon"), check_vma=False
    )
```

```python
import functools

import jax
from jax.experimental import pallas as pl
from jax.experimental.pallas import tpu as pltpu
import jax.numpy as jnp
from jax import lax
from jax.sharding import PartitionSpec as P


def normalize(block, norm_gain):
    values = block.astype(jnp.float32)
    center = jnp.mean(values, axis=1, keepdims=True)
    spread = jnp.mean((values - center) ** 2, axis=1, keepdims=True)
    return ((values - center) * lax.rsqrt(spread + 1e-05) * norm_gain[None, :, None, None]).astype(
        jnp.bfloat16
    )


def vertical(taps, w_vert, b_vert):
    count_lev, channels, rows_lat, cols_lon = taps[0].shape
    groups, width_in, width_out = (w_vert.shape[1], w_vert.shape[2], w_vert.shape[3])
    summed = jnp.zeros((count_lev, groups, width_out, rows_lat, cols_lon), jnp.float32)
    for tap_index in range(len(taps)):
        grouped = taps[tap_index].reshape(count_lev, groups, width_in, rows_lat, cols_lon)
        summed = summed + jnp.einsum(
            "gio,ngiab->ngoab", w_vert[tap_index], grouped, preferred_element_type=jnp.float32
        )
    summed = summed.reshape(count_lev, channels, rows_lat, cols_lon) + b_vert[None, :, None, None]
    return jax.nn.gelu(summed).astype(jnp.bfloat16)


def local(fields, ocean_mask, norm_gain, w_vert, b_vert, w_horiz, b_horiz):
    normed = normalize(fields, norm_gain)
    reach = w_vert.shape[0] // 2
    columns = lax.all_to_all(normed, "lat_lo", split_axis=2, concat_axis=0, tiled=True)
    count_lev = columns.shape[0]
    upper = lax.axis_index("lat_hi") == 0
    send = jnp.where(upper, columns[count_lev - reach :], columns[:reach])
    recv = lax.ppermute(send, "lat_hi", [(0, 1), (1, 0)])
    zeros = jnp.zeros_like(recv)
    below = jnp.where(upper, zeros, recv)
    above = jnp.where(upper, recv, zeros)
    padded = jnp.concatenate([below, columns, above], axis=0)
    taps = [padded[tap_index : tap_index + count_lev] for tap_index in range(w_vert.shape[0])]
    mixed = lax.all_to_all(
        vertical(taps, w_vert, b_vert), "lat_lo", split_axis=0, concat_axis=2, tiled=True
    )
    masked = mixed * ocean_mask[:, None].astype(jnp.bfloat16)
    conv = horizontal(masked, w_horiz)
    ocean = ocean_mask[:, None].astype(jnp.float32)
    return (fields.astype(jnp.float32) + ocean * (conv + b_horiz[None, :, None, None])).astype(
        jnp.bfloat16
    )


def horizontal_kernel(x_ref, w_ref, o_ref):
    rows, channels, cols_lon = o_ref.shape
    taps = w_ref.shape[0] // channels
    segment = x_ref.shape[1] // (rows + taps - 1)
    chunk = 8
    weights = w_ref[...]
    for start in range(0, rows, chunk):
        window = jnp.concatenate(
            [
                x_ref[:, (start + row_tap) * segment : (start + row_tap + chunk) * segment]
                for row_tap in range(taps)
            ],
            axis=0,
        )
        partial = jnp.dot(weights, window, preferred_element_type=jnp.float32)
        total = partial[:channels]
        for col_tap in range(1, taps):
            piece = partial[col_tap * channels : (col_tap + 1) * channels]
            total = total + pltpu.roll(piece, chunk * segment - col_tap, 1)
        for row in range(chunk):
            o_ref[start + row] = total[:, row * segment : row * segment + cols_lon]


def horizontal(masked, w_horiz):
    row_taps, channels, col_taps, _ = w_horiz.shape
    reach_row, reach_col = row_taps // 2, col_taps // 2
    _, _, rows_lat, cols_lon = masked.shape
    before, after = lon_halo(masked, reach_col)
    segment = 2 * cols_lon
    gap = jnp.zeros(masked.shape[:3] + (segment - cols_lon - 2 * reach_col,), masked.dtype)
    wide = jnp.concatenate([before, masked, after, gap], axis=3)[0]
    wide = jnp.pad(wide, ((0, 0), (reach_row, reach_row), (0, 0)))
    wide = wide.reshape(channels, (rows_lat + 2 * reach_row) * segment)
    weights = jnp.transpose(w_horiz, (2, 1, 0, 3)).reshape(col_taps * channels, row_taps * channels)
    conv = pl.pallas_call(
        horizontal_kernel,
        out_shape=jax.ShapeDtypeStruct((rows_lat, channels, cols_lon), jnp.float32),
        in_specs=[pl.BlockSpec(memory_space=pltpu.VMEM)] * 2,
        out_specs=pl.BlockSpec(memory_space=pltpu.VMEM),
        cost_estimate=pl.CostEstimate(
            flops=2 * rows_lat * segment * weights.shape[0] * weights.shape[1],
            bytes_accessed=wide.size * 2 + weights.size * 2 + rows_lat * channels * cols_lon * 4,
            transcendentals=0,
        ),
    )(wide, weights)
    return jnp.transpose(conv, (1, 0, 2))[None]


def halo_kernel(count, edges, halos, send_sems, recv_sems):
    me = lax.axis_index("lon")
    right, left = lax.rem(me + 1, count), lax.rem(me + count - 1, count)
    rest = (lax.axis_index("lat_hi"), lax.axis_index("lat_lo"))
    mesh_ids = pl.DeviceIdType.MESH
    barrier = pltpu.get_barrier_semaphore()
    for neighbour in (left, right):
        pl.semaphore_signal(barrier, inc=1, device_id=(neighbour,) + rest, device_id_type=mesh_ids)
    pl.semaphore_wait(barrier, 2)
    to_right = pltpu.make_async_remote_copy(
        src_ref=edges.at[1],
        dst_ref=halos.at[0],
        send_sem=send_sems.at[0],
        recv_sem=recv_sems.at[0],
        device_id=(right,) + rest,
        device_id_type=mesh_ids,
    )
    to_left = pltpu.make_async_remote_copy(
        src_ref=edges.at[0],
        dst_ref=halos.at[1],
        send_sem=send_sems.at[1],
        recv_sem=recv_sems.at[1],
        device_id=(left,) + rest,
        device_id_type=mesh_ids,
    )
    to_right.start()
    to_left.start()
    to_right.wait()
    to_left.wait()


def lon_halo(block, width):
    count = lax.axis_size("lon")
    length = block.shape[-1]
    edges = jnp.stack([block[0, :, :, :width], block[0, :, :, length - width :]])
    edges = jnp.transpose(edges, (0, 1, 3, 2))
    any_spec = pl.BlockSpec(memory_space=pl.ANY)
    halos = pl.pallas_call(
        functools.partial(halo_kernel, count),
        out_shape=jax.ShapeDtypeStruct(edges.shape, block.dtype),
        in_specs=[any_spec],
        out_specs=any_spec,
        scratch_shapes=[pltpu.SemaphoreType.DMA((2,)), pltpu.SemaphoreType.DMA((2,))],
        compiler_params=pltpu.CompilerParams(collective_id=0, has_side_effects=True),
    )(edges)
    halos = jnp.transpose(halos, (0, 1, 3, 2))[:, None]
    return halos[0], halos[1]


def solution(mesh):
    halves = 2
    lon_count, lat_count = mesh.devices.shape
    split = jax.sharding.Mesh(
        mesh.devices.reshape(lon_count, halves, lat_count // halves), ("lon", "lat_hi", "lat_lo")
    )
    lat = ("lat_hi", "lat_lo")
    placed = (P(lat, None, None, "lon"), P(lat, None, "lon"), P(), P(), P(), P(), P())
    return jax.shard_map(
        local, mesh=split, in_specs=placed, out_specs=P(lat, None, None, "lon"), check_vma=False
    )
```

```python
import functools

import jax
from jax.experimental import pallas as pl
from jax.experimental.pallas import tpu as pltpu
import jax.numpy as jnp
from jax import lax
from jax.sharding import PartitionSpec as P


def normalize(block, norm_gain):
    values = block.astype(jnp.float32)
    center = jnp.mean(values, axis=1, keepdims=True)
    spread = jnp.mean((values - center) ** 2, axis=1, keepdims=True)
    return ((values - center) * lax.rsqrt(spread + 1e-05) * norm_gain[None, :, None, None]).astype(
        jnp.bfloat16
    )


def vertical(taps, w_vert, b_vert):
    count_lev, channels, rows_lat, cols_lon = taps[0].shape
    groups, width_in, width_out = (w_vert.shape[1], w_vert.shape[2], w_vert.shape[3])
    summed = jnp.zeros((count_lev, groups, width_out, rows_lat, cols_lon), jnp.float32)
    for tap_index in range(len(taps)):
        grouped = taps[tap_index].reshape(count_lev, groups, width_in, rows_lat, cols_lon)
        summed = summed + jnp.einsum(
            "gio,ngiab->ngoab", w_vert[tap_index], grouped, preferred_element_type=jnp.float32
        )
    summed = summed.reshape(count_lev, channels, rows_lat, cols_lon) + b_vert[None, :, None, None]
    return jax.nn.gelu(summed).astype(jnp.bfloat16)


def relay_kernel(ring, ys, quarter, send_ref, out_ref, relay, send_sems, recv_sems):
    lon, half, place = (lax.axis_index("lon"), lax.axis_index("lat_hi"), lax.axis_index("lat_lo"))
    spread = ring // 2
    z = half * spread + lon // ys
    y = lon % ys

    def device(step):
        other = (z + step + ring) % ring
        return ((other % spread) * ys + y, other // spread, place)

    ahead, behind = device(quarter), device(-quarter)
    mesh_ids = pl.DeviceIdType.MESH
    barrier = pltpu.get_barrier_semaphore()
    for neighbour in (ahead, behind):
        pl.semaphore_signal(barrier, inc=1, device_id=neighbour, device_id_type=mesh_ids)
    pl.semaphore_wait(barrier, 2)

    def copy(src, dst, index, target):
        return pltpu.make_async_remote_copy(
            src_ref=src,
            dst_ref=dst,
            send_sem=send_sems.at[index],
            recv_sem=recv_sems.at[index],
            device_id=target,
            device_id_type=mesh_ids,
        )

    first = copy(send_ref.at[0], relay.at[0], 0, ahead)
    second = copy(send_ref.at[1], relay.at[1], 1, behind)
    first.start()
    second.start()
    first.wait_recv()
    onward = copy(relay.at[0], out_ref.at[0], 2, ahead)
    onward.start()
    second.wait_recv()
    backward = copy(relay.at[1], out_ref.at[1], 3, behind)
    backward.start()
    onward.wait_recv()
    backward.wait_recv()
    first.wait_send()
    second.wait_send()
    onward.wait_send()
    backward.wait_send()


def across(send):
    ys = 4
    spread = lax.axis_size("lon") // ys
    ring = spread * lax.axis_size("lat_hi")
    any_spec = pl.BlockSpec(memory_space=pl.ANY)
    return pl.pallas_call(
        functools.partial(relay_kernel, ring, ys, ring // 4),
        out_shape=jax.ShapeDtypeStruct(send.shape, send.dtype),
        in_specs=[any_spec],
        out_specs=any_spec,
        scratch_shapes=[
            pltpu.VMEM(send.shape, send.dtype),
            pltpu.SemaphoreType.DMA((4,)),
            pltpu.SemaphoreType.DMA((4,)),
        ],
        compiler_params=pltpu.CompilerParams(collective_id=1, has_side_effects=True),
    )(send)


def local(fields, ocean_mask, norm_gain, w_vert, b_vert, w_horiz, b_horiz):
    normed = normalize(fields, norm_gain)
    reach = w_vert.shape[0] // 2
    columns = lax.all_to_all(normed, "lat_lo", split_axis=2, concat_axis=0, tiled=True)
    count_lev = columns.shape[0]
    upper = lax.axis_index("lat_hi") == 0
    send = jnp.where(upper, columns[count_lev - reach :], columns[:reach])
    recv = across(send)
    zeros = jnp.zeros_like(recv)
    below = jnp.where(upper, zeros, recv)
    above = jnp.where(upper, recv, zeros)
    padded = jnp.concatenate([below, columns, above], axis=0)
    taps = [padded[tap_index : tap_index + count_lev] for tap_index in range(w_vert.shape[0])]
    mixed = lax.all_to_all(
        vertical(taps, w_vert, b_vert), "lat_lo", split_axis=0, concat_axis=2, tiled=True
    )
    masked = mixed * ocean_mask[:, None].astype(jnp.bfloat16)
    conv = horizontal(masked, w_horiz)
    ocean = ocean_mask[:, None].astype(jnp.float32)
    return (fields.astype(jnp.float32) + ocean * (conv + b_horiz[None, :, None, None])).astype(
        jnp.bfloat16
    )


def horizontal_kernel(x_ref, w_ref, o_ref):
    rows, channels, cols_lon = o_ref.shape
    taps = w_ref.shape[0] // channels
    segment = x_ref.shape[1] // (rows + taps - 1)
    chunk = 8
    weights = w_ref[...]
    for start in range(0, rows, chunk):
        window = jnp.concatenate(
            [
                x_ref[:, (start + row_tap) * segment : (start + row_tap + chunk) * segment]
                for row_tap in range(taps)
            ],
            axis=0,
        )
        partial = jnp.dot(weights, window, preferred_element_type=jnp.float32)
        total = partial[:channels]
        for col_tap in range(1, taps):
            piece = partial[col_tap * channels : (col_tap + 1) * channels]
            total = total + pltpu.roll(piece, chunk * segment - col_tap, 1)
        for row in range(chunk):
            o_ref[start + row] = total[:, row * segment : row * segment + cols_lon]


def horizontal(masked, w_horiz):
    row_taps, channels, col_taps, _ = w_horiz.shape
    reach_row, reach_col = row_taps // 2, col_taps // 2
    _, _, rows_lat, cols_lon = masked.shape
    before, after = lon_halo(masked, reach_col)
    segment = 2 * cols_lon
    gap = jnp.zeros(masked.shape[:3] + (segment - cols_lon - 2 * reach_col,), masked.dtype)
    wide = jnp.concatenate([before, masked, after, gap], axis=3)[0]
    wide = jnp.pad(wide, ((0, 0), (reach_row, reach_row), (0, 0)))
    wide = wide.reshape(channels, (rows_lat + 2 * reach_row) * segment)
    weights = jnp.transpose(w_horiz, (2, 1, 0, 3)).reshape(col_taps * channels, row_taps * channels)
    conv = pl.pallas_call(
        horizontal_kernel,
        out_shape=jax.ShapeDtypeStruct((rows_lat, channels, cols_lon), jnp.float32),
        in_specs=[pl.BlockSpec(memory_space=pltpu.VMEM)] * 2,
        out_specs=pl.BlockSpec(memory_space=pltpu.VMEM),
        cost_estimate=pl.CostEstimate(
            flops=2 * rows_lat * segment * weights.shape[0] * weights.shape[1],
            bytes_accessed=wide.size * 2 + weights.size * 2 + rows_lat * channels * cols_lon * 4,
            transcendentals=0,
        ),
    )(wide, weights)
    return jnp.transpose(conv, (1, 0, 2))[None]


def halo_kernel(count, left_edge, right_edge, from_left, from_right, send_sems, recv_sems):
    me = lax.axis_index("lon")
    right, left = lax.rem(me + 1, count), lax.rem(me + count - 1, count)
    rest = (lax.axis_index("lat_hi"), lax.axis_index("lat_lo"))
    mesh_ids = pl.DeviceIdType.MESH
    barrier = pltpu.get_barrier_semaphore()
    for neighbour in (left, right):
        pl.semaphore_signal(barrier, inc=1, device_id=(neighbour,) + rest, device_id_type=mesh_ids)
    pl.semaphore_wait(barrier, 2)
    to_right = pltpu.make_async_remote_copy(
        src_ref=right_edge,
        dst_ref=from_left,
        send_sem=send_sems.at[0],
        recv_sem=recv_sems.at[0],
        device_id=(right,) + rest,
        device_id_type=mesh_ids,
    )
    to_left = pltpu.make_async_remote_copy(
        src_ref=left_edge,
        dst_ref=from_right,
        send_sem=send_sems.at[1],
        recv_sem=recv_sems.at[1],
        device_id=(left,) + rest,
        device_id_type=mesh_ids,
    )
    to_right.start()
    to_left.start()
    to_right.wait()
    to_left.wait()


def lon_halo(block, width):
    count = lax.axis_size("lon")
    length = block.shape[-1]
    edge_shape = block.shape[:-1] + (width,)
    flat = (block.shape[1], block.shape[2] * width)
    left_edge = block[..., :width].reshape(flat)
    right_edge = block[..., length - width :].reshape(flat)
    any_spec = pl.BlockSpec(memory_space=pl.ANY)
    from_left, from_right = pl.pallas_call(
        functools.partial(halo_kernel, count),
        out_shape=(jax.ShapeDtypeStruct(flat, block.dtype),) * 2,
        in_specs=[any_spec] * 2,
        out_specs=(any_spec,) * 2,
        scratch_shapes=[pltpu.SemaphoreType.DMA((2,)), pltpu.SemaphoreType.DMA((2,))],
        compiler_params=pltpu.CompilerParams(collective_id=0, has_side_effects=True),
    )(left_edge, right_edge)
    return from_left.reshape(edge_shape), from_right.reshape(edge_shape)


def solution(mesh):
    halves = 2
    lon_count, lat_count = mesh.devices.shape
    split = jax.sharding.Mesh(
        mesh.devices.reshape(lon_count, halves, lat_count // halves), ("lon", "lat_hi", "lat_lo")
    )
    lat = ("lat_hi", "lat_lo")
    placed = (P(lat, None, None, "lon"), P(lat, None, "lon"), P(), P(), P(), P(), P())
    return jax.shard_map(
        local, mesh=split, in_specs=placed, out_specs=P(lat, None, None, "lon"), check_vma=False
    )
```

```python
import functools

import jax
from jax.experimental import pallas as pl
from jax.experimental.pallas import tpu as pltpu
import jax.numpy as jnp
from jax import lax
from jax.sharding import PartitionSpec as P


def normalize(block, norm_gain):
    values = block.astype(jnp.float32)
    center = jnp.mean(values, axis=1, keepdims=True)
    spread = jnp.mean((values - center) ** 2, axis=1, keepdims=True)
    return ((values - center) * lax.rsqrt(spread + 1e-05) * norm_gain[None, :, None, None]).astype(
        jnp.bfloat16
    )


def vertical(taps, w_vert, b_vert):
    count_lev, channels, rows_lat, cols_lon = taps[0].shape
    groups, width_in, width_out = (w_vert.shape[1], w_vert.shape[2], w_vert.shape[3])
    summed = jnp.zeros((count_lev, groups, width_out, rows_lat, cols_lon), jnp.float32)
    for tap_index in range(len(taps)):
        grouped = taps[tap_index].reshape(count_lev, groups, width_in, rows_lat, cols_lon)
        summed = summed + jnp.einsum(
            "gio,ngiab->ngoab", w_vert[tap_index], grouped, preferred_element_type=jnp.float32
        )
    summed = summed.reshape(count_lev, channels, rows_lat, cols_lon) + b_vert[None, :, None, None]
    return jax.nn.gelu(summed).astype(jnp.bfloat16)


def local(fields, ocean_mask, norm_gain, w_vert, b_vert, w_horiz, b_horiz):
    normed = normalize(fields, norm_gain)
    reach = w_vert.shape[0] // 2
    columns = lax.all_to_all(normed, "lat_lo", split_axis=2, concat_axis=0, tiled=True)
    count_lev = columns.shape[0]
    upper = lax.axis_index("lat_hi") == 0
    send = jnp.where(upper, columns[count_lev - reach :], columns[:reach])
    recv = lax.ppermute(send, "lat_hi", [(0, 1), (1, 0)])
    zeros = jnp.zeros_like(recv)
    below = jnp.where(upper, zeros, recv)
    above = jnp.where(upper, recv, zeros)
    padded = jnp.concatenate([below, columns, above], axis=0)
    taps = [padded[tap_index : tap_index + count_lev] for tap_index in range(w_vert.shape[0])]
    mixed = lax.all_to_all(
        vertical(taps, w_vert, b_vert), "lat_lo", split_axis=0, concat_axis=2, tiled=True
    )
    masked = mixed * ocean_mask[:, None].astype(jnp.bfloat16)
    conv = horizontal(masked, w_horiz)
    ocean = ocean_mask[:, None].astype(jnp.float32)
    return (fields.astype(jnp.float32) + ocean * (conv + b_horiz[None, :, None, None])).astype(
        jnp.bfloat16
    )


def horizontal_kernel(x_ref, w_ref, o_ref):
    channels, rows, cols_lon = o_ref.shape
    taps = w_ref.shape[0] // channels
    segment = x_ref.shape[1] // (rows + taps - 1)
    chunk = 8
    weights = w_ref[...]
    for start in range(0, rows, chunk):
        window = jnp.concatenate(
            [
                x_ref[:, (start + row_tap) * segment : (start + row_tap + chunk) * segment]
                for row_tap in range(taps)
            ],
            axis=0,
        )
        partial = jnp.dot(weights, window, preferred_element_type=jnp.float32)
        total = partial[:channels]
        for col_tap in range(1, taps):
            piece = partial[col_tap * channels : (col_tap + 1) * channels]
            total = total + pltpu.roll(piece, chunk * segment - col_tap, 1)
        for row in range(chunk):
            o_ref[:, start + row, :] = total[:, row * segment : row * segment + cols_lon]


def horizontal(masked, w_horiz):
    row_taps, channels, col_taps, _ = w_horiz.shape
    reach_row, reach_col = row_taps // 2, col_taps // 2
    _, _, rows_lat, cols_lon = masked.shape
    before, after = lon_halo(masked, reach_col)
    segment = 2 * cols_lon
    gap = jnp.zeros(masked.shape[:3] + (segment - cols_lon - 2 * reach_col,), masked.dtype)
    wide = jnp.concatenate([before, masked, after, gap], axis=3)[0]
    wide = jnp.pad(wide, ((0, 0), (reach_row, reach_row), (0, 0)))
    wide = wide.reshape(channels, (rows_lat + 2 * reach_row) * segment)
    weights = jnp.transpose(w_horiz, (2, 1, 0, 3)).reshape(col_taps * channels, row_taps * channels)
    conv = pl.pallas_call(
        horizontal_kernel,
        out_shape=jax.ShapeDtypeStruct((channels, rows_lat, cols_lon), jnp.float32),
        in_specs=[pl.BlockSpec(memory_space=pltpu.VMEM)] * 2,
        out_specs=pl.BlockSpec(memory_space=pltpu.VMEM),
        cost_estimate=pl.CostEstimate(
            flops=2 * rows_lat * segment * weights.shape[0] * weights.shape[1],
            bytes_accessed=wide.size * 2 + weights.size * 2 + rows_lat * channels * cols_lon * 4,
            transcendentals=0,
        ),
    )(wide, weights)
    return conv[None]


def halo_kernel(count, left_edge, right_edge, from_left, from_right, send_sems, recv_sems):
    me = lax.axis_index("lon")
    right, left = lax.rem(me + 1, count), lax.rem(me + count - 1, count)
    rest = (lax.axis_index("lat_hi"), lax.axis_index("lat_lo"))
    mesh_ids = pl.DeviceIdType.MESH
    barrier = pltpu.get_barrier_semaphore()
    for neighbour in (left, right):
        pl.semaphore_signal(barrier, inc=1, device_id=(neighbour,) + rest, device_id_type=mesh_ids)
    pl.semaphore_wait(barrier, 2)
    to_right = pltpu.make_async_remote_copy(
        src_ref=right_edge,
        dst_ref=from_left,
        send_sem=send_sems.at[0],
        recv_sem=recv_sems.at[0],
        device_id=(right,) + rest,
        device_id_type=mesh_ids,
    )
    to_left = pltpu.make_async_remote_copy(
        src_ref=left_edge,
        dst_ref=from_right,
        send_sem=send_sems.at[1],
        recv_sem=recv_sems.at[1],
        device_id=(left,) + rest,
        device_id_type=mesh_ids,
    )
    to_right.start()
    to_left.start()
    to_right.wait()
    to_left.wait()


def lon_halo(block, width):
    count = lax.axis_size("lon")
    length = block.shape[-1]
    edge_shape = block.shape[:-1] + (width,)
    flat = (block.shape[1], block.shape[2] * width)
    left_edge = block[..., :width].reshape(flat)
    right_edge = block[..., length - width :].reshape(flat)
    any_spec = pl.BlockSpec(memory_space=pl.ANY)
    from_left, from_right = pl.pallas_call(
        functools.partial(halo_kernel, count),
        out_shape=(jax.ShapeDtypeStruct(flat, block.dtype),) * 2,
        in_specs=[any_spec] * 2,
        out_specs=(any_spec,) * 2,
        scratch_shapes=[pltpu.SemaphoreType.DMA((2,)), pltpu.SemaphoreType.DMA((2,))],
        compiler_params=pltpu.CompilerParams(collective_id=0, has_side_effects=True),
    )(left_edge, right_edge)
    return from_left.reshape(edge_shape), from_right.reshape(edge_shape)


def solution(mesh):
    halves = 2
    lon_count, lat_count = mesh.devices.shape
    split = jax.sharding.Mesh(
        mesh.devices.reshape(lon_count, halves, lat_count // halves), ("lon", "lat_hi", "lat_lo")
    )
    lat = ("lat_hi", "lat_lo")
    placed = (P(lat, None, None, "lon"), P(lat, None, "lon"), P(), P(), P(), P(), P())
    return jax.shard_map(
        local, mesh=split, in_specs=placed, out_specs=P(lat, None, None, "lon"), check_vma=False
    )
```

```python
import functools

import jax
from jax.experimental import pallas as pl
from jax.experimental.pallas import tpu as pltpu
import jax.numpy as jnp
from jax import lax
from jax.sharding import PartitionSpec as P


def normalize_kernel(x_ref, g_ref, o_ref):
    rows, channels, _ = o_ref.shape
    gain = g_ref[...]
    for row in range(rows):
        values = x_ref[0, :, row, :].astype(jnp.float32)
        center = jnp.sum(values, axis=0, keepdims=True) / channels
        offset = values - center
        spread = jnp.sum(offset * offset, axis=0, keepdims=True) / channels
        o_ref[row] = (offset * lax.rsqrt(spread + 1e-05) * gain).astype(o_ref.dtype)


def normalize(block, norm_gain):
    _, channels, rows_lat, cols_lon = block.shape
    vmem = pl.BlockSpec(memory_space=pltpu.VMEM)
    normed = pl.pallas_call(
        normalize_kernel,
        out_shape=jax.ShapeDtypeStruct((rows_lat, channels, cols_lon), jnp.bfloat16),
        in_specs=[vmem, vmem],
        out_specs=vmem,
    )(block, norm_gain[:, None])
    return jnp.transpose(normed, (1, 0, 2))[None]


def vertical(taps, w_vert, b_vert):
    count_lev, channels, rows_lat, cols_lon = taps[0].shape
    groups, width_in, width_out = (w_vert.shape[1], w_vert.shape[2], w_vert.shape[3])
    summed = jnp.zeros((count_lev, groups, width_out, rows_lat, cols_lon), jnp.float32)
    for tap_index in range(len(taps)):
        grouped = taps[tap_index].reshape(count_lev, groups, width_in, rows_lat, cols_lon)
        summed = summed + jnp.einsum(
            "gio,ngiab->ngoab", w_vert[tap_index], grouped, preferred_element_type=jnp.float32
        )
    summed = summed.reshape(count_lev, channels, rows_lat, cols_lon) + b_vert[None, :, None, None]
    return jax.nn.gelu(summed).astype(jnp.bfloat16)


def local(fields, ocean_mask, norm_gain, w_vert, b_vert, w_horiz, b_horiz):
    normed = normalize(fields, norm_gain)
    reach = w_vert.shape[0] // 2
    columns = lax.all_to_all(normed, "lat_lo", split_axis=2, concat_axis=0, tiled=True)
    count_lev = columns.shape[0]
    upper = lax.axis_index("lat_hi") == 0
    send = jnp.where(upper, columns[count_lev - reach :], columns[:reach])
    recv = lax.ppermute(send, "lat_hi", [(0, 1), (1, 0)])
    zeros = jnp.zeros_like(recv)
    below = jnp.where(upper, zeros, recv)
    above = jnp.where(upper, recv, zeros)
    padded = jnp.concatenate([below, columns, above], axis=0)
    taps = [padded[tap_index : tap_index + count_lev] for tap_index in range(w_vert.shape[0])]
    mixed = lax.all_to_all(
        vertical(taps, w_vert, b_vert), "lat_lo", split_axis=0, concat_axis=2, tiled=True
    )
    masked = mixed * ocean_mask[:, None].astype(jnp.bfloat16)
    conv = horizontal(masked, w_horiz)
    ocean = ocean_mask[:, None].astype(jnp.float32)
    return (fields.astype(jnp.float32) + ocean * (conv + b_horiz[None, :, None, None])).astype(
        jnp.bfloat16
    )


def horizontal_kernel(x_ref, w_ref, o_ref):
    rows, channels, cols_lon = o_ref.shape
    taps = w_ref.shape[0] // channels
    segment = x_ref.shape[1] // (rows + taps - 1)
    chunk = 8
    weights = w_ref[...]
    for start in range(0, rows, chunk):
        window = jnp.concatenate(
            [
                x_ref[:, (start + row_tap) * segment : (start + row_tap + chunk) * segment]
                for row_tap in range(taps)
            ],
            axis=0,
        )
        partial = jnp.dot(weights, window, preferred_element_type=jnp.float32)
        total = partial[:channels]
        for col_tap in range(1, taps):
            piece = partial[col_tap * channels : (col_tap + 1) * channels]
            total = total + pltpu.roll(piece, chunk * segment - col_tap, 1)
        for row in range(chunk):
            o_ref[start + row] = total[:, row * segment : row * segment + cols_lon]


def horizontal(masked, w_horiz):
    row_taps, channels, col_taps, _ = w_horiz.shape
    reach_row, reach_col = row_taps // 2, col_taps // 2
    _, _, rows_lat, cols_lon = masked.shape
    before, after = lon_halo(masked, reach_col)
    segment = 2 * cols_lon
    gap = jnp.zeros(masked.shape[:3] + (segment - cols_lon - 2 * reach_col,), masked.dtype)
    wide = jnp.concatenate([before, masked, after, gap], axis=3)[0]
    wide = jnp.pad(wide, ((0, 0), (reach_row, reach_row), (0, 0)))
    wide = wide.reshape(channels, (rows_lat + 2 * reach_row) * segment)
    weights = jnp.transpose(w_horiz, (2, 1, 0, 3)).reshape(col_taps * channels, row_taps * channels)
    conv = pl.pallas_call(
        horizontal_kernel,
        out_shape=jax.ShapeDtypeStruct((rows_lat, channels, cols_lon), jnp.float32),
        in_specs=[pl.BlockSpec(memory_space=pltpu.VMEM)] * 2,
        out_specs=pl.BlockSpec(memory_space=pltpu.VMEM),
        cost_estimate=pl.CostEstimate(
            flops=2 * rows_lat * segment * weights.shape[0] * weights.shape[1],
            bytes_accessed=wide.size * 2 + weights.size * 2 + rows_lat * channels * cols_lon * 4,
            transcendentals=0,
        ),
    )(wide, weights)
    return jnp.transpose(conv, (1, 0, 2))[None]


def halo_kernel(count, left_edge, right_edge, from_left, from_right, send_sems, recv_sems):
    me = lax.axis_index("lon")
    right, left = lax.rem(me + 1, count), lax.rem(me + count - 1, count)
    rest = (lax.axis_index("lat_hi"), lax.axis_index("lat_lo"))
    mesh_ids = pl.DeviceIdType.MESH
    barrier = pltpu.get_barrier_semaphore()
    for neighbour in (left, right):
        pl.semaphore_signal(barrier, inc=1, device_id=(neighbour,) + rest, device_id_type=mesh_ids)
    pl.semaphore_wait(barrier, 2)
    to_right = pltpu.make_async_remote_copy(
        src_ref=right_edge,
        dst_ref=from_left,
        send_sem=send_sems.at[0],
        recv_sem=recv_sems.at[0],
        device_id=(right,) + rest,
        device_id_type=mesh_ids,
    )
    to_left = pltpu.make_async_remote_copy(
        src_ref=left_edge,
        dst_ref=from_right,
        send_sem=send_sems.at[1],
        recv_sem=recv_sems.at[1],
        device_id=(left,) + rest,
        device_id_type=mesh_ids,
    )
    to_right.start()
    to_left.start()
    to_right.wait()
    to_left.wait()


def lon_halo(block, width):
    count = lax.axis_size("lon")
    length = block.shape[-1]
    edge_shape = block.shape[:-1] + (width,)
    flat = (block.shape[1], block.shape[2] * width)
    left_edge = block[..., :width].reshape(flat)
    right_edge = block[..., length - width :].reshape(flat)
    any_spec = pl.BlockSpec(memory_space=pl.ANY)
    from_left, from_right = pl.pallas_call(
        functools.partial(halo_kernel, count),
        out_shape=(jax.ShapeDtypeStruct(flat, block.dtype),) * 2,
        in_specs=[any_spec] * 2,
        out_specs=(any_spec,) * 2,
        scratch_shapes=[pltpu.SemaphoreType.DMA((2,)), pltpu.SemaphoreType.DMA((2,))],
        compiler_params=pltpu.CompilerParams(collective_id=0, has_side_effects=True),
    )(left_edge, right_edge)
    return from_left.reshape(edge_shape), from_right.reshape(edge_shape)


def solution(mesh):
    halves = 2
    lon_count, lat_count = mesh.devices.shape
    split = jax.sharding.Mesh(
        mesh.devices.reshape(lon_count, halves, lat_count // halves), ("lon", "lat_hi", "lat_lo")
    )
    lat = ("lat_hi", "lat_lo")
    placed = (P(lat, None, None, "lon"), P(lat, None, "lon"), P(), P(), P(), P(), P())
    return jax.shard_map(
        local, mesh=split, in_specs=placed, out_specs=P(lat, None, None, "lon"), check_vma=False
    )
```

```python
import functools

import jax
from jax.experimental import pallas as pl
from jax.experimental.pallas import tpu as pltpu
import jax.numpy as jnp
from jax import lax
from jax.sharding import PartitionSpec as P


def normalize_kernel(x_ref, g_ref, o_ref):
    rows, channels, cols_lon = o_ref.shape
    channel = lax.broadcasted_iota(jnp.int32, (channels, cols_lon), 0)
    gain = jnp.zeros((channels, cols_lon), jnp.float32)
    for index in range(channels):
        gain = jnp.where(channel == index, g_ref[index], gain)
    for row in range(rows):
        values = x_ref[0, :, row, :].astype(jnp.float32)
        center = jnp.sum(values, axis=0, keepdims=True) / channels
        offset = values - center
        spread = jnp.sum(offset * offset, axis=0, keepdims=True) / channels
        o_ref[row] = (offset * lax.rsqrt(spread + 1e-05) * gain).astype(o_ref.dtype)


def normalize(block, norm_gain):
    _, channels, rows_lat, cols_lon = block.shape
    vmem = pl.BlockSpec(memory_space=pltpu.VMEM)
    normed = pl.pallas_call(
        normalize_kernel,
        out_shape=jax.ShapeDtypeStruct((rows_lat, channels, cols_lon), jnp.bfloat16),
        in_specs=[vmem, pl.BlockSpec(memory_space=pltpu.SMEM)],
        out_specs=vmem,
    )(block, norm_gain)
    return jnp.transpose(normed, (1, 0, 2))[None]


def vertical(taps, w_vert, b_vert):
    count_lev, channels, rows_lat, cols_lon = taps[0].shape
    groups, width_in, width_out = (w_vert.shape[1], w_vert.shape[2], w_vert.shape[3])
    summed = jnp.zeros((count_lev, groups, width_out, rows_lat, cols_lon), jnp.float32)
    for tap_index in range(len(taps)):
        grouped = taps[tap_index].reshape(count_lev, groups, width_in, rows_lat, cols_lon)
        summed = summed + jnp.einsum(
            "gio,ngiab->ngoab", w_vert[tap_index], grouped, preferred_element_type=jnp.float32
        )
    summed = summed.reshape(count_lev, channels, rows_lat, cols_lon) + b_vert[None, :, None, None]
    return jax.nn.gelu(summed).astype(jnp.bfloat16)


def local(fields, ocean_mask, norm_gain, w_vert, b_vert, w_horiz, b_horiz):
    normed = normalize(fields, norm_gain)
    reach = w_vert.shape[0] // 2
    columns = lax.all_to_all(normed, "lat_lo", split_axis=2, concat_axis=0, tiled=True)
    count_lev = columns.shape[0]
    upper = lax.axis_index("lat_hi") == 0
    send = jnp.where(upper, columns[count_lev - reach :], columns[:reach])
    recv = lax.ppermute(send, "lat_hi", [(0, 1), (1, 0)])
    zeros = jnp.zeros_like(recv)
    below = jnp.where(upper, zeros, recv)
    above = jnp.where(upper, recv, zeros)
    padded = jnp.concatenate([below, columns, above], axis=0)
    taps = [padded[tap_index : tap_index + count_lev] for tap_index in range(w_vert.shape[0])]
    mixed = lax.all_to_all(
        vertical(taps, w_vert, b_vert), "lat_lo", split_axis=0, concat_axis=2, tiled=True
    )
    masked = mixed * ocean_mask[:, None].astype(jnp.bfloat16)
    conv = horizontal(masked, w_horiz)
    ocean = ocean_mask[:, None].astype(jnp.float32)
    return (fields.astype(jnp.float32) + ocean * (conv + b_horiz[None, :, None, None])).astype(
        jnp.bfloat16
    )


def horizontal_kernel(x_ref, w_ref, o_ref):
    rows, channels, cols_lon = o_ref.shape
    taps = w_ref.shape[0] // channels
    segment = x_ref.shape[1] // (rows + taps - 1)
    chunk = 8
    weights = w_ref[...]
    for start in range(0, rows, chunk):
        window = jnp.concatenate(
            [
                x_ref[:, (start + row_tap) * segment : (start + row_tap + chunk) * segment]
                for row_tap in range(taps)
            ],
            axis=0,
        )
        partial = jnp.dot(weights, window, preferred_element_type=jnp.float32)
        total = partial[:channels]
        for col_tap in range(1, taps):
            piece = partial[col_tap * channels : (col_tap + 1) * channels]
            total = total + pltpu.roll(piece, chunk * segment - col_tap, 1)
        for row in range(chunk):
            o_ref[start + row] = total[:, row * segment : row * segment + cols_lon]


def horizontal(masked, w_horiz):
    row_taps, channels, col_taps, _ = w_horiz.shape
    reach_row, reach_col = row_taps // 2, col_taps // 2
    _, _, rows_lat, cols_lon = masked.shape
    before, after = lon_halo(masked, reach_col)
    segment = 2 * cols_lon
    gap = jnp.zeros(masked.shape[:3] + (segment - cols_lon - 2 * reach_col,), masked.dtype)
    wide = jnp.concatenate([before, masked, after, gap], axis=3)[0]
    wide = jnp.pad(wide, ((0, 0), (reach_row, reach_row), (0, 0)))
    wide = wide.reshape(channels, (rows_lat + 2 * reach_row) * segment)
    weights = jnp.transpose(w_horiz, (2, 1, 0, 3)).reshape(col_taps * channels, row_taps * channels)
    conv = pl.pallas_call(
        horizontal_kernel,
        out_shape=jax.ShapeDtypeStruct((rows_lat, channels, cols_lon), jnp.float32),
        in_specs=[pl.BlockSpec(memory_space=pltpu.VMEM)] * 2,
        out_specs=pl.BlockSpec(memory_space=pltpu.VMEM),
        cost_estimate=pl.CostEstimate(
            flops=2 * rows_lat * segment * weights.shape[0] * weights.shape[1],
            bytes_accessed=wide.size * 2 + weights.size * 2 + rows_lat * channels * cols_lon * 4,
            transcendentals=0,
        ),
    )(wide, weights)
    return jnp.transpose(conv, (1, 0, 2))[None]


def halo_kernel(count, left_edge, right_edge, from_left, from_right, send_sems, recv_sems):
    me = lax.axis_index("lon")
    right, left = lax.rem(me + 1, count), lax.rem(me + count - 1, count)
    rest = (lax.axis_index("lat_hi"), lax.axis_index("lat_lo"))
    mesh_ids = pl.DeviceIdType.MESH
    barrier = pltpu.get_barrier_semaphore()
    for neighbour in (left, right):
        pl.semaphore_signal(barrier, inc=1, device_id=(neighbour,) + rest, device_id_type=mesh_ids)
    pl.semaphore_wait(barrier, 2)
    to_right = pltpu.make_async_remote_copy(
        src_ref=right_edge,
        dst_ref=from_left,
        send_sem=send_sems.at[0],
        recv_sem=recv_sems.at[0],
        device_id=(right,) + rest,
        device_id_type=mesh_ids,
    )
    to_left = pltpu.make_async_remote_copy(
        src_ref=left_edge,
        dst_ref=from_right,
        send_sem=send_sems.at[1],
        recv_sem=recv_sems.at[1],
        device_id=(left,) + rest,
        device_id_type=mesh_ids,
    )
    to_right.start()
    to_left.start()
    to_right.wait()
    to_left.wait()


def lon_halo(block, width):
    count = lax.axis_size("lon")
    length = block.shape[-1]
    edge_shape = block.shape[:-1] + (width,)
    flat = (block.shape[1], block.shape[2] * width)
    left_edge = block[..., :width].reshape(flat)
    right_edge = block[..., length - width :].reshape(flat)
    any_spec = pl.BlockSpec(memory_space=pl.ANY)
    from_left, from_right = pl.pallas_call(
        functools.partial(halo_kernel, count),
        out_shape=(jax.ShapeDtypeStruct(flat, block.dtype),) * 2,
        in_specs=[any_spec] * 2,
        out_specs=(any_spec,) * 2,
        scratch_shapes=[pltpu.SemaphoreType.DMA((2,)), pltpu.SemaphoreType.DMA((2,))],
        compiler_params=pltpu.CompilerParams(collective_id=0, has_side_effects=True),
    )(left_edge, right_edge)
    return from_left.reshape(edge_shape), from_right.reshape(edge_shape)


def solution(mesh):
    halves = 2
    lon_count, lat_count = mesh.devices.shape
    split = jax.sharding.Mesh(
        mesh.devices.reshape(lon_count, halves, lat_count // halves), ("lon", "lat_hi", "lat_lo")
    )
    lat = ("lat_hi", "lat_lo")
    placed = (P(lat, None, None, "lon"), P(lat, None, "lon"), P(), P(), P(), P(), P())
    return jax.shard_map(
        local, mesh=split, in_specs=placed, out_specs=P(lat, None, None, "lon"), check_vma=False
    )
```

```python
import functools

import jax
from jax.experimental import pallas as pl
from jax.experimental.pallas import tpu as pltpu
import jax.numpy as jnp
from jax import lax
from jax.sharding import PartitionSpec as P


def normalize_kernel(x_ref, g_ref, o_ref):
    rows, channels, cols_lon = o_ref.shape
    channel = lax.broadcasted_iota(jnp.int32, (channels, cols_lon), 0)
    gain = jnp.zeros((channels, cols_lon), jnp.float32)
    for index in range(channels):
        gain = jnp.where(channel == index, g_ref[index], gain)
    for row in range(rows):
        values = x_ref[0, :, row, :].astype(jnp.float32)
        center = jnp.sum(values, axis=0, keepdims=True) / channels
        offset = values - center
        spread = jnp.sum(offset * offset, axis=0, keepdims=True) / channels
        o_ref[row] = (offset * lax.rsqrt(spread + 1e-05) * gain).astype(o_ref.dtype)


def normalize(block, norm_gain):
    _, channels, rows_lat, cols_lon = block.shape
    vmem = pl.BlockSpec(memory_space=pltpu.VMEM)
    normed = pl.pallas_call(
        normalize_kernel,
        out_shape=jax.ShapeDtypeStruct((rows_lat, channels, cols_lon), jnp.bfloat16),
        in_specs=[vmem, pl.BlockSpec(memory_space=pltpu.SMEM)],
        out_specs=vmem,
    )(block, norm_gain)
    return jnp.transpose(normed, (1, 0, 2))[None]


def vertical(taps, w_vert, b_vert):
    count_lev, channels, rows_lat, cols_lon = taps[0].shape
    groups, width_in, width_out = (w_vert.shape[1], w_vert.shape[2], w_vert.shape[3])
    summed = jnp.zeros((count_lev, groups, width_out, rows_lat, cols_lon), jnp.float32)
    for tap_index in range(len(taps)):
        grouped = taps[tap_index].reshape(count_lev, groups, width_in, rows_lat, cols_lon)
        summed = summed + jnp.einsum(
            "gio,ngiab->ngoab", w_vert[tap_index], grouped, preferred_element_type=jnp.float32
        )
    summed = summed.reshape(count_lev, channels, rows_lat, cols_lon) + b_vert[None, :, None, None]
    return jax.nn.gelu(summed).astype(jnp.bfloat16)


def local(fields, ocean_mask, norm_gain, w_vert, b_vert, w_horiz, b_horiz):
    normed = normalize(fields, norm_gain)
    reach = w_vert.shape[0] // 2
    columns = lax.all_to_all(normed, "lat_lo", split_axis=2, concat_axis=0, tiled=True)
    count_lev = columns.shape[0]
    upper = lax.axis_index("lat_hi") == 0
    send = jnp.where(upper, columns[count_lev - reach :], columns[:reach])
    recv = lax.ppermute(send, "lat_hi", [(0, 1), (1, 0)])
    zeros = jnp.zeros_like(recv)
    below = jnp.where(upper, zeros, recv)
    above = jnp.where(upper, recv, zeros)
    padded = jnp.concatenate([below, columns, above], axis=0)
    taps = [padded[tap_index : tap_index + count_lev] for tap_index in range(w_vert.shape[0])]
    mixed = lax.all_to_all(
        vertical(taps, w_vert, b_vert), "lat_lo", split_axis=0, concat_axis=2, tiled=True
    )
    masked = mixed * ocean_mask[:, None].astype(jnp.bfloat16)
    conv = horizontal(masked, w_horiz)
    ocean = ocean_mask[:, None].astype(jnp.float32)
    return (fields.astype(jnp.float32) + ocean * (conv + b_horiz[None, :, None, None])).astype(
        jnp.bfloat16
    )


def horizontal_kernel(
    count, x_ref, w_ref, o_ref, wide, edges, from_left, from_right, send_sems, recv_sems
):
    me = lax.axis_index("lon")
    right, left = lax.rem(me + 1, count), lax.rem(me + count - 1, count)
    rest = (lax.axis_index("lat_hi"), lax.axis_index("lat_lo"))
    mesh_ids = pl.DeviceIdType.MESH
    barrier = pltpu.get_barrier_semaphore()
    for neighbour in (left, right):
        pl.semaphore_signal(barrier, inc=1, device_id=(neighbour,) + rest, device_id_type=mesh_ids)

    rows, channels, cols_lon = o_ref.shape
    taps = w_ref.shape[0] // channels
    reach = taps // 2
    segment = 2 * cols_lon
    lane = lax.broadcasted_iota(jnp.int32, (channels, cols_lon), 1)
    packed = jnp.zeros((channels, cols_lon), x_ref.dtype)
    for row in range(rows):
        line = x_ref[row]
        start = 2 * reach * row
        packed = jnp.where(
            jnp.logical_and(lane >= start, lane < start + reach),
            pltpu.roll(line, start, 1),
            packed,
        )
        packed = jnp.where(
            jnp.logical_and(lane >= start + reach, lane < start + 2 * reach),
            pltpu.roll(line, (start + 2 * reach) % cols_lon, 1),
            packed,
        )
    edges[...] = packed

    pl.semaphore_wait(barrier, 2)
    to_right = pltpu.make_async_remote_copy(
        src_ref=edges,
        dst_ref=from_left,
        send_sem=send_sems.at[0],
        recv_sem=recv_sems.at[0],
        device_id=(right,) + rest,
        device_id_type=mesh_ids,
    )
    to_left = pltpu.make_async_remote_copy(
        src_ref=edges,
        dst_ref=from_right,
        send_sem=send_sems.at[1],
        recv_sem=recv_sems.at[1],
        device_id=(left,) + rest,
        device_id_type=mesh_ids,
    )
    to_right.start()
    to_left.start()
    to_right.wait()
    to_left.wait()

    left_halo, right_halo = from_left[...], from_right[...]
    blank = jnp.zeros((channels, cols_lon), x_ref.dtype)
    for padded_row in range(rows + 2 * reach):
        row = padded_row - reach
        base = padded_row * segment
        if row < 0 or row >= rows:
            wide[:, base : base + cols_lon] = blank
            wide[:, base + cols_lon : base + segment] = blank
            continue
        start = 2 * reach * row
        shifted = pltpu.roll(x_ref[row], reach, 1)
        wide[:, base : base + cols_lon] = jnp.where(
            lane < reach, pltpu.roll(left_halo, (cols_lon - start - reach) % cols_lon, 1), shifted
        )
        tail = pltpu.roll(right_halo, (reach - start) % cols_lon, 1)
        wide[:, base + cols_lon : base + segment] = jnp.where(
            lane < reach, shifted, jnp.where(lane < 2 * reach, tail, blank)
        )

    chunk = 8
    weights = w_ref[...]
    for start in range(0, rows, chunk):
        window = jnp.concatenate(
            [
                wide[:, (start + row_tap) * segment : (start + row_tap + chunk) * segment]
                for row_tap in range(taps)
            ],
            axis=0,
        )
        partial = jnp.dot(weights, window, preferred_element_type=jnp.float32)
        total = partial[:channels]
        for col_tap in range(1, taps):
            piece = partial[col_tap * channels : (col_tap + 1) * channels]
            total = total + pltpu.roll(piece, chunk * segment - col_tap, 1)
        for row in range(chunk):
            o_ref[start + row] = total[:, row * segment : row * segment + cols_lon]


def horizontal(masked, w_horiz):
    row_taps, channels, col_taps, _ = w_horiz.shape
    reach_row = row_taps // 2
    _, _, rows_lat, cols_lon = masked.shape
    count = lax.axis_size("lon")
    segment = 2 * cols_lon
    rows_major = jnp.transpose(masked[0], (1, 0, 2))
    weights = jnp.transpose(w_horiz, (2, 1, 0, 3)).reshape(col_taps * channels, row_taps * channels)
    vmem = pl.BlockSpec(memory_space=pltpu.VMEM)
    conv = pl.pallas_call(
        functools.partial(horizontal_kernel, count),
        out_shape=jax.ShapeDtypeStruct((rows_lat, channels, cols_lon), jnp.float32),
        in_specs=[vmem, vmem],
        out_specs=vmem,
        scratch_shapes=[
            pltpu.VMEM((channels, (rows_lat + 2 * reach_row) * segment), masked.dtype),
            pltpu.VMEM((channels, cols_lon), masked.dtype),
            pltpu.VMEM((channels, cols_lon), masked.dtype),
            pltpu.VMEM((channels, cols_lon), masked.dtype),
            pltpu.SemaphoreType.DMA((2,)),
            pltpu.SemaphoreType.DMA((2,)),
        ],
        compiler_params=pltpu.CompilerParams(collective_id=0, has_side_effects=True),
        cost_estimate=pl.CostEstimate(
            flops=2 * rows_lat * segment * weights.shape[0] * weights.shape[1],
            bytes_accessed=masked.size * 2 + weights.size * 2 + rows_lat * channels * cols_lon * 4,
            transcendentals=0,
        ),
    )(rows_major, weights)
    return jnp.transpose(conv, (1, 0, 2))[None]


def solution(mesh):
    halves = 2
    lon_count, lat_count = mesh.devices.shape
    split = jax.sharding.Mesh(
        mesh.devices.reshape(lon_count, halves, lat_count // halves), ("lon", "lat_hi", "lat_lo")
    )
    lat = ("lat_hi", "lat_lo")
    placed = (P(lat, None, None, "lon"), P(lat, None, "lon"), P(), P(), P(), P(), P())
    return jax.shard_map(
        local, mesh=split, in_specs=placed, out_specs=P(lat, None, None, "lon"), check_vma=False
    )
```

```python
import functools

import jax
from jax.experimental import pallas as pl
from jax.experimental.pallas import tpu as pltpu
import jax.numpy as jnp
from jax import lax
from jax.sharding import PartitionSpec as P


def normalize_kernel(x_ref, g_ref, o_ref):
    rows, channels, cols_lon = o_ref.shape
    channel = lax.broadcasted_iota(jnp.int32, (channels, cols_lon), 0)
    gain = jnp.zeros((channels, cols_lon), jnp.float32)
    for index in range(channels):
        gain = jnp.where(channel == index, g_ref[index], gain)
    for row in range(rows):
        values = x_ref[0, :, row, :].astype(jnp.float32)
        center = jnp.sum(values, axis=0, keepdims=True) / channels
        offset = values - center
        spread = jnp.sum(offset * offset, axis=0, keepdims=True) / channels
        o_ref[row] = (offset * lax.rsqrt(spread + 1e-05) * gain).astype(o_ref.dtype)


def normalize(block, norm_gain):
    _, channels, rows_lat, cols_lon = block.shape
    vmem = pl.BlockSpec(memory_space=pltpu.VMEM)
    normed = pl.pallas_call(
        normalize_kernel,
        out_shape=jax.ShapeDtypeStruct((rows_lat, channels, cols_lon), jnp.bfloat16),
        in_specs=[vmem, pl.BlockSpec(memory_space=pltpu.SMEM)],
        out_specs=vmem,
    )(block, norm_gain)
    return jnp.transpose(normed, (1, 0, 2))[None]


def vertical(taps, w_vert, b_vert):
    count_lev, channels, rows_lat, cols_lon = taps[0].shape
    groups, width_in, width_out = (w_vert.shape[1], w_vert.shape[2], w_vert.shape[3])
    summed = jnp.zeros((count_lev, groups, width_out, rows_lat, cols_lon), jnp.float32)
    for tap_index in range(len(taps)):
        grouped = taps[tap_index].reshape(count_lev, groups, width_in, rows_lat, cols_lon)
        summed = summed + jnp.einsum(
            "gio,ngiab->ngoab", w_vert[tap_index], grouped, preferred_element_type=jnp.float32
        )
    summed = summed.reshape(count_lev, channels, rows_lat, cols_lon) + b_vert[None, :, None, None]
    return jax.nn.gelu(summed).astype(jnp.bfloat16)


def local(fields, ocean_mask, norm_gain, w_vert, b_vert, w_horiz, b_horiz):
    normed = normalize(fields, norm_gain)
    reach = w_vert.shape[0] // 2
    columns = lax.all_to_all(normed, "lat_lo", split_axis=2, concat_axis=0, tiled=True)
    count_lev = columns.shape[0]
    upper = lax.axis_index("lat_hi") == 0
    send = jnp.where(upper, columns[count_lev - reach :], columns[:reach])
    recv = lax.ppermute(send, "lat_hi", [(0, 1), (1, 0)])
    zeros = jnp.zeros_like(recv)
    below = jnp.where(upper, zeros, recv)
    above = jnp.where(upper, recv, zeros)
    padded = jnp.concatenate([below, columns, above], axis=0)
    taps = [padded[tap_index : tap_index + count_lev] for tap_index in range(w_vert.shape[0])]
    mixed = lax.all_to_all(
        vertical(taps, w_vert, b_vert), "lat_lo", split_axis=0, concat_axis=2, tiled=True
    )
    masked = mixed * ocean_mask[:, None].astype(jnp.bfloat16)
    return horizontal(masked, w_horiz, fields, ocean_mask, b_horiz)


def horizontal_kernel(
    count, x_ref, w_ref, f_ref, m_ref, b_ref, o_ref, wide, edges, from_left, from_right, send_sems,
    recv_sems,
):
    me = lax.axis_index("lon")
    right, left = lax.rem(me + 1, count), lax.rem(me + count - 1, count)
    rest = (lax.axis_index("lat_hi"), lax.axis_index("lat_lo"))
    mesh_ids = pl.DeviceIdType.MESH
    barrier = pltpu.get_barrier_semaphore()
    for neighbour in (left, right):
        pl.semaphore_signal(barrier, inc=1, device_id=(neighbour,) + rest, device_id_type=mesh_ids)

    rows, channels, cols_lon = x_ref.shape
    taps = w_ref.shape[0] // channels
    reach = taps // 2
    segment = 2 * cols_lon
    lane = lax.broadcasted_iota(jnp.int32, (channels, cols_lon), 1)
    packed = jnp.zeros((channels, cols_lon), x_ref.dtype)
    for row in range(rows):
        line = x_ref[row]
        start = 2 * reach * row
        packed = jnp.where(
            jnp.logical_and(lane >= start, lane < start + reach),
            pltpu.roll(line, start, 1),
            packed,
        )
        packed = jnp.where(
            jnp.logical_and(lane >= start + reach, lane < start + 2 * reach),
            pltpu.roll(line, (start + 2 * reach) % cols_lon, 1),
            packed,
        )
    edges[...] = packed

    pl.semaphore_wait(barrier, 2)
    to_right = pltpu.make_async_remote_copy(
        src_ref=edges,
        dst_ref=from_left,
        send_sem=send_sems.at[0],
        recv_sem=recv_sems.at[0],
        device_id=(right,) + rest,
        device_id_type=mesh_ids,
    )
    to_left = pltpu.make_async_remote_copy(
        src_ref=edges,
        dst_ref=from_right,
        send_sem=send_sems.at[1],
        recv_sem=recv_sems.at[1],
        device_id=(left,) + rest,
        device_id_type=mesh_ids,
    )
    to_right.start()
    to_left.start()
    to_right.wait()
    to_left.wait()

    left_halo, right_halo = from_left[...], from_right[...]
    blank = jnp.zeros((channels, cols_lon), x_ref.dtype)
    for padded_row in range(rows + 2 * reach):
        row = padded_row - reach
        base = padded_row * segment
        if row < 0 or row >= rows:
            wide[:, base : base + cols_lon] = blank
            wide[:, base + cols_lon : base + segment] = blank
            continue
        start = 2 * reach * row
        shifted = pltpu.roll(x_ref[row], reach, 1)
        wide[:, base : base + cols_lon] = jnp.where(
            lane < reach, pltpu.roll(left_halo, (cols_lon - start - reach) % cols_lon, 1), shifted
        )
        tail = pltpu.roll(right_halo, (reach - start) % cols_lon, 1)
        wide[:, base + cols_lon : base + segment] = jnp.where(
            lane < reach, shifted, jnp.where(lane < 2 * reach, tail, blank)
        )

    channel = lax.broadcasted_iota(jnp.int32, (channels, cols_lon), 0)
    bias = jnp.zeros((channels, cols_lon), jnp.float32)
    for index in range(channels):
        bias = jnp.where(channel == index, b_ref[index], bias)
    chunk = 8
    weights = w_ref[...]
    for start in range(0, rows, chunk):
        window = jnp.concatenate(
            [
                wide[:, (start + row_tap) * segment : (start + row_tap + chunk) * segment]
                for row_tap in range(taps)
            ],
            axis=0,
        )
        partial = jnp.dot(weights, window, preferred_element_type=jnp.float32)
        total = partial[:channels]
        for col_tap in range(1, taps):
            piece = partial[col_tap * channels : (col_tap + 1) * channels]
            total = total + pltpu.roll(piece, chunk * segment - col_tap, 1)
        for row in range(chunk):
            line = start + row
            conv = total[:, row * segment : row * segment + cols_lon]
            ocean = m_ref[0, line : line + 1, :].astype(jnp.float32)
            base = f_ref[0, :, line, :].astype(jnp.float32)
            o_ref[0, :, line, :] = (base + ocean * (conv + bias)).astype(o_ref.dtype)


def horizontal(masked, w_horiz, fields, ocean_mask, b_horiz):
    row_taps, channels, col_taps, _ = w_horiz.shape
    reach_row = row_taps // 2
    _, _, rows_lat, cols_lon = masked.shape
    count = lax.axis_size("lon")
    segment = 2 * cols_lon
    rows_major = jnp.transpose(masked[0], (1, 0, 2))
    weights = jnp.transpose(w_horiz, (2, 1, 0, 3)).reshape(col_taps * channels, row_taps * channels)
    vmem = pl.BlockSpec(memory_space=pltpu.VMEM)
    return pl.pallas_call(
        functools.partial(horizontal_kernel, count),
        out_shape=jax.ShapeDtypeStruct(fields.shape, fields.dtype),
        in_specs=[vmem] * 4 + [pl.BlockSpec(memory_space=pltpu.SMEM)],
        out_specs=vmem,
        scratch_shapes=[
            pltpu.VMEM((channels, (rows_lat + 2 * reach_row) * segment), masked.dtype),
            pltpu.VMEM((channels, cols_lon), masked.dtype),
            pltpu.VMEM((channels, cols_lon), masked.dtype),
            pltpu.VMEM((channels, cols_lon), masked.dtype),
            pltpu.SemaphoreType.DMA((2,)),
            pltpu.SemaphoreType.DMA((2,)),
        ],
        compiler_params=pltpu.CompilerParams(collective_id=0, has_side_effects=True),
        cost_estimate=pl.CostEstimate(
            flops=2 * rows_lat * segment * weights.shape[0] * weights.shape[1],
            bytes_accessed=masked.size * 2 + weights.size * 2 + rows_lat * channels * cols_lon * 4,
            transcendentals=0,
        ),
    )(rows_major, weights, fields, ocean_mask, b_horiz)


def solution(mesh):
    halves = 2
    lon_count, lat_count = mesh.devices.shape
    split = jax.sharding.Mesh(
        mesh.devices.reshape(lon_count, halves, lat_count // halves), ("lon", "lat_hi", "lat_lo")
    )
    lat = ("lat_hi", "lat_lo")
    placed = (P(lat, None, None, "lon"), P(lat, None, "lon"), P(), P(), P(), P(), P())
    return jax.shard_map(
        local, mesh=split, in_specs=placed, out_specs=P(lat, None, None, "lon"), check_vma=False
    )
```

```python
import functools

import jax
from jax.experimental import pallas as pl
from jax.experimental.pallas import tpu as pltpu
import jax.numpy as jnp
from jax import lax
from jax.sharding import PartitionSpec as P


def normalize_kernel(x_ref, g_ref, o_ref):
    rows, channels, cols_lon = o_ref.shape
    channel = lax.broadcasted_iota(jnp.int32, (channels, cols_lon), 0)
    gain = jnp.zeros((channels, cols_lon), jnp.float32)
    for index in range(channels):
        gain = jnp.where(channel == index, g_ref[index], gain)
    for row in range(rows):
        values = x_ref[0, :, row, :].astype(jnp.float32)
        center = jnp.sum(values, axis=0, keepdims=True) / channels
        offset = values - center
        spread = jnp.sum(offset * offset, axis=0, keepdims=True) / channels
        o_ref[row] = (offset * lax.rsqrt(spread + 1e-05) * gain).astype(o_ref.dtype)


def normalize(block, norm_gain):
    _, channels, rows_lat, cols_lon = block.shape
    vmem = pl.BlockSpec(memory_space=pltpu.VMEM)
    normed = pl.pallas_call(
        normalize_kernel,
        out_shape=jax.ShapeDtypeStruct((rows_lat, channels, cols_lon), jnp.bfloat16),
        in_specs=[vmem, pl.BlockSpec(memory_space=pltpu.SMEM)],
        out_specs=vmem,
    )(block, norm_gain)
    return jnp.transpose(normed, (1, 0, 2))[None]


def vertical(taps, w_vert, b_vert):
    count_lev, channels, rows_lat, cols_lon = taps[0].shape
    groups, width_in, width_out = (w_vert.shape[1], w_vert.shape[2], w_vert.shape[3])
    summed = jnp.zeros((count_lev, groups, width_out, rows_lat, cols_lon), jnp.float32)
    for tap_index in range(len(taps)):
        grouped = taps[tap_index].reshape(count_lev, groups, width_in, rows_lat, cols_lon)
        summed = summed + jnp.einsum(
            "gio,ngiab->ngoab", w_vert[tap_index], grouped, preferred_element_type=jnp.float32
        )
    summed = summed.reshape(count_lev, channels, rows_lat, cols_lon) + b_vert[None, :, None, None]
    return jax.nn.gelu(summed).astype(jnp.bfloat16)


def local(fields, ocean_mask, norm_gain, w_vert, b_vert, w_horiz, b_horiz):
    normed = normalize(fields, norm_gain)
    reach = w_vert.shape[0] // 2
    columns = lax.all_to_all(normed, "lat_lo", split_axis=2, concat_axis=0, tiled=True)
    count_lev = columns.shape[0]
    upper = lax.axis_index("lat_hi") == 0
    send = jnp.where(upper, columns[count_lev - reach :], columns[:reach])
    recv = lax.ppermute(send, "lat_hi", [(0, 1), (1, 0)])
    zeros = jnp.zeros_like(recv)
    below = jnp.where(upper, zeros, recv)
    above = jnp.where(upper, recv, zeros)
    padded = jnp.concatenate([below, columns, above], axis=0)
    taps = [padded[tap_index : tap_index + count_lev] for tap_index in range(w_vert.shape[0])]
    mixed = lax.all_to_all(
        vertical(taps, w_vert, b_vert), "lat_lo", split_axis=0, concat_axis=2, tiled=True
    )
    return horizontal(mixed, w_horiz, fields, ocean_mask, b_horiz)


def horizontal_kernel(
    count, x_ref, w_ref, f_ref, m_ref, b_ref, o_ref, wide, edges, from_left, from_right, send_sems,
    recv_sems,
):
    me = lax.axis_index("lon")
    right, left = lax.rem(me + 1, count), lax.rem(me + count - 1, count)
    rest = (lax.axis_index("lat_hi"), lax.axis_index("lat_lo"))
    mesh_ids = pl.DeviceIdType.MESH
    barrier = pltpu.get_barrier_semaphore()
    for neighbour in (left, right):
        pl.semaphore_signal(barrier, inc=1, device_id=(neighbour,) + rest, device_id_type=mesh_ids)

    rows, channels, cols_lon = x_ref.shape
    taps = w_ref.shape[0] // channels
    reach = taps // 2
    segment = 2 * cols_lon
    lane = lax.broadcasted_iota(jnp.int32, (channels, cols_lon), 1)
    packed = jnp.zeros((channels, cols_lon), x_ref.dtype)
    def masked_row(row):
        return x_ref[row] * m_ref[0, row : row + 1, :].astype(x_ref.dtype)

    for row in range(rows):
        line = masked_row(row)
        start = 2 * reach * row
        packed = jnp.where(
            jnp.logical_and(lane >= start, lane < start + reach),
            pltpu.roll(line, start, 1),
            packed,
        )
        packed = jnp.where(
            jnp.logical_and(lane >= start + reach, lane < start + 2 * reach),
            pltpu.roll(line, (start + 2 * reach) % cols_lon, 1),
            packed,
        )
    edges[...] = packed

    pl.semaphore_wait(barrier, 2)
    to_right = pltpu.make_async_remote_copy(
        src_ref=edges,
        dst_ref=from_left,
        send_sem=send_sems.at[0],
        recv_sem=recv_sems.at[0],
        device_id=(right,) + rest,
        device_id_type=mesh_ids,
    )
    to_left = pltpu.make_async_remote_copy(
        src_ref=edges,
        dst_ref=from_right,
        send_sem=send_sems.at[1],
        recv_sem=recv_sems.at[1],
        device_id=(left,) + rest,
        device_id_type=mesh_ids,
    )
    to_right.start()
    to_left.start()
    to_right.wait()
    to_left.wait()

    left_halo, right_halo = from_left[...], from_right[...]
    blank = jnp.zeros((channels, cols_lon), x_ref.dtype)
    for padded_row in range(rows + 2 * reach):
        row = padded_row - reach
        base = padded_row * segment
        if row < 0 or row >= rows:
            wide[:, base : base + cols_lon] = blank
            wide[:, base + cols_lon : base + segment] = blank
            continue
        start = 2 * reach * row
        shifted = pltpu.roll(masked_row(row), reach, 1)
        wide[:, base : base + cols_lon] = jnp.where(
            lane < reach, pltpu.roll(left_halo, (cols_lon - start - reach) % cols_lon, 1), shifted
        )
        tail = pltpu.roll(right_halo, (reach - start) % cols_lon, 1)
        wide[:, base + cols_lon : base + segment] = jnp.where(
            lane < reach, shifted, jnp.where(lane < 2 * reach, tail, blank)
        )

    channel = lax.broadcasted_iota(jnp.int32, (channels, cols_lon), 0)
    bias = jnp.zeros((channels, cols_lon), jnp.float32)
    for index in range(channels):
        bias = jnp.where(channel == index, b_ref[index], bias)
    chunk = 8
    weights = w_ref[...]
    for start in range(0, rows, chunk):
        window = jnp.concatenate(
            [
                wide[:, (start + row_tap) * segment : (start + row_tap + chunk) * segment]
                for row_tap in range(taps)
            ],
            axis=0,
        )
        partial = jnp.dot(weights, window, preferred_element_type=jnp.float32)
        total = partial[:channels]
        for col_tap in range(1, taps):
            piece = partial[col_tap * channels : (col_tap + 1) * channels]
            total = total + pltpu.roll(piece, chunk * segment - col_tap, 1)
        for row in range(chunk):
            line = start + row
            conv = total[:, row * segment : row * segment + cols_lon]
            ocean = m_ref[0, line : line + 1, :].astype(jnp.float32)
            base = f_ref[0, :, line, :].astype(jnp.float32)
            o_ref[0, :, line, :] = (base + ocean * (conv + bias)).astype(o_ref.dtype)


def horizontal(masked, w_horiz, fields, ocean_mask, b_horiz):
    row_taps, channels, col_taps, _ = w_horiz.shape
    reach_row = row_taps // 2
    _, _, rows_lat, cols_lon = masked.shape
    count = lax.axis_size("lon")
    segment = 2 * cols_lon
    rows_major = jnp.transpose(masked[0], (1, 0, 2))
    weights = jnp.transpose(w_horiz, (2, 1, 0, 3)).reshape(col_taps * channels, row_taps * channels)
    vmem = pl.BlockSpec(memory_space=pltpu.VMEM)
    return pl.pallas_call(
        functools.partial(horizontal_kernel, count),
        out_shape=jax.ShapeDtypeStruct(fields.shape, fields.dtype),
        in_specs=[vmem] * 4 + [pl.BlockSpec(memory_space=pltpu.SMEM)],
        out_specs=vmem,
        scratch_shapes=[
            pltpu.VMEM((channels, (rows_lat + 2 * reach_row) * segment), masked.dtype),
            pltpu.VMEM((channels, cols_lon), masked.dtype),
            pltpu.VMEM((channels, cols_lon), masked.dtype),
            pltpu.VMEM((channels, cols_lon), masked.dtype),
            pltpu.SemaphoreType.DMA((2,)),
            pltpu.SemaphoreType.DMA((2,)),
        ],
        compiler_params=pltpu.CompilerParams(collective_id=0, has_side_effects=True),
        cost_estimate=pl.CostEstimate(
            flops=2 * rows_lat * segment * weights.shape[0] * weights.shape[1],
            bytes_accessed=masked.size * 2 + weights.size * 2 + rows_lat * channels * cols_lon * 4,
            transcendentals=0,
        ),
    )(rows_major, weights, fields, ocean_mask, b_horiz)


def solution(mesh):
    halves = 2
    lon_count, lat_count = mesh.devices.shape
    split = jax.sharding.Mesh(
        mesh.devices.reshape(lon_count, halves, lat_count // halves), ("lon", "lat_hi", "lat_lo")
    )
    lat = ("lat_hi", "lat_lo")
    placed = (P(lat, None, None, "lon"), P(lat, None, "lon"), P(), P(), P(), P(), P())
    return jax.shard_map(
        local, mesh=split, in_specs=placed, out_specs=P(lat, None, None, "lon"), check_vma=False
    )
```

```python
import functools

import jax
from jax.experimental import pallas as pl
from jax.experimental.pallas import tpu as pltpu
import jax.numpy as jnp
from jax import lax
from jax.sharding import PartitionSpec as P


def normalize_kernel(x_ref, g_ref, o_ref):
    rows, channels, cols_lon = o_ref.shape
    channel = lax.broadcasted_iota(jnp.int32, (channels, cols_lon), 0)
    gain = jnp.zeros((channels, cols_lon), jnp.float32)
    for index in range(channels):
        gain = jnp.where(channel == index, g_ref[index], gain)
    for row in range(rows):
        values = x_ref[0, :, row, :].astype(jnp.float32)
        center = jnp.sum(values, axis=0, keepdims=True) / channels
        offset = values - center
        spread = jnp.sum(offset * offset, axis=0, keepdims=True) / channels
        o_ref[row] = (offset * lax.rsqrt(spread + 1e-05) * gain).astype(o_ref.dtype)


def normalize(block, norm_gain):
    _, channels, rows_lat, cols_lon = block.shape
    vmem = pl.BlockSpec(memory_space=pltpu.VMEM)
    normed = pl.pallas_call(
        normalize_kernel,
        out_shape=jax.ShapeDtypeStruct((rows_lat, channels, cols_lon), jnp.bfloat16),
        in_specs=[vmem, pl.BlockSpec(memory_space=pltpu.SMEM)],
        out_specs=vmem,
    )(block, norm_gain)
    return jnp.transpose(normed, (1, 0, 2))[None]


def vertical(taps, w_vert, b_vert):
    count_lev, channels, rows_lat, cols_lon = taps[0].shape
    groups, width_in, width_out = (w_vert.shape[1], w_vert.shape[2], w_vert.shape[3])
    summed = jnp.zeros((count_lev, groups, width_out, rows_lat, cols_lon), jnp.float32)
    for tap_index in range(len(taps)):
        grouped = taps[tap_index].reshape(count_lev, groups, width_in, rows_lat, cols_lon)
        summed = summed + jnp.einsum(
            "gio,ngiab->ngoab", w_vert[tap_index], grouped, preferred_element_type=jnp.float32
        )
    summed = summed.reshape(count_lev, channels, rows_lat, cols_lon) + b_vert[None, :, None, None]
    return jax.nn.gelu(summed).astype(jnp.bfloat16)


def partner_kernel(halves, send_ref, out_ref, send_sem, recv_sem):
    partner = (lax.axis_index("lon"), halves - 1 - lax.axis_index("lat_hi"), lax.axis_index("lat_lo"))
    mesh_ids = pl.DeviceIdType.MESH
    barrier = pltpu.get_barrier_semaphore()
    pl.semaphore_signal(barrier, inc=1, device_id=partner, device_id_type=mesh_ids)
    pl.semaphore_wait(barrier, 1)
    swap = pltpu.make_async_remote_copy(
        src_ref=send_ref,
        dst_ref=out_ref,
        send_sem=send_sem.at[0],
        recv_sem=recv_sem.at[0],
        device_id=partner,
        device_id_type=mesh_ids,
    )
    swap.start()
    swap.wait()


def across(send):
    any_spec = pl.BlockSpec(memory_space=pl.ANY)
    return pl.pallas_call(
        functools.partial(partner_kernel, lax.axis_size("lat_hi")),
        out_shape=jax.ShapeDtypeStruct(send.shape, send.dtype),
        in_specs=[any_spec],
        out_specs=any_spec,
        scratch_shapes=[pltpu.SemaphoreType.DMA((1,)), pltpu.SemaphoreType.DMA((1,))],
        compiler_params=pltpu.CompilerParams(collective_id=1, has_side_effects=True),
    )(send)


def local(fields, ocean_mask, norm_gain, w_vert, b_vert, w_horiz, b_horiz):
    normed = normalize(fields, norm_gain)
    reach = w_vert.shape[0] // 2
    columns = lax.all_to_all(normed, "lat_lo", split_axis=2, concat_axis=0, tiled=True)
    count_lev = columns.shape[0]
    upper = lax.axis_index("lat_hi") == 0
    send = jnp.where(upper, columns[count_lev - reach :], columns[:reach])
    recv = across(send)
    zeros = jnp.zeros_like(recv)
    below = jnp.where(upper, zeros, recv)
    above = jnp.where(upper, recv, zeros)
    padded = jnp.concatenate([below, columns, above], axis=0)
    taps = [padded[tap_index : tap_index + count_lev] for tap_index in range(w_vert.shape[0])]
    mixed = lax.all_to_all(
        vertical(taps, w_vert, b_vert), "lat_lo", split_axis=0, concat_axis=2, tiled=True
    )
    masked = mixed * ocean_mask[:, None].astype(jnp.bfloat16)
    return horizontal(masked, w_horiz, fields, ocean_mask, b_horiz)


def horizontal_kernel(
    count, x_ref, w_ref, f_ref, m_ref, b_ref, o_ref, wide, edges, from_left, from_right, send_sems,
    recv_sems,
):
    me = lax.axis_index("lon")
    right, left = lax.rem(me + 1, count), lax.rem(me + count - 1, count)
    rest = (lax.axis_index("lat_hi"), lax.axis_index("lat_lo"))
    mesh_ids = pl.DeviceIdType.MESH
    barrier = pltpu.get_barrier_semaphore()
    for neighbour in (left, right):
        pl.semaphore_signal(barrier, inc=1, device_id=(neighbour,) + rest, device_id_type=mesh_ids)

    rows, channels, cols_lon = x_ref.shape
    taps = w_ref.shape[0] // channels
    reach = taps // 2
    segment = 2 * cols_lon
    lane = lax.broadcasted_iota(jnp.int32, (channels, cols_lon), 1)
    packed = jnp.zeros((channels, cols_lon), x_ref.dtype)
    for row in range(rows):
        line = x_ref[row]
        start = 2 * reach * row
        packed = jnp.where(
            jnp.logical_and(lane >= start, lane < start + reach),
            pltpu.roll(line, start, 1),
            packed,
        )
        packed = jnp.where(
            jnp.logical_and(lane >= start + reach, lane < start + 2 * reach),
            pltpu.roll(line, (start + 2 * reach) % cols_lon, 1),
            packed,
        )
    edges[...] = packed

    pl.semaphore_wait(barrier, 2)
    to_right = pltpu.make_async_remote_copy(
        src_ref=edges,
        dst_ref=from_left,
        send_sem=send_sems.at[0],
        recv_sem=recv_sems.at[0],
        device_id=(right,) + rest,
        device_id_type=mesh_ids,
    )
    to_left = pltpu.make_async_remote_copy(
        src_ref=edges,
        dst_ref=from_right,
        send_sem=send_sems.at[1],
        recv_sem=recv_sems.at[1],
        device_id=(left,) + rest,
        device_id_type=mesh_ids,
    )
    to_right.start()
    to_left.start()
    to_right.wait()
    to_left.wait()

    left_halo, right_halo = from_left[...], from_right[...]
    blank = jnp.zeros((channels, cols_lon), x_ref.dtype)
    for padded_row in range(rows + 2 * reach):
        row = padded_row - reach
        base = padded_row * segment
        if row < 0 or row >= rows:
            wide[:, base : base + cols_lon] = blank
            wide[:, base + cols_lon : base + segment] = blank
            continue
        start = 2 * reach * row
        shifted = pltpu.roll(x_ref[row], reach, 1)
        wide[:, base : base + cols_lon] = jnp.where(
            lane < reach, pltpu.roll(left_halo, (cols_lon - start - reach) % cols_lon, 1), shifted
        )
        tail = pltpu.roll(right_halo, (reach - start) % cols_lon, 1)
        wide[:, base + cols_lon : base + segment] = jnp.where(
            lane < reach, shifted, jnp.where(lane < 2 * reach, tail, blank)
        )

    channel = lax.broadcasted_iota(jnp.int32, (channels, cols_lon), 0)
    bias = jnp.zeros((channels, cols_lon), jnp.float32)
    for index in range(channels):
        bias = jnp.where(channel == index, b_ref[index], bias)
    chunk = 8
    weights = w_ref[...]
    for start in range(0, rows, chunk):
        window = jnp.concatenate(
            [
                wide[:, (start + row_tap) * segment : (start + row_tap + chunk) * segment]
                for row_tap in range(taps)
            ],
            axis=0,
        )
        partial = jnp.dot(weights, window, preferred_element_type=jnp.float32)
        total = partial[:channels]
        for col_tap in range(1, taps):
            piece = partial[col_tap * channels : (col_tap + 1) * channels]
            total = total + pltpu.roll(piece, chunk * segment - col_tap, 1)
        for row in range(chunk):
            line = start + row
            conv = total[:, row * segment : row * segment + cols_lon]
            ocean = m_ref[0, line : line + 1, :].astype(jnp.float32)
            base = f_ref[0, :, line, :].astype(jnp.float32)
            o_ref[0, :, line, :] = (base + ocean * (conv + bias)).astype(o_ref.dtype)


def horizontal(masked, w_horiz, fields, ocean_mask, b_horiz):
    row_taps, channels, col_taps, _ = w_horiz.shape
    reach_row = row_taps // 2
    _, _, rows_lat, cols_lon = masked.shape
    count = lax.axis_size("lon")
    segment = 2 * cols_lon
    rows_major = jnp.transpose(masked[0], (1, 0, 2))
    weights = jnp.transpose(w_horiz, (2, 1, 0, 3)).reshape(col_taps * channels, row_taps * channels)
    vmem = pl.BlockSpec(memory_space=pltpu.VMEM)
    return pl.pallas_call(
        functools.partial(horizontal_kernel, count),
        out_shape=jax.ShapeDtypeStruct(fields.shape, fields.dtype),
        in_specs=[vmem] * 4 + [pl.BlockSpec(memory_space=pltpu.SMEM)],
        out_specs=vmem,
        scratch_shapes=[
            pltpu.VMEM((channels, (rows_lat + 2 * reach_row) * segment), masked.dtype),
            pltpu.VMEM((channels, cols_lon), masked.dtype),
            pltpu.VMEM((channels, cols_lon), masked.dtype),
            pltpu.VMEM((channels, cols_lon), masked.dtype),
            pltpu.SemaphoreType.DMA((2,)),
            pltpu.SemaphoreType.DMA((2,)),
        ],
        compiler_params=pltpu.CompilerParams(collective_id=0, has_side_effects=True),
        cost_estimate=pl.CostEstimate(
            flops=2 * rows_lat * segment * weights.shape[0] * weights.shape[1],
            bytes_accessed=masked.size * 2 + weights.size * 2 + rows_lat * channels * cols_lon * 4,
            transcendentals=0,
        ),
    )(rows_major, weights, fields, ocean_mask, b_horiz)


def solution(mesh):
    halves = 2
    lon_count, lat_count = mesh.devices.shape
    split = jax.sharding.Mesh(
        mesh.devices.reshape(lon_count, halves, lat_count // halves), ("lon", "lat_hi", "lat_lo")
    )
    lat = ("lat_hi", "lat_lo")
    placed = (P(lat, None, None, "lon"), P(lat, None, "lon"), P(), P(), P(), P(), P())
    return jax.shard_map(
        local, mesh=split, in_specs=placed, out_specs=P(lat, None, None, "lon"), check_vma=False
    )
```

```python
import functools

import jax
from jax.experimental import pallas as pl
from jax.experimental.pallas import tpu as pltpu
import jax.numpy as jnp
from jax import lax
from jax.sharding import PartitionSpec as P


def normalize_kernel(x_ref, g_ref, o_ref):
    rows, channels, cols_lon = o_ref.shape
    channel = lax.broadcasted_iota(jnp.int32, (channels, cols_lon), 0)
    gain = jnp.zeros((channels, cols_lon), jnp.float32)
    for index in range(channels):
        gain = jnp.where(channel == index, g_ref[index], gain)
    for row in range(rows):
        values = x_ref[0, :, row, :].astype(jnp.float32)
        center = jnp.sum(values, axis=0, keepdims=True) / channels
        offset = values - center
        spread = jnp.sum(offset * offset, axis=0, keepdims=True) / channels
        o_ref[row] = (offset * lax.rsqrt(spread + 1e-05) * gain).astype(o_ref.dtype)


def normalize(block, norm_gain):
    _, channels, rows_lat, cols_lon = block.shape
    vmem = pl.BlockSpec(memory_space=pltpu.VMEM)
    normed = pl.pallas_call(
        normalize_kernel,
        out_shape=jax.ShapeDtypeStruct((rows_lat, channels, cols_lon), jnp.bfloat16),
        in_specs=[vmem, pl.BlockSpec(memory_space=pltpu.SMEM)],
        out_specs=vmem,
    )(block, norm_gain)
    return jnp.transpose(normed, (1, 0, 2))[None]


def vertical(taps, w_vert, b_vert):
    count_lev, channels, rows_lat, cols_lon = taps[0].shape
    groups, width_in, width_out = (w_vert.shape[1], w_vert.shape[2], w_vert.shape[3])
    stacked = jnp.stack(
        [tap.reshape(count_lev, groups, width_in, rows_lat, cols_lon) for tap in taps], axis=2
    ).reshape(count_lev, groups, len(taps) * width_in, rows_lat, cols_lon)
    weights = jnp.transpose(w_vert, (1, 0, 2, 3)).reshape(groups, len(taps) * width_in, width_out)
    summed = jnp.einsum("gjo,ngjab->ngoab", weights, stacked, preferred_element_type=jnp.float32)
    summed = summed.reshape(count_lev, channels, rows_lat, cols_lon) + b_vert[None, :, None, None]
    return jax.nn.gelu(summed).astype(jnp.bfloat16)


def local(fields, ocean_mask, norm_gain, w_vert, b_vert, w_horiz, b_horiz):
    normed = normalize(fields, norm_gain)
    reach = w_vert.shape[0] // 2
    columns = lax.all_to_all(normed, "lat_lo", split_axis=2, concat_axis=0, tiled=True)
    count_lev = columns.shape[0]
    upper = lax.axis_index("lat_hi") == 0
    send = jnp.where(upper, columns[count_lev - reach :], columns[:reach])
    recv = lax.ppermute(send, "lat_hi", [(0, 1), (1, 0)])
    zeros = jnp.zeros_like(recv)
    below = jnp.where(upper, zeros, recv)
    above = jnp.where(upper, recv, zeros)
    padded = jnp.concatenate([below, columns, above], axis=0)
    taps = [padded[tap_index : tap_index + count_lev] for tap_index in range(w_vert.shape[0])]
    mixed = lax.all_to_all(
        vertical(taps, w_vert, b_vert), "lat_lo", split_axis=0, concat_axis=2, tiled=True
    )
    masked = mixed * ocean_mask[:, None].astype(jnp.bfloat16)
    return horizontal(masked, w_horiz, fields, ocean_mask, b_horiz)


def horizontal_kernel(
    count, x_ref, w_ref, f_ref, m_ref, b_ref, o_ref, wide, edges, from_left, from_right, send_sems,
    recv_sems,
):
    me = lax.axis_index("lon")
    right, left = lax.rem(me + 1, count), lax.rem(me + count - 1, count)
    rest = (lax.axis_index("lat_hi"), lax.axis_index("lat_lo"))
    mesh_ids = pl.DeviceIdType.MESH
    barrier = pltpu.get_barrier_semaphore()
    for neighbour in (left, right):
        pl.semaphore_signal(barrier, inc=1, device_id=(neighbour,) + rest, device_id_type=mesh_ids)

    rows, channels, cols_lon = x_ref.shape
    taps = w_ref.shape[0] // channels
    reach = taps // 2
    segment = 2 * cols_lon
    lane = lax.broadcasted_iota(jnp.int32, (channels, cols_lon), 1)
    packed = jnp.zeros((channels, cols_lon), x_ref.dtype)
    for row in range(rows):
        line = x_ref[row]
        start = 2 * reach * row
        packed = jnp.where(
            jnp.logical_and(lane >= start, lane < start + reach),
            pltpu.roll(line, start, 1),
            packed,
        )
        packed = jnp.where(
            jnp.logical_and(lane >= start + reach, lane < start + 2 * reach),
            pltpu.roll(line, (start + 2 * reach) % cols_lon, 1),
            packed,
        )
    edges[...] = packed

    pl.semaphore_wait(barrier, 2)
    to_right = pltpu.make_async_remote_copy(
        src_ref=edges,
        dst_ref=from_left,
        send_sem=send_sems.at[0],
        recv_sem=recv_sems.at[0],
        device_id=(right,) + rest,
        device_id_type=mesh_ids,
    )
    to_left = pltpu.make_async_remote_copy(
        src_ref=edges,
        dst_ref=from_right,
        send_sem=send_sems.at[1],
        recv_sem=recv_sems.at[1],
        device_id=(left,) + rest,
        device_id_type=mesh_ids,
    )
    to_right.start()
    to_left.start()
    to_right.wait()
    to_left.wait()

    left_halo, right_halo = from_left[...], from_right[...]
    blank = jnp.zeros((channels, cols_lon), x_ref.dtype)
    for padded_row in range(rows + 2 * reach):
        row = padded_row - reach
        base = padded_row * segment
        if row < 0 or row >= rows:
            wide[:, base : base + cols_lon] = blank
            wide[:, base + cols_lon : base + segment] = blank
            continue
        start = 2 * reach * row
        shifted = pltpu.roll(x_ref[row], reach, 1)
        wide[:, base : base + cols_lon] = jnp.where(
            lane < reach, pltpu.roll(left_halo, (cols_lon - start - reach) % cols_lon, 1), shifted
        )
        tail = pltpu.roll(right_halo, (reach - start) % cols_lon, 1)
        wide[:, base + cols_lon : base + segment] = jnp.where(
            lane < reach, shifted, jnp.where(lane < 2 * reach, tail, blank)
        )

    channel = lax.broadcasted_iota(jnp.int32, (channels, cols_lon), 0)
    bias = jnp.zeros((channels, cols_lon), jnp.float32)
    for index in range(channels):
        bias = jnp.where(channel == index, b_ref[index], bias)
    chunk = 8
    weights = w_ref[...]
    for start in range(0, rows, chunk):
        window = jnp.concatenate(
            [
                wide[:, (start + row_tap) * segment : (start + row_tap + chunk) * segment]
                for row_tap in range(taps)
            ],
            axis=0,
        )
        partial = jnp.dot(weights, window, preferred_element_type=jnp.float32)
        total = partial[:channels]
        for col_tap in range(1, taps):
            piece = partial[col_tap * channels : (col_tap + 1) * channels]
            total = total + pltpu.roll(piece, chunk * segment - col_tap, 1)
        for row in range(chunk):
            line = start + row
            conv = total[:, row * segment : row * segment + cols_lon]
            ocean = m_ref[0, line : line + 1, :].astype(jnp.float32)
            base = f_ref[0, :, line, :].astype(jnp.float32)
            o_ref[0, :, line, :] = (base + ocean * (conv + bias)).astype(o_ref.dtype)


def horizontal(masked, w_horiz, fields, ocean_mask, b_horiz):
    row_taps, channels, col_taps, _ = w_horiz.shape
    reach_row = row_taps // 2
    _, _, rows_lat, cols_lon = masked.shape
    count = lax.axis_size("lon")
    segment = 2 * cols_lon
    rows_major = jnp.transpose(masked[0], (1, 0, 2))
    weights = jnp.transpose(w_horiz, (2, 1, 0, 3)).reshape(col_taps * channels, row_taps * channels)
    vmem = pl.BlockSpec(memory_space=pltpu.VMEM)
    return pl.pallas_call(
        functools.partial(horizontal_kernel, count),
        out_shape=jax.ShapeDtypeStruct(fields.shape, fields.dtype),
        in_specs=[vmem] * 4 + [pl.BlockSpec(memory_space=pltpu.SMEM)],
        out_specs=vmem,
        scratch_shapes=[
            pltpu.VMEM((channels, (rows_lat + 2 * reach_row) * segment), masked.dtype),
            pltpu.VMEM((channels, cols_lon), masked.dtype),
            pltpu.VMEM((channels, cols_lon), masked.dtype),
            pltpu.VMEM((channels, cols_lon), masked.dtype),
            pltpu.SemaphoreType.DMA((2,)),
            pltpu.SemaphoreType.DMA((2,)),
        ],
        compiler_params=pltpu.CompilerParams(collective_id=0, has_side_effects=True),
        cost_estimate=pl.CostEstimate(
            flops=2 * rows_lat * segment * weights.shape[0] * weights.shape[1],
            bytes_accessed=masked.size * 2 + weights.size * 2 + rows_lat * channels * cols_lon * 4,
            transcendentals=0,
        ),
    )(rows_major, weights, fields, ocean_mask, b_horiz)


def solution(mesh):
    halves = 2
    lon_count, lat_count = mesh.devices.shape
    split = jax.sharding.Mesh(
        mesh.devices.reshape(lon_count, halves, lat_count // halves), ("lon", "lat_hi", "lat_lo")
    )
    lat = ("lat_hi", "lat_lo")
    placed = (P(lat, None, None, "lon"), P(lat, None, "lon"), P(), P(), P(), P(), P())
    return jax.shard_map(
        local, mesh=split, in_specs=placed, out_specs=P(lat, None, None, "lon"), check_vma=False
    )
```

```python
import functools

import jax
from jax.experimental import pallas as pl
from jax.experimental.pallas import tpu as pltpu
import jax.numpy as jnp
from jax import lax
from jax.sharding import PartitionSpec as P


def normalize_kernel(x_ref, g_ref, o_ref):
    rows, channels, cols_lon = o_ref.shape
    channel = lax.broadcasted_iota(jnp.int32, (channels, cols_lon), 0)
    gain = jnp.zeros((channels, cols_lon), jnp.float32)
    for index in range(channels):
        gain = jnp.where(channel == index, g_ref[index], gain)
    values = x_ref[0].astype(jnp.float32)
    center = jnp.sum(values, axis=0) / channels
    offset = values - center[None]
    scale = lax.rsqrt(jnp.sum(offset * offset, axis=0) / channels + 1e-05)
    for row in range(rows):
        o_ref[row] = (offset[:, row, :] * scale[row : row + 1, :] * gain).astype(o_ref.dtype)


def normalize(block, norm_gain):
    _, channels, rows_lat, cols_lon = block.shape
    vmem = pl.BlockSpec(memory_space=pltpu.VMEM)
    normed = pl.pallas_call(
        normalize_kernel,
        out_shape=jax.ShapeDtypeStruct((rows_lat, channels, cols_lon), jnp.bfloat16),
        in_specs=[vmem, pl.BlockSpec(memory_space=pltpu.SMEM)],
        out_specs=vmem,
    )(block, norm_gain)
    return jnp.transpose(normed, (1, 0, 2))[None]


def vertical(taps, w_vert, b_vert):
    count_lev, channels, rows_lat, cols_lon = taps[0].shape
    groups, width_in, width_out = (w_vert.shape[1], w_vert.shape[2], w_vert.shape[3])
    stacked = jnp.stack(
        [tap.reshape(count_lev, groups, width_in, rows_lat, cols_lon) for tap in taps], axis=2
    ).reshape(count_lev, groups, len(taps) * width_in, rows_lat, cols_lon)
    weights = jnp.transpose(w_vert, (1, 0, 2, 3)).reshape(groups, len(taps) * width_in, width_out)
    summed = jnp.einsum("gjo,ngjab->ngoab", weights, stacked, preferred_element_type=jnp.float32)
    summed = summed.reshape(count_lev, channels, rows_lat, cols_lon) + b_vert[None, :, None, None]
    return jax.nn.gelu(summed).astype(jnp.bfloat16)


def local(fields, ocean_mask, norm_gain, w_vert, b_vert, w_horiz, b_horiz):
    normed = normalize(fields, norm_gain)
    reach = w_vert.shape[0] // 2
    columns = lax.all_to_all(normed, "lat_lo", split_axis=2, concat_axis=0, tiled=True)
    count_lev = columns.shape[0]
    upper = lax.axis_index("lat_hi") == 0
    send = jnp.where(upper, columns[count_lev - reach :], columns[:reach])
    recv = lax.ppermute(send, "lat_hi", [(0, 1), (1, 0)])
    zeros = jnp.zeros_like(recv)
    below = jnp.where(upper, zeros, recv)
    above = jnp.where(upper, recv, zeros)
    padded = jnp.concatenate([below, columns, above], axis=0)
    taps = [padded[tap_index : tap_index + count_lev] for tap_index in range(w_vert.shape[0])]
    mixed = lax.all_to_all(
        vertical(taps, w_vert, b_vert), "lat_lo", split_axis=0, concat_axis=2, tiled=True
    )
    masked = mixed * ocean_mask[:, None].astype(jnp.bfloat16)
    return horizontal(masked, w_horiz, fields, ocean_mask, b_horiz)


def horizontal_kernel(
    count, x_ref, w_ref, f_ref, m_ref, b_ref, o_ref, wide, edges, from_left, from_right, send_sems,
    recv_sems,
):
    me = lax.axis_index("lon")
    right, left = lax.rem(me + 1, count), lax.rem(me + count - 1, count)
    rest = (lax.axis_index("lat_hi"), lax.axis_index("lat_lo"))
    mesh_ids = pl.DeviceIdType.MESH
    barrier = pltpu.get_barrier_semaphore()
    for neighbour in (left, right):
        pl.semaphore_signal(barrier, inc=1, device_id=(neighbour,) + rest, device_id_type=mesh_ids)

    rows, channels, cols_lon = x_ref.shape
    taps = w_ref.shape[0] // channels
    reach = taps // 2
    segment = 2 * cols_lon
    lane = lax.broadcasted_iota(jnp.int32, (channels, cols_lon), 1)
    packed = jnp.zeros((channels, cols_lon), x_ref.dtype)
    for row in range(rows):
        line = x_ref[row]
        start = 2 * reach * row
        packed = jnp.where(
            jnp.logical_and(lane >= start, lane < start + reach),
            pltpu.roll(line, start, 1),
            packed,
        )
        packed = jnp.where(
            jnp.logical_and(lane >= start + reach, lane < start + 2 * reach),
            pltpu.roll(line, (start + 2 * reach) % cols_lon, 1),
            packed,
        )
    edges[...] = packed

    pl.semaphore_wait(barrier, 2)
    to_right = pltpu.make_async_remote_copy(
        src_ref=edges,
        dst_ref=from_left,
        send_sem=send_sems.at[0],
        recv_sem=recv_sems.at[0],
        device_id=(right,) + rest,
        device_id_type=mesh_ids,
    )
    to_left = pltpu.make_async_remote_copy(
        src_ref=edges,
        dst_ref=from_right,
        send_sem=send_sems.at[1],
        recv_sem=recv_sems.at[1],
        device_id=(left,) + rest,
        device_id_type=mesh_ids,
    )
    to_right.start()
    to_left.start()
    to_right.wait()
    to_left.wait()

    left_halo, right_halo = from_left[...], from_right[...]
    blank = jnp.zeros((channels, cols_lon), x_ref.dtype)
    for padded_row in range(rows + 2 * reach):
        row = padded_row - reach
        base = padded_row * segment
        if row < 0 or row >= rows:
            wide[:, base : base + cols_lon] = blank
            wide[:, base + cols_lon : base + segment] = blank
            continue
        start = 2 * reach * row
        shifted = pltpu.roll(x_ref[row], reach, 1)
        wide[:, base : base + cols_lon] = jnp.where(
            lane < reach, pltpu.roll(left_halo, (cols_lon - start - reach) % cols_lon, 1), shifted
        )
        tail = pltpu.roll(right_halo, (reach - start) % cols_lon, 1)
        wide[:, base + cols_lon : base + segment] = jnp.where(
            lane < reach, shifted, jnp.where(lane < 2 * reach, tail, blank)
        )

    channel = lax.broadcasted_iota(jnp.int32, (channels, cols_lon), 0)
    bias = jnp.zeros((channels, cols_lon), jnp.float32)
    for index in range(channels):
        bias = jnp.where(channel == index, b_ref[index], bias)
    chunk = 8
    weights = w_ref[...]
    for start in range(0, rows, chunk):
        window = jnp.concatenate(
            [
                wide[:, (start + row_tap) * segment : (start + row_tap + chunk) * segment]
                for row_tap in range(taps)
            ],
            axis=0,
        )
        partial = jnp.dot(weights, window, preferred_element_type=jnp.float32)
        total = partial[:channels]
        for col_tap in range(1, taps):
            piece = partial[col_tap * channels : (col_tap + 1) * channels]
            total = total + pltpu.roll(piece, chunk * segment - col_tap, 1)
        for row in range(chunk):
            line = start + row
            conv = total[:, row * segment : row * segment + cols_lon]
            ocean = m_ref[0, line : line + 1, :].astype(jnp.float32)
            base = f_ref[0, :, line, :].astype(jnp.float32)
            o_ref[0, :, line, :] = (base + ocean * (conv + bias)).astype(o_ref.dtype)


def horizontal(masked, w_horiz, fields, ocean_mask, b_horiz):
    row_taps, channels, col_taps, _ = w_horiz.shape
    reach_row = row_taps // 2
    _, _, rows_lat, cols_lon = masked.shape
    count = lax.axis_size("lon")
    segment = 2 * cols_lon
    rows_major = jnp.transpose(masked[0], (1, 0, 2))
    weights = jnp.transpose(w_horiz, (2, 1, 0, 3)).reshape(col_taps * channels, row_taps * channels)
    vmem = pl.BlockSpec(memory_space=pltpu.VMEM)
    return pl.pallas_call(
        functools.partial(horizontal_kernel, count),
        out_shape=jax.ShapeDtypeStruct(fields.shape, fields.dtype),
        in_specs=[vmem] * 4 + [pl.BlockSpec(memory_space=pltpu.SMEM)],
        out_specs=vmem,
        scratch_shapes=[
            pltpu.VMEM((channels, (rows_lat + 2 * reach_row) * segment), masked.dtype),
            pltpu.VMEM((channels, cols_lon), masked.dtype),
            pltpu.VMEM((channels, cols_lon), masked.dtype),
            pltpu.VMEM((channels, cols_lon), masked.dtype),
            pltpu.SemaphoreType.DMA((2,)),
            pltpu.SemaphoreType.DMA((2,)),
        ],
        compiler_params=pltpu.CompilerParams(collective_id=0, has_side_effects=True),
        cost_estimate=pl.CostEstimate(
            flops=2 * rows_lat * segment * weights.shape[0] * weights.shape[1],
            bytes_accessed=masked.size * 2 + weights.size * 2 + rows_lat * channels * cols_lon * 4,
            transcendentals=0,
        ),
    )(rows_major, weights, fields, ocean_mask, b_horiz)


def solution(mesh):
    halves = 2
    lon_count, lat_count = mesh.devices.shape
    split = jax.sharding.Mesh(
        mesh.devices.reshape(lon_count, halves, lat_count // halves), ("lon", "lat_hi", "lat_lo")
    )
    lat = ("lat_hi", "lat_lo")
    placed = (P(lat, None, None, "lon"), P(lat, None, "lon"), P(), P(), P(), P(), P())
    return jax.shard_map(
        local, mesh=split, in_specs=placed, out_specs=P(lat, None, None, "lon"), check_vma=False
    )
```

```python
import functools

import jax
from jax.experimental import pallas as pl
from jax.experimental.pallas import tpu as pltpu
import jax.numpy as jnp
from jax import lax
from jax.sharding import PartitionSpec as P


def normalize_kernel(x_ref, g_ref, o_ref):
    rows, channels, cols_lon = o_ref.shape
    channel = lax.broadcasted_iota(jnp.int32, (channels, cols_lon), 0)
    gain = jnp.zeros((channels, cols_lon), jnp.float32)
    for index in range(channels):
        gain = jnp.where(channel == index, g_ref[index], gain)
    values = x_ref[0].astype(jnp.float32)
    center = jnp.sum(values, axis=0) / channels
    offset = values - center[None]
    scale = lax.rsqrt(jnp.sum(offset * offset, axis=0) / channels + 1e-05)
    for row in range(rows):
        o_ref[row] = (offset[:, row, :] * scale[row : row + 1, :] * gain).astype(o_ref.dtype)


def normalize(block, norm_gain):
    _, channels, rows_lat, cols_lon = block.shape
    vmem = pl.BlockSpec(memory_space=pltpu.VMEM)
    normed = pl.pallas_call(
        normalize_kernel,
        out_shape=jax.ShapeDtypeStruct((rows_lat, channels, cols_lon), jnp.bfloat16),
        in_specs=[vmem, pl.BlockSpec(memory_space=pltpu.SMEM)],
        out_specs=vmem,
    )(block, norm_gain)
    return jnp.transpose(normed, (1, 0, 2))[None]


def vertical(taps, w_vert, b_vert):
    count_lev, channels, rows_lat, cols_lon = taps[0].shape
    groups, width_in, width_out = (w_vert.shape[1], w_vert.shape[2], w_vert.shape[3])
    stacked = jnp.stack(
        [tap.reshape(count_lev, groups, width_in, rows_lat, cols_lon) for tap in taps], axis=2
    ).reshape(count_lev, groups, len(taps) * width_in, rows_lat, cols_lon)
    weights = jnp.transpose(w_vert, (1, 0, 2, 3)).reshape(groups, len(taps) * width_in, width_out)
    summed = jnp.einsum("gjo,ngjab->ngoab", weights, stacked, preferred_element_type=jnp.float32)
    summed = summed.reshape(count_lev, channels, rows_lat, cols_lon) + b_vert[None, :, None, None]
    return jax.nn.gelu(summed).astype(jnp.bfloat16)


def local(fields, ocean_mask, norm_gain, w_vert, b_vert, w_horiz, b_horiz):
    normed = normalize(fields, norm_gain)
    reach = w_vert.shape[0] // 2
    columns = lax.all_to_all(normed, "lat_lo", split_axis=2, concat_axis=0, tiled=True)
    count_lev = columns.shape[0]
    upper = lax.axis_index("lat_hi") == 0
    send = jnp.where(upper, columns[count_lev - reach :], columns[:reach])
    recv = lax.ppermute(send, "lat_hi", [(0, 1), (1, 0)])
    zeros = jnp.zeros_like(recv)
    below = jnp.where(upper, zeros, recv)
    above = jnp.where(upper, recv, zeros)
    padded = jnp.concatenate([below, columns, above], axis=0)
    taps = [padded[tap_index : tap_index + count_lev] for tap_index in range(w_vert.shape[0])]
    mixed = lax.all_to_all(
        vertical(taps, w_vert, b_vert), "lat_lo", split_axis=0, concat_axis=2, tiled=True
    )
    return horizontal(mixed, w_horiz, fields, ocean_mask, b_horiz)


def horizontal_kernel(
    count, x_ref, w_ref, f_ref, m_ref, b_ref, o_ref, wide, edges, from_left, from_right, send_sems,
    recv_sems,
):
    me = lax.axis_index("lon")
    right, left = lax.rem(me + 1, count), lax.rem(me + count - 1, count)
    rest = (lax.axis_index("lat_hi"), lax.axis_index("lat_lo"))
    mesh_ids = pl.DeviceIdType.MESH
    barrier = pltpu.get_barrier_semaphore()
    for neighbour in (left, right):
        pl.semaphore_signal(barrier, inc=1, device_id=(neighbour,) + rest, device_id_type=mesh_ids)

    rows, channels, cols_lon = x_ref.shape
    taps = w_ref.shape[0] // channels
    reach = taps // 2
    segment = 2 * cols_lon
    lane = lax.broadcasted_iota(jnp.int32, (channels, cols_lon), 1)
    packed = jnp.zeros((channels, cols_lon), x_ref.dtype)
    def masked_row(row):
        return x_ref[row] * m_ref[0, row : row + 1, :].astype(x_ref.dtype)

    for row in range(rows):
        line = masked_row(row)
        start = 2 * reach * row
        packed = jnp.where(
            jnp.logical_and(lane >= start, lane < start + reach),
            pltpu.roll(line, start, 1),
            packed,
        )
        packed = jnp.where(
            jnp.logical_and(lane >= start + reach, lane < start + 2 * reach),
            pltpu.roll(line, (start + 2 * reach) % cols_lon, 1),
            packed,
        )
    edges[...] = packed

    pl.semaphore_wait(barrier, 2)
    to_right = pltpu.make_async_remote_copy(
        src_ref=edges,
        dst_ref=from_left,
        send_sem=send_sems.at[0],
        recv_sem=recv_sems.at[0],
        device_id=(right,) + rest,
        device_id_type=mesh_ids,
    )
    to_left = pltpu.make_async_remote_copy(
        src_ref=edges,
        dst_ref=from_right,
        send_sem=send_sems.at[1],
        recv_sem=recv_sems.at[1],
        device_id=(left,) + rest,
        device_id_type=mesh_ids,
    )
    to_right.start()
    to_left.start()
    to_right.wait()
    to_left.wait()

    left_halo, right_halo = from_left[...], from_right[...]
    blank = jnp.zeros((channels, cols_lon), x_ref.dtype)
    for padded_row in range(rows + 2 * reach):
        row = padded_row - reach
        base = padded_row * segment
        if row < 0 or row >= rows:
            wide[:, base : base + cols_lon] = blank
            wide[:, base + cols_lon : base + segment] = blank
            continue
        start = 2 * reach * row
        shifted = pltpu.roll(masked_row(row), reach, 1)
        wide[:, base : base + cols_lon] = jnp.where(
            lane < reach, pltpu.roll(left_halo, (cols_lon - start - reach) % cols_lon, 1), shifted
        )
        tail = pltpu.roll(right_halo, (reach - start) % cols_lon, 1)
        wide[:, base + cols_lon : base + segment] = jnp.where(
            lane < reach, shifted, jnp.where(lane < 2 * reach, tail, blank)
        )

    channel = lax.broadcasted_iota(jnp.int32, (channels, cols_lon), 0)
    bias = jnp.zeros((channels, cols_lon), jnp.float32)
    for index in range(channels):
        bias = jnp.where(channel == index, b_ref[index], bias)
    chunk = 8
    weights = w_ref[...]
    for start in range(0, rows, chunk):
        window = jnp.concatenate(
            [
                wide[:, (start + row_tap) * segment : (start + row_tap + chunk) * segment]
                for row_tap in range(taps)
            ],
            axis=0,
        )
        partial = jnp.dot(weights, window, preferred_element_type=jnp.float32)
        total = partial[:channels]
        for col_tap in range(1, taps):
            piece = partial[col_tap * channels : (col_tap + 1) * channels]
            total = total + pltpu.roll(piece, chunk * segment - col_tap, 1)
        for row in range(chunk):
            line = start + row
            conv = total[:, row * segment : row * segment + cols_lon]
            ocean = m_ref[0, line : line + 1, :].astype(jnp.float32)
            base = f_ref[0, :, line, :].astype(jnp.float32)
            o_ref[0, :, line, :] = (base + ocean * (conv + bias)).astype(o_ref.dtype)


def horizontal(masked, w_horiz, fields, ocean_mask, b_horiz):
    row_taps, channels, col_taps, _ = w_horiz.shape
    reach_row = row_taps // 2
    _, _, rows_lat, cols_lon = masked.shape
    count = lax.axis_size("lon")
    segment = 2 * cols_lon
    rows_major = jnp.transpose(masked[0], (1, 0, 2))
    weights = jnp.transpose(w_horiz, (2, 1, 0, 3)).reshape(col_taps * channels, row_taps * channels)
    vmem = pl.BlockSpec(memory_space=pltpu.VMEM)
    return pl.pallas_call(
        functools.partial(horizontal_kernel, count),
        out_shape=jax.ShapeDtypeStruct(fields.shape, fields.dtype),
        in_specs=[vmem] * 4 + [pl.BlockSpec(memory_space=pltpu.SMEM)],
        out_specs=vmem,
        scratch_shapes=[
            pltpu.VMEM((channels, (rows_lat + 2 * reach_row) * segment), masked.dtype),
            pltpu.VMEM((channels, cols_lon), masked.dtype),
            pltpu.VMEM((channels, cols_lon), masked.dtype),
            pltpu.VMEM((channels, cols_lon), masked.dtype),
            pltpu.SemaphoreType.DMA((2,)),
            pltpu.SemaphoreType.DMA((2,)),
        ],
        compiler_params=pltpu.CompilerParams(collective_id=0, has_side_effects=True),
        cost_estimate=pl.CostEstimate(
            flops=2 * rows_lat * segment * weights.shape[0] * weights.shape[1],
            bytes_accessed=masked.size * 2 + weights.size * 2 + rows_lat * channels * cols_lon * 4,
            transcendentals=0,
        ),
    )(rows_major, weights, fields, ocean_mask, b_horiz)


def solution(mesh):
    halves = 2
    lon_count, lat_count = mesh.devices.shape
    split = jax.sharding.Mesh(
        mesh.devices.reshape(lon_count, halves, lat_count // halves), ("lon", "lat_hi", "lat_lo")
    )
    lat = ("lat_hi", "lat_lo")
    placed = (P(lat, None, None, "lon"), P(lat, None, "lon"), P(), P(), P(), P(), P())
    return jax.shard_map(
        local, mesh=split, in_specs=placed, out_specs=P(lat, None, None, "lon"), check_vma=False
    )
```

```python
import functools

import jax
from jax.experimental import pallas as pl
from jax.experimental.pallas import tpu as pltpu
import jax.numpy as jnp
from jax import lax
from jax.sharding import PartitionSpec as P


def normalize_kernel(x_ref, g_ref, o_ref):
    rows, channels, cols_lon = o_ref.shape
    channel = lax.broadcasted_iota(jnp.int32, (channels, cols_lon), 0)
    gain = jnp.zeros((channels, cols_lon), jnp.float32)
    for index in range(channels):
        gain = jnp.where(channel == index, g_ref[index], gain)
    values = x_ref[0].astype(jnp.float32)
    center = jnp.sum(values, axis=0) / channels
    offset = values - center[None]
    scale = lax.rsqrt(jnp.sum(offset * offset, axis=0) / channels + 1e-05)
    for row in range(rows):
        o_ref[row] = (offset[:, row, :] * scale[row : row + 1, :] * gain).astype(o_ref.dtype)


def normalize(block, norm_gain):
    _, channels, rows_lat, cols_lon = block.shape
    vmem = pl.BlockSpec(memory_space=pltpu.VMEM)
    normed = pl.pallas_call(
        normalize_kernel,
        out_shape=jax.ShapeDtypeStruct((rows_lat, channels, cols_lon), jnp.bfloat16),
        in_specs=[vmem, pl.BlockSpec(memory_space=pltpu.SMEM)],
        out_specs=vmem,
    )(block, norm_gain)
    return jnp.transpose(normed, (1, 0, 2))[None]


def vertical(taps, w_vert, b_vert):
    count_lev, channels, rows_lat, cols_lon = taps[0].shape
    groups, width_in, width_out = (w_vert.shape[1], w_vert.shape[2], w_vert.shape[3])
    stacked = jnp.stack(
        [tap.reshape(count_lev, groups, width_in, rows_lat, cols_lon) for tap in taps], axis=2
    ).reshape(count_lev, groups, len(taps) * width_in, rows_lat, cols_lon)
    weights = jnp.transpose(w_vert, (1, 0, 2, 3)).reshape(groups, len(taps) * width_in, width_out)
    summed = jnp.einsum("gjo,ngjab->ngoab", weights, stacked, preferred_element_type=jnp.float32)
    summed = summed.reshape(count_lev, channels, rows_lat, cols_lon) + b_vert[None, :, None, None]
    return jax.nn.gelu(summed).astype(jnp.bfloat16)


def local(fields, ocean_mask, norm_gain, w_vert, b_vert, w_horiz, b_horiz):
    normed = normalize(fields, norm_gain)
    reach = w_vert.shape[0] // 2
    columns = lax.all_to_all(normed, "lat_lo", split_axis=2, concat_axis=0, tiled=True)
    count_lev = columns.shape[0]
    upper = lax.axis_index("lat_hi") == 0
    send = jnp.where(upper, columns[count_lev - reach :], columns[:reach])
    recv = lax.ppermute(send, "lat_hi", [(0, 1), (1, 0)])
    zeros = jnp.zeros_like(recv)
    below = jnp.where(upper, zeros, recv)
    above = jnp.where(upper, recv, zeros)
    padded = jnp.concatenate([below, columns, above], axis=0)
    taps = [padded[tap_index : tap_index + count_lev] for tap_index in range(w_vert.shape[0])]
    mixed = lax.all_to_all(
        vertical(taps, w_vert, b_vert), "lat_lo", split_axis=0, concat_axis=2, tiled=True
    )
    return horizontal(mixed, w_horiz, fields, ocean_mask, b_horiz)


def horizontal_kernel(
    count, x_ref, w_ref, f_ref, m_ref, b_ref, o_ref, wide, edges, from_left, from_right, send_sems,
    recv_sems,
):
    me = lax.axis_index("lon")
    right, left = lax.rem(me + 1, count), lax.rem(me + count - 1, count)
    rest = (lax.axis_index("lat_hi"), lax.axis_index("lat_lo"))
    mesh_ids = pl.DeviceIdType.MESH
    barrier = pltpu.get_barrier_semaphore()
    for neighbour in (left, right):
        pl.semaphore_signal(barrier, inc=1, device_id=(neighbour,) + rest, device_id_type=mesh_ids)

    rows, channels, cols_lon = x_ref.shape
    taps = w_ref.shape[0] // channels
    reach = taps // 2
    segment = 2 * cols_lon
    lane = lax.broadcasted_iota(jnp.int32, (channels, cols_lon), 1)
    packed = jnp.zeros((channels, cols_lon), x_ref.dtype)
    def masked_row(row):
        return x_ref[row] * m_ref[0, row : row + 1, :].astype(x_ref.dtype)

    for row in range(rows):
        line = masked_row(row)
        start = 2 * reach * row
        packed = jnp.where(
            jnp.logical_and(lane >= start, lane < start + reach),
            pltpu.roll(line, start, 1),
            packed,
        )
        packed = jnp.where(
            jnp.logical_and(lane >= start + reach, lane < start + 2 * reach),
            pltpu.roll(line, (start + 2 * reach) % cols_lon, 1),
            packed,
        )
    edges[...] = packed

    pl.semaphore_wait(barrier, 2)
    to_right = pltpu.make_async_remote_copy(
        src_ref=edges,
        dst_ref=from_left,
        send_sem=send_sems.at[0],
        recv_sem=recv_sems.at[0],
        device_id=(right,) + rest,
        device_id_type=mesh_ids,
    )
    to_left = pltpu.make_async_remote_copy(
        src_ref=edges,
        dst_ref=from_right,
        send_sem=send_sems.at[1],
        recv_sem=recv_sems.at[1],
        device_id=(left,) + rest,
        device_id_type=mesh_ids,
    )
    to_right.start()
    to_left.start()
    to_right.wait()
    to_left.wait()

    left_halo, right_halo = from_left[...], from_right[...]
    blank = jnp.zeros((channels, cols_lon), x_ref.dtype)
    for padded_row in range(rows + 2 * reach):
        row = padded_row - reach
        base = padded_row * segment
        if row < 0 or row >= rows:
            wide[:, base : base + cols_lon] = blank
            wide[:, base + cols_lon : base + segment] = blank
            continue
        start = 2 * reach * row
        shifted = pltpu.roll(masked_row(row), reach, 1)
        wide[:, base : base + cols_lon] = jnp.where(
            lane < reach, pltpu.roll(left_halo, (cols_lon - start - reach) % cols_lon, 1), shifted
        )
        tail = pltpu.roll(right_halo, (reach - start) % cols_lon, 1)
        wide[:, base + cols_lon : base + segment] = jnp.where(
            lane < reach, shifted, jnp.where(lane < 2 * reach, tail, blank)
        )

    channel = lax.broadcasted_iota(jnp.int32, (channels, cols_lon), 0)
    bias = jnp.zeros((channels, cols_lon), jnp.float32)
    for index in range(channels):
        bias = jnp.where(channel == index, b_ref[index], bias)
    chunk = 16
    weights = w_ref[...]
    for start in range(0, rows, chunk):
        window = jnp.concatenate(
            [
                wide[:, (start + row_tap) * segment : (start + row_tap + chunk) * segment]
                for row_tap in range(taps)
            ],
            axis=0,
        )
        partial = jnp.dot(weights, window, preferred_element_type=jnp.float32)
        total = partial[:channels]
        for col_tap in range(1, taps):
            piece = partial[col_tap * channels : (col_tap + 1) * channels]
            total = total + pltpu.roll(piece, chunk * segment - col_tap, 1)
        for row in range(chunk):
            line = start + row
            conv = total[:, row * segment : row * segment + cols_lon]
            ocean = m_ref[0, line : line + 1, :].astype(jnp.float32)
            base = f_ref[0, :, line, :].astype(jnp.float32)
            o_ref[0, :, line, :] = (base + ocean * (conv + bias)).astype(o_ref.dtype)


def horizontal(masked, w_horiz, fields, ocean_mask, b_horiz):
    row_taps, channels, col_taps, _ = w_horiz.shape
    reach_row = row_taps // 2
    _, _, rows_lat, cols_lon = masked.shape
    count = lax.axis_size("lon")
    segment = 2 * cols_lon
    rows_major = jnp.transpose(masked[0], (1, 0, 2))
    weights = jnp.transpose(w_horiz, (2, 1, 0, 3)).reshape(col_taps * channels, row_taps * channels)
    vmem = pl.BlockSpec(memory_space=pltpu.VMEM)
    return pl.pallas_call(
        functools.partial(horizontal_kernel, count),
        out_shape=jax.ShapeDtypeStruct(fields.shape, fields.dtype),
        in_specs=[vmem] * 4 + [pl.BlockSpec(memory_space=pltpu.SMEM)],
        out_specs=vmem,
        scratch_shapes=[
            pltpu.VMEM((channels, (rows_lat + 2 * reach_row) * segment), masked.dtype),
            pltpu.VMEM((channels, cols_lon), masked.dtype),
            pltpu.VMEM((channels, cols_lon), masked.dtype),
            pltpu.VMEM((channels, cols_lon), masked.dtype),
            pltpu.SemaphoreType.DMA((2,)),
            pltpu.SemaphoreType.DMA((2,)),
        ],
        compiler_params=pltpu.CompilerParams(collective_id=0, has_side_effects=True),
        cost_estimate=pl.CostEstimate(
            flops=2 * rows_lat * segment * weights.shape[0] * weights.shape[1],
            bytes_accessed=masked.size * 2 + weights.size * 2 + rows_lat * channels * cols_lon * 4,
            transcendentals=0,
        ),
    )(rows_major, weights, fields, ocean_mask, b_horiz)


def solution(mesh):
    halves = 2
    lon_count, lat_count = mesh.devices.shape
    split = jax.sharding.Mesh(
        mesh.devices.reshape(lon_count, halves, lat_count // halves), ("lon", "lat_hi", "lat_lo")
    )
    lat = ("lat_hi", "lat_lo")
    placed = (P(lat, None, None, "lon"), P(lat, None, "lon"), P(), P(), P(), P(), P())
    return jax.shard_map(
        local, mesh=split, in_specs=placed, out_specs=P(lat, None, None, "lon"), check_vma=False
    )
```

```python
import functools

import jax
from jax.experimental import pallas as pl
from jax.experimental.pallas import tpu as pltpu
import jax.numpy as jnp
from jax import lax
from jax.sharding import PartitionSpec as P


def normalize_kernel(x_ref, g_ref, o_ref):
    rows, channels, cols_lon = o_ref.shape
    channel = lax.broadcasted_iota(jnp.int32, (channels, cols_lon), 0)
    gain = jnp.zeros((channels, cols_lon), jnp.float32)
    for index in range(channels):
        gain = jnp.where(channel == index, g_ref[index], gain)
    values = x_ref[0].astype(jnp.float32)
    center = jnp.sum(values, axis=0) / channels
    offset = values - center[None]
    scale = lax.rsqrt(jnp.sum(offset * offset, axis=0) / channels + 1e-05)
    for row in range(rows):
        o_ref[row] = (offset[:, row, :] * scale[row : row + 1, :] * gain).astype(o_ref.dtype)


def normalize(block, norm_gain):
    _, channels, rows_lat, cols_lon = block.shape
    vmem = pl.BlockSpec(memory_space=pltpu.VMEM)
    normed = pl.pallas_call(
        normalize_kernel,
        out_shape=jax.ShapeDtypeStruct((rows_lat, channels, cols_lon), jnp.bfloat16),
        in_specs=[vmem, pl.BlockSpec(memory_space=pltpu.SMEM)],
        out_specs=vmem,
    )(block, norm_gain)
    return jnp.transpose(normed, (1, 0, 2))[None]


def vertical(taps, w_vert, b_vert):
    count_lev, channels, rows_lat, cols_lon = taps[0].shape
    groups, width_in, width_out = (w_vert.shape[1], w_vert.shape[2], w_vert.shape[3])
    stacked = jnp.stack(
        [tap.reshape(count_lev, groups, width_in, rows_lat, cols_lon) for tap in taps], axis=2
    ).reshape(count_lev, groups, len(taps) * width_in, rows_lat, cols_lon)
    weights = jnp.transpose(w_vert, (1, 0, 2, 3)).reshape(groups, len(taps) * width_in, width_out)
    summed = jnp.einsum("gjo,ngjab->ngoab", weights, stacked, preferred_element_type=jnp.float32)
    summed = summed.reshape(count_lev, channels, rows_lat, cols_lon) + b_vert[None, :, None, None]
    return jax.nn.gelu(summed).astype(jnp.bfloat16)


def local(fields, ocean_mask, norm_gain, w_vert, b_vert, w_horiz, b_horiz):
    normed = normalize(fields, norm_gain)
    reach = w_vert.shape[0] // 2
    columns = lax.all_to_all(normed, "lat_lo", split_axis=2, concat_axis=0, tiled=True)
    count_lev = columns.shape[0]
    upper = lax.axis_index("lat_hi") == 0
    send = jnp.where(upper, columns[count_lev - reach :], columns[:reach])
    recv = lax.ppermute(send, "lat_hi", [(0, 1), (1, 0)])
    zeros = jnp.zeros_like(recv)
    below = jnp.where(upper, zeros, recv)
    above = jnp.where(upper, recv, zeros)
    padded = jnp.concatenate([below, columns, above], axis=0)
    taps = [padded[tap_index : tap_index + count_lev] for tap_index in range(w_vert.shape[0])]
    mixed = lax.all_to_all(
        vertical(taps, w_vert, b_vert), "lat_lo", split_axis=0, concat_axis=2, tiled=True
    )
    return horizontal(mixed, w_horiz, fields, ocean_mask, b_horiz)


def horizontal_kernel(
    count, x_ref, w_ref, f_ref, m_ref, b_ref, o_ref, wide, edges, from_left, from_right, send_sems,
    recv_sems,
):
    me = lax.axis_index("lon")
    right, left = lax.rem(me + 1, count), lax.rem(me + count - 1, count)
    rest = (lax.axis_index("lat_hi"), lax.axis_index("lat_lo"))
    mesh_ids = pl.DeviceIdType.MESH
    barrier = pltpu.get_barrier_semaphore()
    for neighbour in (left, right):
        pl.semaphore_signal(barrier, inc=1, device_id=(neighbour,) + rest, device_id_type=mesh_ids)

    rows, channels, cols_lon = x_ref.shape
    taps = w_ref.shape[0] // channels
    reach = taps // 2
    segment = 2 * cols_lon
    lane = lax.broadcasted_iota(jnp.int32, (channels, cols_lon), 1)
    packed = jnp.zeros((channels, cols_lon), x_ref.dtype)
    def masked_row(row):
        return x_ref[row] * m_ref[0, row : row + 1, :].astype(x_ref.dtype)

    for row in range(rows):
        line = masked_row(row)
        start = 2 * reach * row
        packed = jnp.where(
            jnp.logical_and(lane >= start, lane < start + reach),
            pltpu.roll(line, start, 1),
            packed,
        )
        packed = jnp.where(
            jnp.logical_and(lane >= start + reach, lane < start + 2 * reach),
            pltpu.roll(line, (start + 2 * reach) % cols_lon, 1),
            packed,
        )
    edges[...] = packed

    pl.semaphore_wait(barrier, 2)
    to_right = pltpu.make_async_remote_copy(
        src_ref=edges,
        dst_ref=from_left,
        send_sem=send_sems.at[0],
        recv_sem=recv_sems.at[0],
        device_id=(right,) + rest,
        device_id_type=mesh_ids,
    )
    to_left = pltpu.make_async_remote_copy(
        src_ref=edges,
        dst_ref=from_right,
        send_sem=send_sems.at[1],
        recv_sem=recv_sems.at[1],
        device_id=(left,) + rest,
        device_id_type=mesh_ids,
    )
    to_right.start()
    to_left.start()
    to_right.wait()
    to_left.wait()

    left_halo, right_halo = from_left[...], from_right[...]
    blank = jnp.zeros((channels, cols_lon), x_ref.dtype)
    for padded_row in range(rows + 2 * reach):
        row = padded_row - reach
        base = padded_row * segment
        if row < 0 or row >= rows:
            wide[:, base : base + cols_lon] = blank
            wide[:, base + cols_lon : base + segment] = blank
            continue
        start = 2 * reach * row
        shifted = pltpu.roll(masked_row(row), reach, 1)
        wide[:, base : base + cols_lon] = jnp.where(
            lane < reach, pltpu.roll(left_halo, (cols_lon - start - reach) % cols_lon, 1), shifted
        )
        tail = pltpu.roll(right_halo, (reach - start) % cols_lon, 1)
        wide[:, base + cols_lon : base + segment] = jnp.where(
            lane < reach, shifted, jnp.where(lane < 2 * reach, tail, blank)
        )

    channel = lax.broadcasted_iota(jnp.int32, (channels, cols_lon), 0)
    bias = jnp.zeros((channels, cols_lon), jnp.float32)
    for index in range(channels):
        bias = jnp.where(channel == index, b_ref[index], bias)
    chunk = 8
    weights = w_ref[...]
    for start in range(0, rows, chunk):
        window = jnp.concatenate(
            [
                wide[:, (start + row_tap) * segment : (start + row_tap + chunk) * segment]
                for row_tap in range(taps)
            ],
            axis=0,
        )
        partial = jnp.dot(weights, window, preferred_element_type=jnp.float32)
        total = partial[:channels]
        for col_tap in range(1, taps):
            piece = partial[col_tap * channels : (col_tap + 1) * channels]
            total = total + pltpu.roll(piece, chunk * segment - col_tap, 1)
        for row in range(chunk):
            line = start + row
            conv = total[:, row * segment : row * segment + cols_lon]
            ocean = m_ref[0, line : line + 1, :].astype(jnp.float32)
            base = f_ref[0, :, line, :].astype(jnp.float32)
            o_ref[line] = (base + ocean * (conv + bias)).astype(o_ref.dtype)


def horizontal(masked, w_horiz, fields, ocean_mask, b_horiz):
    row_taps, channels, col_taps, _ = w_horiz.shape
    reach_row = row_taps // 2
    _, _, rows_lat, cols_lon = masked.shape
    count = lax.axis_size("lon")
    segment = 2 * cols_lon
    rows_major = jnp.transpose(masked[0], (1, 0, 2))
    weights = jnp.transpose(w_horiz, (2, 1, 0, 3)).reshape(col_taps * channels, row_taps * channels)
    vmem = pl.BlockSpec(memory_space=pltpu.VMEM)
    updated = pl.pallas_call(
        functools.partial(horizontal_kernel, count),
        out_shape=jax.ShapeDtypeStruct((rows_lat, channels, cols_lon), fields.dtype),
        in_specs=[vmem] * 4 + [pl.BlockSpec(memory_space=pltpu.SMEM)],
        out_specs=vmem,
        scratch_shapes=[
            pltpu.VMEM((channels, (rows_lat + 2 * reach_row) * segment), masked.dtype),
            pltpu.VMEM((channels, cols_lon), masked.dtype),
            pltpu.VMEM((channels, cols_lon), masked.dtype),
            pltpu.VMEM((channels, cols_lon), masked.dtype),
            pltpu.SemaphoreType.DMA((2,)),
            pltpu.SemaphoreType.DMA((2,)),
        ],
        compiler_params=pltpu.CompilerParams(collective_id=0, has_side_effects=True),
        cost_estimate=pl.CostEstimate(
            flops=2 * rows_lat * segment * weights.shape[0] * weights.shape[1],
            bytes_accessed=masked.size * 2 + weights.size * 2 + rows_lat * channels * cols_lon * 4,
            transcendentals=0,
        ),
    )(rows_major, weights, fields, ocean_mask, b_horiz)
    return jnp.transpose(updated, (1, 0, 2))[None]


def solution(mesh):
    halves = 2
    lon_count, lat_count = mesh.devices.shape
    split = jax.sharding.Mesh(
        mesh.devices.reshape(lon_count, halves, lat_count // halves), ("lon", "lat_hi", "lat_lo")
    )
    lat = ("lat_hi", "lat_lo")
    placed = (P(lat, None, None, "lon"), P(lat, None, "lon"), P(), P(), P(), P(), P())
    return jax.shard_map(
        local, mesh=split, in_specs=placed, out_specs=P(lat, None, None, "lon"), check_vma=False
    )
```
